128 devices in a mesh: gx: 16 (over x_lo, z, core), gy: 8 (over x_hi, y).
Axes of the slice: x: 4 (x_hi: 2, x_lo: 2; x = x_hi * 2 + x_lo), y: 4, z: 4, core: 2. Of those that a mesh axis runs over, the one named last changes fastest.
Arguments:
- offset: float32 [3, 3072, 128], P(None, ('gx', 'gy')), may hold values from 0.5 to 1.5
- particle_mass: float32 [3072, 128], P(('gx', 'gy')), may hold values from 0.5 to 2
- velocity: float32 [3, 3072, 128], P(None, ('gx', 'gy')), may hold values from -6 to 6
- affine: float32 [9, 3072, 128], P(None, ('gx', 'gy')), may hold values from -3 to 3
- deform: float32 [9, 3072, 128], P(None, ('gx', 'gy')), may hold values from -0.3 to 1.3, as said below
- particle_cell: int32 [3072, 128], P(('gx', 'gy')), may hold values from 0 to 127
- body_id: int32 [3072, 128], P(('gx', 'gy')), may hold values from 0 to 63
- slot_tile_number: int32 [3072], P(('gx', 'gy')), may hold values from 0 to 127, as said below
- block_count: int32 [16, 8], P('gx', 'gy'), may hold values from 12 to 24, as said below
- normal_code: int32 [128, 64, 256], P('gx', 'gy'), may hold values from 0 to 25
Outputs:
- new_velocity: float32 [3, 3072, 128], P(None, ('gx', 'gy'))
- new_affine: float32 [9, 3072, 128], P(None, ('gx', 'gy'))
- new_deform: float32 [9, 3072, 128], P(None, ('gx', 'gy'))
- new_stress: float32 [6, 3072, 128], P(None, ('gx', 'gy'))
The draws below stay inside these ranges and needn't reach their ends.
Inputs may be any that keep to these rules, and one draw needn't show every extreme that they name: `deform`: A 3 x 3 identity plus entries between -0.3 and 0.3. `slot_tile_number`: on every device the first four slots lie in tiles on the low x, high x, low y and high y faces of its part of the grid, in that order. `block_count`: slots below the count are live; some device has exactly 24.
All inputs are finite; a program needn't handle non-finite values.
Results may differ from the reference program's by a relative error of at most 0.000073.
Values sent between devices are 32-bit elements; how exact they have to be, the bound alone decides.
No kernel may reach another device: no remote copies, remote signals or barrier semaphores. Data moves between devices by JAX's collectives and lax.ppermute only.
A program may use at most 128 MiB of HBM per device.

```python
import math
import jax
import jax.numpy as jnp
from jax import lax

TX = 8
TY = 8
NZ = 256
BLK_CAP = 24
PB = 128
BODIES = 64
NX = 128
NY = 64
NBLK = 3072
N_GX = 16
N_GY = 8


def draw_deform(key, part):
    noise = jnp.clip(0.1 * jax.random.normal(key, (9, NBLK, PB), jnp.float32), -0.3, 0.3)
    diagonal = (jnp.arange(9) % 4 == 0).astype(jnp.float32)
    return diagonal[:, None, None] + noise


def draw_slot_tile_number(key, part):
    tiles_x = TX // 4
    vertical_tiles = TY // 4
    tiles_z = NZ // 8
    devices = NBLK // BLK_CAP
    subkeys = jax.random.split(key, 3)
    coord_x = jax.random.randint(subkeys[0], (devices, BLK_CAP), 0, tiles_x)
    coord_y = jax.random.randint(subkeys[1], (devices, BLK_CAP), 0, vertical_tiles)
    coord_z = jax.random.randint(subkeys[2], (devices, BLK_CAP), 0, tiles_z)
    slot_position = jnp.arange(BLK_CAP)[None, :]
    coord_x = jnp.where(slot_position == 0, 0, jnp.where(slot_position == 1, tiles_x - 1, coord_x))
    coord_y = jnp.where(slot_position == 2, 0, jnp.where(slot_position == 3, vertical_tiles - 1, coord_y))
    return ((coord_x * vertical_tiles + coord_y) * tiles_z + coord_z).reshape(-1).astype(jnp.int32)


def draw_block_count(key, part):
    subkeys = jax.random.split(key, 2)
    lowest = BLK_CAP // 2
    counts = lowest + jax.random.randint(subkeys[0], (N_GX * N_GY,), 0, BLK_CAP - lowest + 1)
    busiest = jax.random.randint(subkeys[1], (), 0, N_GX * N_GY)
    counts = counts.at[busiest].set(BLK_CAP)
    return counts.reshape(N_GX, N_GY).astype(jnp.int32)


def touch_ends(values, stream_key, smallest, high):
    extent = values.shape
    index_at = [jax.random.randint(jax.random.fold_in(stream_key, axis), (), 0, extent[axis]) for axis in range(len(extent))]
    values = values.at[tuple(index_at)].set(smallest)
    longest = extent.index(max(extent))
    index_at[longest] = (index_at[longest] + 1) % extent[longest]
    return values.at[tuple(index_at)].set(high)


def levels(own_key, dims, shards, low, largest):
    level = 1.0
    for position, blocks in shards:
        draws = jax.random.uniform(jax.random.fold_in(jax.random.fold_in(own_key, 6), position), (blocks,), jnp.float32, low / len(shards), largest / len(shards))
        level = level * jnp.repeat(jnp.exp(draws), dims[position] // blocks).reshape((-1,) + (1,) * (len(dims) - 1 - position))
    return level


def gaussian(stream_key, shape, scale, bound, cuts=(), kind=jnp.bfloat16):
    values = jax.random.normal(stream_key, shape, jnp.float32) * scale
    if len(cuts) > 0:
        values = levels(stream_key, shape, cuts, -0.22, 0.18) * values
    return jnp.clip(values, min=-bound, max=bound).astype(kind)


def setup_inputs(seed: int = 0) -> dict:
    arg_keys = jax.random.split(jax.random.key(seed), 11)
    return {
        "offset": jnp.clip(0.5 + 1.0 * jax.random.uniform(arg_keys[0], (3, NBLK, PB), jnp.float32) ** levels(arg_keys[0], (3, NBLK, PB), ((1, 128),), -0.2, 0.2), 0.5, 1.5),
        "particle_mass": jnp.clip(jnp.exp(math.log(2.0) - 1.3862944 * jax.random.uniform(arg_keys[1], (NBLK, PB), jnp.float32) ** levels(arg_keys[1], (NBLK, PB), ((0, 128),), -0.2, 0.2)), 0.5, 2.0),
        "velocity": gaussian(arg_keys[2], (3, NBLK, PB), 1.0, 6.0, ((1, 128),), jnp.float32),
        "affine": gaussian(arg_keys[3], (9, NBLK, PB), 0.5, 3.0, ((1, 128),), jnp.float32),
        "deform": draw_deform(jax.random.fold_in(arg_keys[10], 71), 0),
        "particle_cell": touch_ends(jax.random.randint(arg_keys[5], (NBLK, PB), 0, 128), jax.random.fold_in(arg_keys[5], 1), 0, 127).astype(jnp.int32),
        "body_id": touch_ends(jax.random.randint(arg_keys[6], (NBLK, PB), 0, BODIES), jax.random.fold_in(arg_keys[6], 1), 0, BODIES - 1).astype(jnp.int32),
        "slot_tile_number": draw_slot_tile_number(jax.random.fold_in(arg_keys[10], 71), 0),
        "block_count": draw_block_count(jax.random.fold_in(arg_keys[10], 71), 0),
        "normal_code": touch_ends(jax.random.randint(arg_keys[9], (NX, NY, NZ), 0, 26), jax.random.fold_in(arg_keys[9], 1), 0, 25).astype(jnp.int32),
    }


DT = 0.1
MU = 2.0
LAM = 3.0
GRAVITY = -2.0
FLOOR = 0.25

def spline_weights(fraction):
    return [0.5 * (1.5 - fraction) * (1.5 - fraction), 0.75 - (fraction - 1.0) * (fraction - 1.0), 0.5 * (fraction - 0.5) * (fraction - 0.5)]

def determinant(matrix):
    return matrix[0] * (matrix[4] * matrix[8] - matrix[5] * matrix[7]) - matrix[1] * (matrix[3] * matrix[8] - matrix[5] * matrix[6]) + matrix[2] * (matrix[3] * matrix[7] - matrix[4] * matrix[6])

def kirchhoff(matrix):
    volume_ratio = determinant(matrix)
    pressure = 0.5 * LAM * (volume_ratio * volume_ratio - 1.0)
    entries = []
    for row_index in range(3):
        for column_position in range(3):
            element = matrix[3 * row_index] * matrix[3 * column_position] + matrix[3 * row_index + 1] * matrix[3 * column_position + 1] + matrix[3 * row_index + 2] * matrix[3 * column_position + 2]
            if row_index == column_position:
                element = MU * (element - 1.0) + pressure
            else:
                element = MU * element
            entries.append(element)
    return jnp.stack(entries)

def advance_deform(affine_new, deform):
    entries = []
    for row_index in range(3):
        for column_position in range(3):
            element = deform[3 * row_index + column_position]
            for inner_index in range(3):
                element = element + DT * affine_new[3 * row_index + inner_index] * deform[3 * inner_index + column_position]
            entries.append(element)
    return jnp.stack(entries)

def unit_normals(direction):
    shifted = direction + (direction >= 13).astype(jnp.int32)
    components = [shifted // 9 - 1, shifted // 3 % 3 - 1, shifted % 3 - 1]
    components = [part_value.astype(jnp.float32) for part_value in components]
    length = jnp.sqrt(components[0] * components[0] + components[1] * components[1] + components[2] * components[2])
    return jnp.stack([part_value / length for part_value in components])

def node_update(node_grid, normal):
    first_body_mass = node_grid[0]
    momentum_zero = node_grid[1:4]
    mass_one = node_grid[4]
    momentum_one = node_grid[5:8]
    gravity_step = jnp.array([0.0, 0.0, DT * GRAVITY], dtype=node_grid.dtype).reshape((3,) + (1,) * (node_grid.ndim - 1))
    speed_zero = momentum_zero / jnp.maximum(first_body_mass, FLOOR) + gravity_step
    speed_one = momentum_one / jnp.maximum(mass_one, FLOOR) + gravity_step
    center_speed = (momentum_zero + momentum_one) / jnp.maximum(first_body_mass + mass_one, FLOOR) + gravity_step
    contact_share = jnp.minimum(1.0, jnp.minimum(first_body_mass, mass_one) / FLOOR)
    approach_zero = jnp.maximum(lax.optimization_barrier(jnp.sum((speed_zero - center_speed) * normal, 0)), 0.0)
    approach_one = jnp.maximum(lax.optimization_barrier(jnp.sum((center_speed - speed_one) * normal, 0)), 0.0)
    speed_zero = speed_zero - (contact_share * approach_zero)[None] * normal
    speed_one = speed_one + (contact_share * approach_one)[None] * normal
    return jnp.concatenate([speed_zero, speed_one], 0)

def reference(offset, particle_mass, velocity, affine, deform, particle_cell, body_id, slot_tile_number, block_count, normal_code):
    slot_total = slot_tile_number.shape[0]
    slot_position = jnp.arange(slot_total, dtype=jnp.int32)
    device = slot_position // BLK_CAP
    index_x = device // N_GY
    index_y = device % N_GY
    live_mask = (slot_position % BLK_CAP < block_count.reshape(-1)[device]).astype(jnp.float32)[:, None]
    vertical_tiles = TY // 4
    tiles_z = NZ // 8
    tile_x = slot_tile_number // (vertical_tiles * tiles_z)
    tile_y = slot_tile_number // tiles_z % vertical_tiles
    tile_z = slot_tile_number % tiles_z
    cell_x = particle_cell // 32
    cell_y = particle_cell // 8 % 4
    cell_z = particle_cell % 8
    base_x = (index_x * TX + tile_x * 4)[:, None] + cell_x
    base_y = (index_y * TY + tile_y * 4)[:, None] + cell_y
    base_z = (tile_z * 8)[:, None] + cell_z
    size_x = TX * N_GX + 2
    vertical_size = TY * N_GY + 2
    size_z = NZ + 2
    weight_x = spline_weights(offset[0])
    weight_y = spline_weights(offset[1])
    weight_z = spline_weights(offset[2])
    field_zero = (body_id % 2 == 0).astype(jnp.float32)
    field_one = 1.0 - field_zero
    weighted = particle_mass * live_mask
    stress_old = kirchhoff(deform)
    affine_force = weighted[None] * (affine - 4.0 * DT * stress_old)
    node_grid = jnp.zeros((8, size_x * vertical_size * size_z), jnp.float32)
    for shift_x in range(3):
        for shift_y in range(3):
            for shift_z in range(3):
                weight = weight_x[shift_x] * weight_y[shift_y] * weight_z[shift_z]
                distance = [shift_x - offset[0], shift_y - offset[1], shift_z - offset[2]]
                momentum = []
                for row_index in range(3):
                    element = weighted * velocity[row_index]
                    for column_position in range(3):
                        element = element + affine_force[3 * row_index + column_position] * distance[column_position]
                    momentum.append(weight * element)
                values = [weight * weighted * field_zero] + [part_value * field_zero for part_value in momentum] + [weight * weighted * field_one] + [part_value * field_one for part_value in momentum]
                flat_index = ((base_x + shift_x) * vertical_size + base_y + shift_y) * size_z + base_z + shift_z
                node_grid = node_grid.at[:, flat_index.reshape(-1)].add(jnp.stack(values).reshape(8, -1))
    node_grid = node_grid.reshape(8, size_x, vertical_size, size_z)
    normal = jnp.pad(unit_normals(normal_code), ((0, 0), (1, 1), (1, 1), (1, 1)))
    inside = jnp.pad(jnp.ones((size_x - 2, vertical_size - 2, size_z - 2), jnp.float32), 1)
    node_speeds = node_update(node_grid, normal) * inside[None]
    flat_speeds = node_speeds.reshape(6, -1)
    speed_sum = jnp.zeros((3,) + particle_mass.shape, jnp.float32)
    moment_sums = jnp.zeros((9,) + particle_mass.shape, jnp.float32)
    for shift_x in range(3):
        for shift_y in range(3):
            for shift_z in range(3):
                weight = weight_x[shift_x] * weight_y[shift_y] * weight_z[shift_z]
                distance = [shift_x - offset[0], shift_y - offset[1], shift_z - offset[2]]
                flat_index = ((base_x + shift_x) * vertical_size + base_y + shift_y) * size_z + base_z + shift_z
                gathered = flat_speeds[:, flat_index.reshape(-1)].reshape((6,) + particle_mass.shape)
                chosen = gathered[0:3] * field_zero + gathered[3:6] * field_one
                speed_sum = speed_sum + weight * chosen
                moment_sums = moment_sums + jnp.stack([weight * distance[column_position] * chosen[row_index] for row_index in range(3) for column_position in range(3)])
    new_velocity = speed_sum * live_mask
    new_affine = 4.0 * moment_sums * live_mask
    new_deform = advance_deform(new_affine, deform) * live_mask
    stress_new = kirchhoff(new_deform)
    new_stress = jnp.stack([stress_new[0], stress_new[4], stress_new[8], stress_new[1], stress_new[2], stress_new[5]]) * live_mask
    return (new_velocity, new_affine, new_deform, new_stress)
```

```python
import functools

import jax
import jax.numpy as jnp
from jax import lax
from jax.experimental import pallas as pl
from jax.experimental.pallas import tpu as pltpu
from jax.sharding import PartitionSpec as P

DT = 0.1
MU = 2.0
LAM = 3.0
GRAVITY = -2.0
FLOOR = 0.25

F32 = jnp.float32
BF16 = jnp.bfloat16
VMEM_LIMIT = 24 * 1024 * 1024

SIDE = 10
DEPTH = 256
SLOTS = 24
LANES = 128
FACE_ROWS = 176

POS_Y, POS_Z, FIELD0, FIELD1, POS_X, WX = 0, 1, 2, 3, 4, 5
MASS = WX + 6
VEL = MASS + 1
AFF = VEL + 3
SCATTER_ROWS = AFF + 9
GATHER_ROWS = WX + 6


def spline(distance):
    size = jnp.abs(distance)
    outer = jnp.maximum(1.5 - size, 0.0)
    inner = jnp.maximum(0.5 - size, 0.0)
    return 0.5 * outer * outer - 1.5 * inner * inner


def determinant(m):
    return (
        m[0] * (m[4] * m[8] - m[5] * m[7])
        - m[1] * (m[3] * m[8] - m[5] * m[6])
        + m[2] * (m[3] * m[7] - m[4] * m[6])
    )


def kirchhoff(m):
    ratio = determinant(m)
    pressure = 0.5 * LAM * (ratio * ratio - 1.0)
    entries = []
    for i in range(3):
        for j in range(3):
            e = m[3 * i] * m[3 * j] + m[3 * i + 1] * m[3 * j + 1] + m[3 * i + 2] * m[3 * j + 2]
            entries.append(MU * (e - 1.0) + pressure if i == j else MU * e)
    return entries


def split(x):
    high = x.astype(BF16)
    return high, (x - high.astype(F32)).astype(BF16)


def matmul_t(a, b):
    return lax.dot_general(a, b, (((1,), (1,)), ((), ())), preferred_element_type=F32)


def matmul(a, b):
    return lax.dot_general(a, b, (((1,), (0,)), ((), ())), preferred_element_type=F32)


def iota(shape, axis):
    return lax.broadcasted_iota(jnp.int32, shape, axis)


def common_rows(table, offset, cell, body):
    cell_x = lax.shift_right_logical(cell, 5).astype(F32)
    cell_y = (lax.shift_right_logical(cell, 3) & 3).astype(F32)
    cell_z = (cell & 7).astype(F32)
    field_one = (body & 1).astype(F32)
    pos_x = cell_x + offset[0]
    table[POS_X] = pos_x
    table[POS_Y] = cell_y + offset[1]
    table[POS_Z] = cell_z + offset[2]
    table[FIELD0] = 1.0 - field_one
    table[FIELD1] = field_one
    for x in range(6):
        table[WX + x] = spline(float(x) - pos_x)


def y_coords(tile_y):
    s = iota((8, LANES), 0)
    wrapped = jnp.where(s < 4, s + 4, s - 4)
    return jnp.where(tile_y == 0, s, wrapped).astype(F32)


def low_side(axis):
    return lax.axis_index(axis) % 2


def scatter_kernel(
    tile_ref, count_ref, offset, mass, velocity, affine, deform, cell, body, code,
    grid, planes, face_a, face_d,
    table, left_hi, left_lo, acc, turned,
):
    live = (iota((SLOTS, LANES), 0) < count_ref[0, 0]).astype(F32)
    common_rows(table, offset, cell[...], body[...])
    weighted = mass[...] * live
    table[MASS] = weighted
    for k in range(3):
        table[VEL + k] = weighted * velocity[k]
    stress = kirchhoff([deform[k] for k in range(9)])
    for k in range(9):
        table[AFF + k] = weighted * (affine[k] - 4.0 * DT * stress[k])

    acc[...] = jnp.zeros_like(acc)
    zeros = jnp.zeros((48, LANES), BF16)
    for u in range(2):
        left_hi[u, 0:48, LANES : 2 * LANES] = zeros
        left_lo[u, 0:48, LANES : 2 * LANES] = zeros

    def one(s, u):
        tile = tile_ref[s]
        tile_x = lax.shift_right_logical(tile, 6)
        tile_y = lax.shift_right_logical(tile, 5) & 1
        tile_z = tile & 31

        def row(k):
            return table[k, pl.ds(s, 1), :]

        dy = y_coords(tile_y) - row(POS_Y)
        wy = spline(dy)
        pos_x = row(POS_X)
        wxy = [wy * row(WX + x) for x in range(6)]

        def put(channel, column, values):
            for pair in range(3):
                hi, lo = split(jnp.concatenate(values[2 * pair : 2 * pair + 2], 0))
                at = channel * 48 + pair * 16
                left_hi[u, at : at + 16, column * LANES : (column + 1) * LANES] = hi
                left_lo[u, at : at + 16, column * LANES : (column + 1) * LANES] = lo

        m = row(MASS)
        put(0, 0, [w * m for w in wxy])
        for k in range(3):
            base = row(VEL + k) + row(AFF + 3 * k + 1) * dy
            ax = row(AFF + 3 * k)
            az = row(AFF + 3 * k + 2)
            put(1 + k, 0, [wxy[x] * (base + ax * (float(x) - pos_x)) for x in range(6)])
            put(1 + k, 1, [wxy[x] * az for x in range(6)])

        dz = iota((16, LANES), 0).astype(F32) - row(POS_Z)
        wz = spline(dz)
        mz = wz * dz
        parts = []
        for f in range(2):
            mask = row(FIELD0 + f)
            parts.append([split(wz * mask), split(mz * mask)])
        right_hi = jnp.concatenate(
            [jnp.concatenate([parts[f][0][0], parts[f][1][0]], 1) for f in range(2)], 0
        )
        right_lo = jnp.concatenate(
            [jnp.concatenate([parts[f][0][1], parts[f][1][1]], 1) for f in range(2)], 0
        )
        both = matmul_t(jnp.concatenate([right_hi, right_lo], 0), left_hi[u])
        rest = matmul_t(right_hi, left_lo[u])
        total = both[0:32] + both[32:64] + rest
        quadrant = tile_x * 2 + tile_y
        start = pl.multiple_of(tile_z * 8, 8)
        for f in range(2):
            acc[quadrant, f, pl.ds(start, 16), 0:192] += total[16 * f : 16 * f + 16]

    def step(pair, carry):
        one(pair * 2, 0)
        one(pair * 2 + 1, 1)
        return carry

    lax.fori_loop(0, SLOTS // 2, step, 0)

    for q in range(4):
        for f in range(2):
            for h in range(2):
                piece = acc[q, f, pl.ds(1 + LANES * h, LANES), 0:256]
                turned[q, f, :, h * LANES : (h + 1) * LANES] = piece.T[0:192]

    s8 = iota((8, DEPTH), 0)
    for f in range(2):
        for c in range(4):
            for x in range(SIDE):
                low = None
                high = None
                for tx in range(2):
                    local = x - 4 * tx
                    if not 0 <= local < 6:
                        continue
                    at = (c * 6 + local) * 8
                    v0 = turned[2 * tx, f, at : at + 8, :]
                    v1 = turned[2 * tx + 1, f, at : at + 8, :]
                    low_v = v0 + jnp.where(s8 >= 4, v1, 0.0)
                    high_v = jnp.where(s8 < 2, v1, 0.0)
                    low = low_v if low is None else low + low_v
                    high = high_v if high is None else high + high_v
                channel = 4 * f + c
                grid[channel, x, 0:8, :] = low
                grid[channel, x, 8:16, :] = high
                if x in (0, 1, 8, 9):
                    plane = x if x < 2 else x - 6
                    planes[channel, plane, 0:8, :] = low
                    planes[channel, plane, 8:16, :] = high

    side = low_side("gy")
    start_a = pl.multiple_of((1 - side) * 8, 8)
    start_d = pl.multiple_of(side * 8, 8)
    for face, start, owned in ((face_a, start_a, (1 - side) * 7), (face_d, start_d, side * 7)):
        for channel in range(8):
            for x in range(SIDE):
                at = channel * 20 + x * 2
                face[at : at + 2, :] = grid[channel, x, pl.ds(start, 2), :]
        for x in range(8):
            face[160 + x : 161 + x, :] = code[x, pl.ds(owned, 1), :].astype(F32)
        face[168:176, :] = jnp.zeros((8, DEPTH), F32)


def corner_kernel(planes, recv_a, recv_d, code, face_a, face_d, work, codes):
    side_y = low_side("gy")
    side_x = low_side("gx")
    work[...] = planes[...]
    for recv, start in ((recv_a, (1 - side_y) * 8), (recv_d, side_y * 8)):
        start = pl.multiple_of(start, 8)
        for channel in range(8):
            for plane in range(4):
                x = plane if plane < 2 else plane + 6
                at = channel * 20 + x * 2
                work[channel, plane, pl.ds(start, 2), :] += recv[at : at + 2, :]
    y_code_a = jnp.where(side_y == 0, 9, 0)
    y_code_d = jnp.where(side_y == 0, 0, 9)
    for face, first, owned in (
        (face_a, (1 - side_x) * 2, (1 - side_x) * 7),
        (face_d, side_x * 2, side_x * 7),
    ):
        for channel in range(8):
            for p in range(2):
                at = channel * 2 + p
                face[at * 8 : at * 8 + 8, :] = work[channel, first + p, 0:8, :]
                face[128 + at * 2 : 130 + at * 2, :] = work[channel, first + p, 8:10, :]
        codes[1:9, :] = code[owned].astype(F32)
        codes[pl.ds(y_code_a, 1), :] = recv_a[pl.ds(160 + owned, 1), :]
        codes[pl.ds(y_code_d, 1), :] = recv_d[pl.ds(160 + owned, 1), :]
        face[160:170, :] = codes[0:10, :]
        face[170:176, :] = jnp.zeros((6, DEPTH), F32)


def node_speeds(sums, code, inside):
    m0, m1 = sums[0], sums[4]
    r0 = 1.0 / jnp.maximum(m0, FLOOR)
    r1 = 1.0 / jnp.maximum(m1, FLOOR)
    rc = 1.0 / jnp.maximum(m0 + m1, FLOOR)
    share = jnp.minimum(1.0, jnp.minimum(m0, m1) * (1.0 / FLOOR))
    shifted = code + jnp.where(code >= 13.0, 1.0, 0.0)
    third = jnp.where(shifted >= 9.0, 1.0, 0.0) + jnp.where(shifted >= 18.0, 1.0, 0.0)
    rest = shifted - 9.0 * third
    second = jnp.where(rest >= 3.0, 1.0, 0.0) + jnp.where(rest >= 6.0, 1.0, 0.0)
    direction = [third - 1.0, second - 1.0, rest - 3.0 * second - 1.0]
    square = (
        direction[0] * direction[0] + direction[1] * direction[1] + direction[2] * direction[2]
    )
    inverse = jnp.where(square > 2.5, 1.0 / 3.0, jnp.where(square > 1.5, 0.5, 1.0))
    u0 = [sums[1 + k] * r0 for k in range(3)]
    u1 = [sums[5 + k] * r1 for k in range(3)]
    uc = [(sums[1 + k] + sums[5 + k]) * rc for k in range(3)]
    approach0 = sum((u0[k] - uc[k]) * direction[k] for k in range(3))
    approach1 = sum((uc[k] - u1[k]) * direction[k] for k in range(3))
    scale = share * inverse
    push0 = scale * jnp.maximum(approach0, 0.0)
    push1 = scale * jnp.maximum(approach1, 0.0)
    gravity = [0.0, 0.0, DT * GRAVITY]
    v0 = [(u0[k] - push0 * direction[k] + gravity[k]) * inside for k in range(3)]
    v1 = [(u1[k] + push1 * direction[k] + gravity[k]) * inside for k in range(3)]
    return v0, v1


def gather_kernel(
    last_x, last_y, tile_ref, count_ref, grid, y_a, y_d, x_a, x_d, code,
    offset, cell, body, deform,
    new_velocity, new_affine, new_deform, new_stress,
    table, work, codes, nodes_hi, nodes_lo, partial,
):
    side_y = low_side("gy")
    side_x = low_side("gx")
    common_rows(table, offset, cell[...], body[...])

    work[...] = grid[...]
    for x in range(8):
        codes[x + 1, 1:9, :] = code[x].astype(F32)
    for recv, start, halo in (
        (y_a, (1 - side_y) * 8, (1 - side_y) * 9),
        (y_d, side_y * 8, side_y * 9),
    ):
        start = pl.multiple_of(start, 8)
        for channel in range(8):
            for x in range(SIDE):
                at = channel * 20 + x * 2
                work[channel, x, pl.ds(start, 2), :] += recv[at : at + 2, :]
        for x in range(8):
            codes[x + 1, pl.ds(halo, 1), :] = recv[160 + x : 161 + x, :]
    for recv, first, halo in (
        (x_a, (1 - side_x) * 8, (1 - side_x) * 9),
        (x_d, side_x * 8, side_x * 9),
    ):
        for channel in range(8):
            for p in range(2):
                at = channel * 2 + p
                work[channel, first + p, 0:8, :] += recv[at * 8 : at * 8 + 8, :]
                work[channel, first + p, 8:10, :] += recv[128 + at * 2 : 130 + at * 2, :]
        codes[halo, 0:10, :] = recv[160:170, :]

    index_x = lax.axis_index("gx")
    index_y = lax.axis_index("gy")
    s8 = iota((8, LANES), 0)
    lane = iota((8, LANES), 1)
    inside_low = jnp.where((s8 == 0) & (index_y == 0), 0.0, 1.0)
    inside_high = jnp.where((s8 == 1) & (index_y == last_y), 0.0, 1.0)

    def tiles(v):
        a, b = v
        first = jnp.where(lane < 1, 0.0, pltpu.roll(a, 1, 1))
        second = jnp.where(lane < 9, pltpu.roll(a, 9, 1), pltpu.roll(b, 9, 1))
        third = jnp.where(lane < 17, pltpu.roll(b, 17, 1), 0.0)
        return first, second, third

    def node_step(pair, carry):
        found = []
        for k in range(2):
            x = pair * 2 + k
            edge = ((x == 0) & (index_x == 0)) | ((x == SIDE - 1) & (index_x == last_x))
            inside_x = jnp.where(edge, 0.0, 1.0)
            rows = []
            for r in range(2):
                inside = (inside_low if r == 0 else inside_high) * inside_x
                halves = []
                for h in range(2):
                    lanes = slice(h * LANES, (h + 1) * LANES)
                    sums = [work[c, x, 8 * r : 8 * r + 8, lanes] for c in range(8)]
                    halves.append(node_speeds(sums, codes[x, 8 * r : 8 * r + 8, lanes], inside))
                rows.append(halves)
            found.append(rows)
        at = pl.multiple_of(pair * 16, 16)
        for f in range(2):
            for c in range(3):
                ready = []
                for k in range(2):
                    low = tiles([found[k][0][h][f][c] for h in range(2)])
                    high = tiles([found[k][1][h][f][c] for h in range(2)])
                    ready.append((low, high))
                for j in range(3):
                    for ty in range(2):
                        pieces = []
                        for k in range(2):
                            low, high = ready[k][0][j], ready[k][1][j]
                            pieces.append(low if ty == 0 else jnp.where(s8 < 2, high, low))
                        hi, lo = split(jnp.concatenate(pieces, 0))
                        lanes = slice(f * LANES, (f + 1) * LANES)
                        nodes_hi[ty, j, c, pl.ds(at, 16), lanes] = hi
                        nodes_lo[ty, j, c, pl.ds(at, 16), lanes] = lo
        return carry

    lax.fori_loop(0, SIDE // 2, node_step, 0)

    def one(s):
        tile = tile_ref[s]
        tile_x = lax.shift_right_logical(tile, 6)
        tile_y = lax.shift_right_logical(tile, 5) & 1
        tile_z = tile & 31
        j = (tile_z >= 15).astype(jnp.int32) + (tile_z >= 30).astype(jnp.int32)
        local = tile_z - 15 * j
        odd = local & 1

        def row(k):
            return table[k, pl.ds(s, 1), :]

        pos_z = row(POS_Z) + (odd * 8).astype(F32)
        tile_row = lax.shift_right_logical(local, 1)
        windows = []
        for r in range(2):
            dz = (iota((16, LANES), 0) + 16 * r).astype(F32) - pos_z
            wz = spline(dz)
            mz = wz * dz
            for f in range(2):
                mask = row(FIELD0 + f)
                windows.append(split(wz * mask) + split(mz * mask))
        none = jnp.zeros((16, LANES), BF16)

        def spread(f, part):
            w0, w1 = windows[f][part], windows[2 + f][part]
            rows = []
            for k in range(8):
                tail = jnp.where(tile_row == k - 1, w1, none) if k else none
                rows.append(jnp.where(tile_row == k, w0, tail))
            return jnp.concatenate(rows, 0)

        def weights(part):
            columns = [
                jnp.concatenate([spread(f, p) for f in range(2)], 0) for p in (part, part + 2)
            ]
            return jnp.concatenate(columns, 1)

        first = pl.multiple_of(tile_x * 32, 32)
        hi = [nodes_hi[tile_y, j, c, pl.ds(first, 48), :] for c in range(3)]
        lo = [nodes_lo[tile_y, j, c, pl.ds(first, 48), :] for c in range(3)]
        weights_hi = weights(0)
        nodes = jnp.concatenate(hi, 0)
        summed = (
            matmul(nodes, weights_hi)
            + matmul(jnp.concatenate(lo, 0), weights_hi)
            + matmul(nodes, weights(1))
        )

        dy = y_coords(tile_y) - row(POS_Y)
        wy = spline(dy)
        pos_x = row(POS_X)
        wxy = [wy * row(WX + x) for x in range(6)]
        dx = [float(x) - pos_x for x in range(6)]
        place = pl.ds(pl.multiple_of(s * 8, 8), 8)
        for c in range(3):
            speed = jnp.zeros((8, LANES), F32)
            along_x = jnp.zeros((8, LANES), F32)
            along_z = jnp.zeros((8, LANES), F32)
            for x in range(6):
                at = (c * 6 + x) * 8
                part = wxy[x] * summed[at : at + 8, 0:LANES]
                speed = speed + part
                along_x = along_x + part * dx[x]
                along_z = along_z + wxy[x] * summed[at : at + 8, LANES : 2 * LANES]
            partial[4 * c, place, :] = speed
            partial[4 * c + 1, place, :] = along_x
            partial[4 * c + 2, place, :] = speed * dy
            partial[4 * c + 3, place, :] = along_z

    def step(pair, carry):
        one(pair * 2)
        one(pair * 2 + 1)
        return carry

    lax.fori_loop(0, SLOTS // 2, step, 0)

    live = (iota((SLOTS, LANES), 0) < count_ref[0, 0]).astype(F32)

    def collect(k):
        total = partial[k, pl.ds(0, SLOTS, stride=8), :]
        for y in range(1, 8):
            total = total + partial[k, pl.ds(y, SLOTS, stride=8), :]
        return total * live

    moved = []
    for c in range(3):
        new_velocity[c] = collect(4 * c)
        for k in range(3):
            value = 4.0 * collect(4 * c + 1 + k)
            new_affine[3 * c + k] = value
            moved.append(value)
    old = [deform[k] for k in range(9)]
    fresh = []
    for i in range(3):
        for j in range(3):
            value = old[3 * i + j]
            for k in range(3):
                value = value + DT * moved[3 * i + k] * old[3 * k + j]
            fresh.append(value * live)
    for k in range(9):
        new_deform[k] = fresh[k]
    stress = kirchhoff(fresh)
    for k, entry in enumerate((0, 4, 8, 1, 2, 5)):
        new_stress[k] = stress[entry] * live


def vmem(shape, dtype=F32):
    return pltpu.VMEM(shape, dtype)


def swap(block, axis, shift):
    size = lax.axis_size(axis)
    route = [(i, ((i + shift) ^ 1) - shift) for i in range(size)]
    return lax.ppermute(block, axis, [(i, k) for i, k in route if 0 <= k < size])


def per_device(
    offset, particle_mass, velocity, affine, deform,
    particle_cell, body_id, slot_tile_number, block_count, normal_code,
):
    params = pltpu.CompilerParams(vmem_limit_bytes=VMEM_LIMIT)
    smem = pl.BlockSpec(memory_space=pltpu.SMEM)
    whole = pl.BlockSpec(memory_space=pltpu.VMEM)
    face = jax.ShapeDtypeStruct((FACE_ROWS, DEPTH), F32)

    grid, planes, y_a, y_d = pl.pallas_call(
        scatter_kernel,
        out_shape=(
            jax.ShapeDtypeStruct((8, SIDE, 16, DEPTH), F32),
            jax.ShapeDtypeStruct((8, 4, 16, DEPTH), F32),
            face,
            face,
        ),
        in_specs=[smem, smem] + [whole] * 8,
        out_specs=(whole,) * 4,
        scratch_shapes=[
            vmem((SCATTER_ROWS, SLOTS, LANES)),
            vmem((2, 192, 256), BF16),
            vmem((2, 192, 256), BF16),
            vmem((4, 2, 272, 256)),
            vmem((4, 2, 192, DEPTH)),
        ],
        compiler_params=params,
        name="scatter",
    )(
        slot_tile_number, block_count, offset, particle_mass, velocity, affine, deform,
        particle_cell, body_id, normal_code,
    )
    got_y_a = swap(y_a, "gy", 0)
    got_y_d = swap(y_d, "gy", 1)
    x_a, x_d = pl.pallas_call(
        corner_kernel,
        out_shape=(face, face),
        in_specs=[whole] * 4,
        out_specs=(whole,) * 2,
        scratch_shapes=[vmem((8, 4, 16, DEPTH)), vmem((16, DEPTH))],
        compiler_params=params,
        name="corners",
    )(planes, got_y_a, got_y_d, normal_code)
    got_x_a = swap(x_a, "gx", 0)
    got_x_d = swap(x_d, "gx", 1)

    slots, particles = particle_mass.shape
    return pl.pallas_call(
        functools.partial(gather_kernel, lax.axis_size("gx") - 1, lax.axis_size("gy") - 1),
        out_shape=tuple(
            jax.ShapeDtypeStruct((k, slots, particles), F32) for k in (3, 9, 9, 6)
        ),
        in_specs=[smem, smem] + [whole] * 10,
        out_specs=(whole,) * 4,
        scratch_shapes=[
            vmem((GATHER_ROWS, SLOTS, LANES)),
            vmem((8, SIDE, 16, DEPTH)),
            vmem((SIDE, 16, DEPTH)),
            vmem((2, 3, 3, 8 * SIDE, 256), BF16),
            vmem((2, 3, 3, 8 * SIDE, 256), BF16),
            vmem((12, 8 * SLOTS, LANES)),
        ],
        compiler_params=params,
        name="gather",
    )(
        slot_tile_number, block_count, grid, got_y_a, got_y_d, got_x_a, got_x_d, normal_code,
        offset, particle_cell, body_id, deform,
    )


def solution(mesh):
    both = ("gx", "gy")
    field = P(None, both, None)
    flat = P(both, None)
    return jax.shard_map(
        per_device,
        mesh=mesh,
        in_specs=(
            field, flat, field, field, field, flat, flat, P(both), P("gx", "gy"),
            P("gx", "gy", None),
        ),
        out_specs=(field,) * 4,
        check_vma=False,
    )
```

```python
import functools

import jax
import jax.numpy as jnp
from jax import lax
from jax.experimental import pallas as pl
from jax.experimental.pallas import tpu as pltpu
from jax.sharding import PartitionSpec as P

DT = 0.1
MU = 2.0
LAM = 3.0
GRAVITY = -2.0
FLOOR = 0.25

F32 = jnp.float32
BF16 = jnp.bfloat16
VMEM_LIMIT = 24 * 1024 * 1024

SIDE = 10
DEPTH = 256
SLOTS = 24
LANES = 128
FACE_ROWS = 176

POS_Y, POS_Z, FIELD0, FIELD1, POS_X, LIVE, WX = 0, 1, 2, 3, 4, 5, 6
GATHER_ROWS = WX + 6
MASS = GATHER_ROWS
VEL = MASS + 1
AFF = VEL + 3
SCATTER_ROWS = AFF + 9


def spline(distance):
    size = jnp.abs(distance)
    outer = jnp.maximum(1.5 - size, 0.0)
    inner = jnp.maximum(0.5 - size, 0.0)
    return 0.5 * outer * outer - 1.5 * inner * inner


def determinant(m):
    return (
        m[0] * (m[4] * m[8] - m[5] * m[7])
        - m[1] * (m[3] * m[8] - m[5] * m[6])
        + m[2] * (m[3] * m[7] - m[4] * m[6])
    )


def kirchhoff(m):
    ratio = determinant(m)
    pressure = 0.5 * LAM * (ratio * ratio - 1.0)
    entries = []
    for i in range(3):
        for j in range(3):
            e = m[3 * i] * m[3 * j] + m[3 * i + 1] * m[3 * j + 1] + m[3 * i + 2] * m[3 * j + 2]
            entries.append(MU * (e - 1.0) + pressure if i == j else MU * e)
    return entries


def split(x):
    high = x.astype(BF16)
    return high, (x - high.astype(F32)).astype(BF16)


def matmul_t(a, b):
    return lax.dot_general(a, b, (((1,), (1,)), ((), ())), preferred_element_type=F32)


def matmul(a, b):
    return lax.dot_general(a, b, (((1,), (0,)), ((), ())), preferred_element_type=F32)


def iota(shape, axis):
    return lax.broadcasted_iota(jnp.int32, shape, axis)


def common_rows(table, offset, cell, body):
    cell_x = lax.shift_right_logical(cell, 5).astype(F32)
    cell_y = (lax.shift_right_logical(cell, 3) & 3).astype(F32)
    cell_z = (cell & 7).astype(F32)
    field_one = (body & 1).astype(F32)
    pos_x = cell_x + offset[0]
    table[POS_X] = pos_x
    table[POS_Y] = cell_y + offset[1]
    table[POS_Z] = cell_z + offset[2]
    table[FIELD0] = 1.0 - field_one
    table[FIELD1] = field_one
    for x in range(6):
        table[WX + x] = spline(float(x) - pos_x)


def y_coords(tile_y):
    s = iota((8, LANES), 0)
    wrapped = jnp.where(s < 4, s + 4, s - 4)
    return jnp.where(tile_y == 0, s, wrapped).astype(F32)


def low_side(axis):
    return lax.axis_index(axis) % 2


def scatter_kernel(
    count_ref, tile_in, offset_in, mass_in, velocity_in, affine_in, deform_in, cell_in, body_in,
    code_in,
    grid, face_a, face_d, table, codes,
    tile_ref, offset, mass, velocity, affine, deform, cell, body, code,
    rows, left_hi, left_lo, acc, turned, sems,
):
    pairs = (
        (tile_in, tile_ref), (deform_in, deform), (affine_in, affine),
        (offset_in, offset), (velocity_in, velocity), (mass_in, mass), (cell_in, cell),
        (body_in, body), (code_in, code),
    )
    copies = [
        pltpu.make_async_copy(src, dst, sems.at[i]) for i, (src, dst) in enumerate(pairs)
    ]
    for copy in copies:
        copy.start()
    acc[...] = jnp.zeros_like(acc)
    codes[...] = jnp.zeros_like(codes)
    zeros = jnp.zeros((48, LANES), BF16)
    for u in range(2):
        left_hi[u, 0:48, LANES : 2 * LANES] = zeros
        left_lo[u, 0:48, LANES : 2 * LANES] = zeros
    for copy in copies:
        copy.wait()

    for x in range(8):
        codes[x + 1, 1:9, :] = code[x].astype(F32)
    live = (iota((SLOTS, LANES), 0) < count_ref[0, 0]).astype(F32)
    table[LIVE] = live
    common_rows(table, offset, cell[...], body[...])
    weighted = mass[...] * live
    rows[0] = weighted
    for k in range(3):
        rows[VEL - MASS + k] = weighted * velocity[k]
    stress = kirchhoff([deform[k] for k in range(9)])
    for k in range(9):
        rows[AFF - MASS + k] = weighted * (affine[k] - 4.0 * DT * stress[k])

    def one(s, u):
        tile = tile_ref[s]
        tile_x = lax.shift_right_logical(tile, 6)
        tile_y = lax.shift_right_logical(tile, 5) & 1
        tile_z = tile & 31

        def row(k):
            return (table if k < MASS else rows)[k if k < MASS else k - MASS, pl.ds(s, 1), :]

        dy = y_coords(tile_y) - row(POS_Y)
        wy = spline(dy)
        pos_x = row(POS_X)
        wxy = [wy * row(WX + x) for x in range(6)]

        def put(channel, column, values):
            for pair in range(3):
                hi, lo = split(jnp.concatenate(values[2 * pair : 2 * pair + 2], 0))
                at = channel * 48 + pair * 16
                left_hi[u, at : at + 16, column * LANES : (column + 1) * LANES] = hi
                left_lo[u, at : at + 16, column * LANES : (column + 1) * LANES] = lo

        m = row(MASS)
        put(0, 0, [w * m for w in wxy])
        for k in range(3):
            base = row(VEL + k) + row(AFF + 3 * k + 1) * dy
            ax = row(AFF + 3 * k)
            az = row(AFF + 3 * k + 2)
            put(1 + k, 0, [wxy[x] * (base + ax * (float(x) - pos_x)) for x in range(6)])
            put(1 + k, 1, [wxy[x] * az for x in range(6)])

        dz = iota((16, LANES), 0).astype(F32) - row(POS_Z)
        wz = spline(dz)
        mz = wz * dz
        parts = []
        for f in range(2):
            mask = row(FIELD0 + f)
            parts.append([split(wz * mask), split(mz * mask)])
        right_hi = jnp.concatenate(
            [jnp.concatenate([parts[f][0][0], parts[f][1][0]], 1) for f in range(2)], 0
        )
        right_lo = jnp.concatenate(
            [jnp.concatenate([parts[f][0][1], parts[f][1][1]], 1) for f in range(2)], 0
        )
        both = matmul_t(jnp.concatenate([right_hi, right_lo], 0), left_hi[u])
        rest = matmul_t(right_hi, left_lo[u])
        total = both[0:32] + both[32:64] + rest
        quadrant = tile_x * 2 + tile_y
        start = pl.multiple_of(tile_z * 8, 8)
        for f in range(2):
            acc[quadrant, f, pl.ds(start, 16), 0:192] += total[16 * f : 16 * f + 16]

    def step(pair, carry):
        one(pair * 2, 0)
        one(pair * 2 + 1, 1)
        return carry

    lax.fori_loop(0, SLOTS // 2, step, 0)

    for q in range(4):
        for f in range(2):
            for h in range(2):
                piece = acc[q, f, pl.ds(1 + LANES * h, LANES), 0:256]
                turned[q, f, :, h * LANES : (h + 1) * LANES] = piece.T[0:192]

    s8 = iota((8, DEPTH), 0)
    for f in range(2):
        for c in range(4):
            for x in range(SIDE):
                low = None
                high = None
                for tx in range(2):
                    local = x - 4 * tx
                    if not 0 <= local < 6:
                        continue
                    at = (c * 6 + local) * 8
                    v0 = turned[2 * tx, f, at : at + 8, :]
                    v1 = turned[2 * tx + 1, f, at : at + 8, :]
                    low_v = v0 + jnp.where(s8 >= 4, v1, 0.0)
                    high_v = jnp.where(s8 < 2, v1, 0.0)
                    low = low_v if low is None else low + low_v
                    high = high_v if high is None else high + high_v
                channel = 4 * f + c
                grid[channel, x, 0:8, :] = low
                grid[channel, x, 8:16, :] = high

    side = low_side("gy")
    start_a = pl.multiple_of((1 - side) * 8, 8)
    start_d = pl.multiple_of(side * 8, 8)
    for face, start, owned in ((face_a, start_a, (1 - side) * 7), (face_d, start_d, side * 7)):
        for channel in range(8):
            for x in range(SIDE):
                at = channel * 20 + x * 2
                face[at : at + 2, :] = grid[channel, x, pl.ds(start, 2), :]
        for x in range(8):
            face[160 + x : 161 + x, :] = code[x, pl.ds(owned, 1), :].astype(F32)
        face[168:176, :] = jnp.zeros((8, DEPTH), F32)


def prepare_kernel(tile_ref, table, right_hi, right_lo):
    none = jnp.zeros((16, LANES), BF16)

    def one(s, carry):
        tile_z = tile_ref[s] & 31
        j = (tile_z >= 15).astype(jnp.int32) + (tile_z >= 30).astype(jnp.int32)
        local = tile_z - 15 * j
        odd = local & 1
        tile_row = lax.shift_right_logical(local, 1)
        pos_z = table[POS_Z, pl.ds(s, 1), :] + (odd * 8).astype(F32)
        windows = []
        for r in range(2):
            dz = (iota((16, LANES), 0) + 16 * r).astype(F32) - pos_z
            wz = spline(dz)
            mz = wz * dz
            for f in range(2):
                mask = table[FIELD0 + f, pl.ds(s, 1), :]
                windows.append(split(wz * mask) + split(mz * mask))
        for f in range(2):
            for part in range(4):
                w0, w1 = windows[f][part], windows[2 + f][part]
                out = right_hi if part % 2 == 0 else right_lo
                column = part // 2 * LANES
                for k in range(8):
                    tail = jnp.where(tile_row == k - 1, w1, none) if k else none
                    at = f * LANES + 16 * k
                    out[s, at : at + 16, column : column + LANES] = jnp.where(
                        tile_row == k, w0, tail
                    )
        return carry

    lax.fori_loop(0, SLOTS, one, 0)


def corner_kernel(order, grid, recv_a, recv_d, codes, face_a, face_d, edge, edge_codes):
    side_y = low_side("gy")
    side_x = low_side("gx")
    for plane in range(4):
        x = plane if plane < 2 else plane + 6
        for channel in range(8):
            edge[channel, plane, :, :] = grid[channel, x, :, :]
    for recv, start in ((recv_a, (1 - side_y) * 8), (recv_d, side_y * 8)):
        start = pl.multiple_of(start, 8)
        for channel in range(8):
            for plane in range(4):
                x = plane if plane < 2 else plane + 6
                at = channel * 20 + x * 2
                edge[channel, plane, pl.ds(start, 2), :] += recv[at : at + 2, :]
    edge_codes[0] = codes[1]
    edge_codes[1] = codes[8]
    for recv, halo in ((recv_a, (1 - side_y) * 9), (recv_d, side_y * 9)):
        edge_codes[0, pl.ds(halo, 1), :] = recv[160:161, :]
        edge_codes[1, pl.ds(halo, 1), :] = recv[167:168, :]
    for face, high in ((face_a, 1 - side_x), (face_d, side_x)):
        first = high * 2
        for channel in range(8):
            for p in range(2):
                at = channel * 2 + p
                face[at * 8 : at * 8 + 8, :] = edge[channel, first + p, 0:8, :]
                face[128 + at * 2 : 130 + at * 2, :] = edge[channel, first + p, 8:10, :]
        face[160:170, :] = edge_codes[high, 0:10, :]
        face[170:176, :] = jnp.zeros((6, DEPTH), F32)


def node_speeds(sums, code, inside):
    m0, m1 = sums[0], sums[4]
    r0 = 1.0 / jnp.maximum(m0, FLOOR)
    r1 = 1.0 / jnp.maximum(m1, FLOOR)
    rc = 1.0 / jnp.maximum(m0 + m1, FLOOR)
    share = jnp.minimum(1.0, jnp.minimum(m0, m1) * (1.0 / FLOOR))
    shifted = code + jnp.where(code >= 13.0, 1.0, 0.0)
    third = jnp.where(shifted >= 9.0, 1.0, 0.0) + jnp.where(shifted >= 18.0, 1.0, 0.0)
    rest = shifted - 9.0 * third
    second = jnp.where(rest >= 3.0, 1.0, 0.0) + jnp.where(rest >= 6.0, 1.0, 0.0)
    direction = [third - 1.0, second - 1.0, rest - 3.0 * second - 1.0]
    square = (
        direction[0] * direction[0] + direction[1] * direction[1] + direction[2] * direction[2]
    )
    inverse = jnp.where(square > 2.5, 1.0 / 3.0, jnp.where(square > 1.5, 0.5, 1.0))
    u0 = [sums[1 + k] * r0 for k in range(3)]
    u1 = [sums[5 + k] * r1 for k in range(3)]
    uc = [(sums[1 + k] + sums[5 + k]) * rc for k in range(3)]
    approach0 = sum((u0[k] - uc[k]) * direction[k] for k in range(3))
    approach1 = sum((uc[k] - u1[k]) * direction[k] for k in range(3))
    scale = share * inverse
    push0 = scale * jnp.maximum(approach0, 0.0)
    push1 = scale * jnp.maximum(approach1, 0.0)
    gravity = [0.0, 0.0, DT * GRAVITY]
    v0 = [(u0[k] - push0 * direction[k] + gravity[k]) * inside for k in range(3)]
    v1 = [(u1[k] + push1 * direction[k] + gravity[k]) * inside for k in range(3)]
    return v0, v1


def store_nodes(pair, x_first, sums_at, code_at, last, nodes_hi, nodes_lo):
    index_x = lax.axis_index("gx")
    index_y = lax.axis_index("gy")
    s8 = iota((8, LANES), 0)
    lane = iota((8, LANES), 1)
    inside_low = jnp.where((s8 == 0) & (index_y == 0), 0.0, 1.0)
    inside_high = jnp.where((s8 == 1) & (index_y == last[1]), 0.0, 1.0)

    def tiles(a, b):
        first = jnp.where(lane < 1, 0.0, pltpu.roll(a, 1, 1))
        second = jnp.where(lane < 9, pltpu.roll(a, 9, 1), pltpu.roll(b, 9, 1))
        third = jnp.where(lane < 17, pltpu.roll(b, 17, 1), 0.0)
        return first, second, third

    found = []
    for k in range(2):
        x = x_first + k
        edge = ((x == 0) & (index_x == 0)) | ((x == SIDE - 1) & (index_x == last[0]))
        inside_x = jnp.where(edge, 0.0, 1.0)
        rows = []
        for r in range(2):
            inside = (inside_low if r == 0 else inside_high) * inside_x
            halves = []
            for h in range(2):
                sums = [sums_at(c, k, r, h) for c in range(8)]
                halves.append(node_speeds(sums, code_at(k, r, h), inside))
            rows.append(halves)
        found.append(rows)
    at = pl.multiple_of(pair * 16, 16)
    for f in range(2):
        for c in range(3):
            ready = []
            for k in range(2):
                ready.append([tiles(*(found[k][r][h][f][c] for h in range(2))) for r in range(2)])
            for j in range(3):
                for ty in range(2):
                    pieces = []
                    for k in range(2):
                        low, high = ready[k][0][j], ready[k][1][j]
                        pieces.append(low if ty == 0 else jnp.where(s8 < 2, high, low))
                    hi, lo = split(jnp.concatenate(pieces, 0))
                    lanes = slice(f * LANES, (f + 1) * LANES)
                    nodes_hi[ty, j, c, pl.ds(at, 16), lanes] = hi
                    nodes_lo[ty, j, c, pl.ds(at, 16), lanes] = lo


def half(h):
    return slice(h * LANES, (h + 1) * LANES)


def middle_kernel(last, order, grid, y_a, y_d, codes, nodes_hi, nodes_lo, work, own):
    side_y = low_side("gy")
    for x in range(2, 8):
        own[x - 2] = codes[x]
        for channel in range(8):
            work[channel, x - 2, :, :] = grid[channel, x, :, :]
    for recv, high in ((y_a, 1 - side_y), (y_d, side_y)):
        start = pl.multiple_of(high * 8, 8)
        for x in range(2, 8):
            for channel in range(8):
                at = channel * 20 + x * 2
                work[channel, x - 2, pl.ds(start, 2), :] += recv[at : at + 2, :]
            own[x - 2, pl.ds(high * 9, 1), :] = recv[159 + x : 160 + x, :]

    def step(pair, carry):
        x = pair * 2

        def sums_at(c, k, r, h):
            return work[c, x - 2 + k, 8 * r : 8 * r + 8, half(h)]

        def code_at(k, r, h):
            return own[x - 2 + k, 8 * r : 8 * r + 8, half(h)]

        store_nodes(pair, x, sums_at, code_at, last, nodes_hi, nodes_lo)
        return carry

    lax.fori_loop(1, 4, step, 0)


def gather_kernel(
    last, tile_ref, mid_hi, mid_lo, edge, edge_codes, x_a, x_d,
    table, right_hi, right_lo, deform,
    new_velocity, new_affine, new_deform, new_stress, nodes_hi, nodes_lo,
    work, own, partial,
):
    side_x = low_side("gx")
    for recv, high in ((x_a, 1 - side_x), (x_d, side_x)):
        first = high * 2
        for channel in range(8):
            for p in range(2):
                at = channel * 2 + p
                plane = first + p
                work[channel, plane, 0:8, :] = (
                    edge[channel, plane, 0:8, :] + recv[at * 8 : at * 8 + 8, :]
                )
                work[channel, plane, 8:16, :] = edge[channel, plane, 8:16, :]
                work[channel, plane, 8:10, :] += recv[128 + at * 2 : 130 + at * 2, :]
        own[first + high, 0:10, :] = recv[160:170, :]
        own[first + 1 - high] = edge_codes[high]

    def edge_step(high, carry):
        def sums_at(c, k, r, h):
            return work[c, high * 2 + k, 8 * r : 8 * r + 8, half(h)]

        def code_at(k, r, h):
            return own[high * 2 + k, 8 * r : 8 * r + 8, half(h)]

        store_nodes(high * 4, high * 8, sums_at, code_at, last, nodes_hi, nodes_lo)
        return carry

    lax.fori_loop(0, 2, edge_step, 0)

    def one(s):
        tile = tile_ref[s]
        tile_x = lax.shift_right_logical(tile, 6)
        tile_y = lax.shift_right_logical(tile, 5) & 1
        tile_z = tile & 31
        j = (tile_z >= 15).astype(jnp.int32) + (tile_z >= 30).astype(jnp.int32)

        def row(k):
            return table[k, pl.ds(s, 1), :]

        first = pl.multiple_of(tile_x * 32, 32)
        hi = [nodes_hi[tile_y, j, c, pl.ds(first, 48), :] for c in range(3)]
        lo = [nodes_lo[tile_y, j, c, pl.ds(first, 48), :] for c in range(3)]
        weights = right_hi[s]
        nodes = jnp.concatenate(hi, 0)
        summed = (
            matmul(nodes, weights)
            + matmul(jnp.concatenate(lo, 0), weights)
            + matmul(nodes, right_lo[s])
        )

        dy = y_coords(tile_y) - row(POS_Y)
        wy = spline(dy)
        pos_x = row(POS_X)
        wxy = [wy * row(WX + x) for x in range(6)]
        place = pl.ds(pl.multiple_of(s * 8, 8), 8)
        for c in range(3):
            speed = along_x = along_z = None
            for x in range(5, -1, -1):
                at = (c * 6 + x) * 8
                part = wxy[x] * summed[at : at + 8, 0:LANES]
                moment = wxy[x] * summed[at : at + 8, LANES : 2 * LANES]
                speed = part if speed is None else speed + part
                along_z = moment if along_z is None else along_z + moment
                if x:
                    along_x = speed if along_x is None else along_x + speed
            partial[4 * c, place, :] = speed
            partial[4 * c + 1, place, :] = along_x - pos_x * speed
            partial[4 * c + 2, place, :] = speed * dy
            partial[4 * c + 3, place, :] = along_z

    def step(pair, carry):
        one(pair * 2)
        one(pair * 2 + 1)
        return carry

    lax.fori_loop(0, SLOTS // 2, step, 0)

    live = table[LIVE]

    def collect(k):
        total = partial[k, pl.ds(0, SLOTS, stride=8), :]
        for y in range(1, 8):
            total = total + partial[k, pl.ds(y, SLOTS, stride=8), :]
        return total * live

    moved = []
    for c in range(3):
        new_velocity[c] = collect(4 * c)
        for k in range(3):
            value = 4.0 * collect(4 * c + 1 + k)
            new_affine[3 * c + k] = value
            moved.append(value)
    old = [deform[k] for k in range(9)]
    fresh = []
    for i in range(3):
        for j in range(3):
            value = old[3 * i + j]
            for k in range(3):
                value = value + DT * moved[3 * i + k] * old[3 * k + j]
            fresh.append(value * live)
    for k in range(9):
        new_deform[k] = fresh[k]
    stress = kirchhoff(fresh)
    for k, entry in enumerate((0, 4, 8, 1, 2, 5)):
        new_stress[k] = stress[entry] * live


def vmem(shape, dtype=F32):
    return pltpu.VMEM(shape, dtype)


def cost(flops):
    return pl.CostEstimate(flops=flops, bytes_accessed=4000000, transcendentals=0)


def swap(block, axis, shift):
    size = lax.axis_size(axis)
    route = [(i, ((i + shift) ^ 1) - shift) for i in range(size)]
    return lax.ppermute(block, axis, [(i, k) for i, k in route if 0 <= k < size])


def per_device(
    offset, particle_mass, velocity, affine, deform,
    particle_cell, body_id, slot_tile_number, block_count, normal_code,
):
    params = pltpu.CompilerParams(vmem_limit_bytes=VMEM_LIMIT)
    smem = pl.BlockSpec(memory_space=pltpu.SMEM)
    hbm = pl.BlockSpec(memory_space=pltpu.HBM)
    whole = pl.BlockSpec(memory_space=pltpu.VMEM)
    face = jax.ShapeDtypeStruct((FACE_ROWS, DEPTH), F32)
    nodes = jax.ShapeDtypeStruct((2, 3, 3, 8 * SIDE, 256), BF16)
    right = jax.ShapeDtypeStruct((SLOTS, 256, 256), BF16)
    last = (lax.axis_size("gx") - 1, lax.axis_size("gy") - 1)
    inputs = (
        slot_tile_number, offset, particle_mass, velocity, affine, deform, particle_cell,
        body_id, normal_code,
    )

    grid, y_a, y_d, table, codes = pl.pallas_call(
        scatter_kernel,
        out_shape=(
            jax.ShapeDtypeStruct((8, SIDE, 16, DEPTH), F32),
            face,
            face,
            jax.ShapeDtypeStruct((GATHER_ROWS, SLOTS, LANES), F32),
            jax.ShapeDtypeStruct((SIDE, 16, DEPTH), F32),
        ),
        in_specs=[smem] + [hbm] * 9,
        out_specs=(whole,) * 5,
        scratch_shapes=[pltpu.SMEM(x.shape, x.dtype) for x in inputs[:1]]
        + [vmem(x.shape, x.dtype) for x in inputs[1:]]
        + [
            vmem((SCATTER_ROWS - GATHER_ROWS, SLOTS, LANES)),
            vmem((2, 192, 256), BF16),
            vmem((2, 192, 256), BF16),
            vmem((4, 2, 272, 256)),
            vmem((4, 2, 192, DEPTH)),
            pltpu.SemaphoreType.DMA((9,)),
        ],
        compiler_params=params,
        cost_estimate=pl.CostEstimate(flops=10**9, bytes_accessed=1, transcendentals=0),
        name="scatter",
    )(
        block_count,
        *(pltpu.with_memory_space_constraint(x, pltpu.HBM) for x in inputs),
    )
    got_y_a = swap(y_a, "gy", 0)
    got_y_d = swap(y_d, "gy", 1)
    right_hi, right_lo = pl.pallas_call(
        prepare_kernel,
        out_shape=(right, right),
        in_specs=[smem, whole],
        out_specs=(whole,) * 2,
        compiler_params=params,
        cost_estimate=cost(3000000),
        name="prepare",
    )(slot_tile_number, table)
    x_a, x_d, edge, edge_codes = pl.pallas_call(
        corner_kernel,
        out_shape=(
            face,
            face,
            jax.ShapeDtypeStruct((8, 4, 16, DEPTH), F32),
            jax.ShapeDtypeStruct((2, 16, DEPTH), F32),
        ),
        in_specs=[pl.BlockSpec(memory_space=pl.ANY)] + [whole] * 4,
        out_specs=(whole,) * 4,
        compiler_params=params,
        name="corners",
    )(right_hi, grid, got_y_a, got_y_d, codes)
    got_x_a = swap(x_a, "gx", 0)
    got_x_d = swap(x_d, "gx", 1)
    mid_hi, mid_lo = pl.pallas_call(
        functools.partial(middle_kernel, last),
        out_shape=(nodes, nodes),
        in_specs=[pl.BlockSpec(memory_space=pl.ANY)] + [whole] * 4,
        out_specs=(whole,) * 2,
        scratch_shapes=[vmem((8, 6, 16, DEPTH)), vmem((6, 16, DEPTH))],
        compiler_params=params,
        cost_estimate=cost(3000000),
        name="middle",
    )(edge_codes, grid, got_y_a, got_y_d, codes)

    slots, particles = particle_mass.shape
    out = pl.pallas_call(
        functools.partial(gather_kernel, last),
        out_shape=tuple(jax.ShapeDtypeStruct((k, slots, particles), F32) for k in (3, 9, 9, 6))
        + (nodes, nodes),
        in_specs=[smem] + [whole] * 10,
        out_specs=(whole,) * 6,
        scratch_shapes=[
            vmem((8, 4, 16, DEPTH)),
            vmem((4, 16, DEPTH)),
            vmem((12, 8 * SLOTS, LANES)),
        ],
        input_output_aliases={1: 4, 2: 5},
        compiler_params=params,
        name="gather",
    )(
        slot_tile_number, mid_hi, mid_lo, edge, edge_codes, got_x_a, got_x_d,
        table, right_hi, right_lo, deform,
    )
    return out[:4]


def solution(mesh):
    both = ("gx", "gy")
    field = P(None, both, None)
    flat = P(both, None)
    return jax.shard_map(
        per_device,
        mesh=mesh,
        in_specs=(
            field, flat, field, field, field, flat, flat, P(both), P("gx", "gy"),
            P("gx", "gy", None),
        ),
        out_specs=(field,) * 4,
        check_vma=False,
    )
```

```python
import functools

import jax
import jax.numpy as jnp
from jax import lax
from jax.experimental import pallas as pl
from jax.experimental.pallas import tpu as pltpu
from jax.sharding import PartitionSpec as P


DT = 0.1
MU = 2.0
LAM = 3.0
GRAVITY = -2.0
FLOOR = 0.25

F32 = jnp.float32
BF16 = jnp.bfloat16
VMEM_LIMIT = 24 * 1024 * 1024

SIDE = 10
DEPTH = 256
SLOTS = 24
LANES = 128
FACE_ROWS = 176
CHUNK = 8

POS_Y, POS_Z, FIELD0, FIELD1, POS_X, LIVE, WX = 0, 1, 2, 3, 4, 5, 6
GATHER_ROWS = WX + 6
MASS = GATHER_ROWS
VEL = MASS + 1
AFF = VEL + 3
SCATTER_ROWS = AFF + 9


def spline(distance):
    size = jnp.abs(distance)
    outer = jnp.maximum(1.5 - size, 0.0)
    inner = jnp.maximum(0.5 - size, 0.0)
    return 0.5 * outer * outer - 1.5 * inner * inner


def determinant(m):
    return (
        m[0] * (m[4] * m[8] - m[5] * m[7])
        - m[1] * (m[3] * m[8] - m[5] * m[6])
        + m[2] * (m[3] * m[7] - m[4] * m[6])
    )


def kirchhoff(m):
    ratio = determinant(m)
    pressure = 0.5 * LAM * (ratio * ratio - 1.0)
    entries = []
    for i in range(3):
        for j in range(3):
            e = m[3 * i] * m[3 * j] + m[3 * i + 1] * m[3 * j + 1] + m[3 * i + 2] * m[3 * j + 2]
            entries.append(MU * (e - 1.0) + pressure if i == j else MU * e)
    return entries


def split(x):
    high = x.astype(BF16)
    return high, (x - high.astype(F32)).astype(BF16)


def matmul_t(a, b):
    return lax.dot_general(a, b, (((1,), (1,)), ((), ())), preferred_element_type=F32)


def matmul(a, b):
    return lax.dot_general(a, b, (((1,), (0,)), ((), ())), preferred_element_type=F32)


def iota(shape, axis):
    return lax.broadcasted_iota(jnp.int32, shape, axis)


def y_coords(tile_y):
    s = iota((8, LANES), 0)
    wrapped = jnp.where(s < 4, s + 4, s - 4)
    return jnp.where(tile_y == 0, s, wrapped).astype(F32)


def low_side(axis):
    return lax.axis_index(axis) % 2


def half(h):
    return slice(h * LANES, (h + 1) * LANES)


def matching_slots(order, tile_ref, tile_y):
    def body(s, n):
        order[n] = s
        return n + ((lax.shift_right_logical(tile_ref[0, s], 5) & 1) == tile_y).astype(jnp.int32)

    n = lax.fori_loop(0, SLOTS, body, 0)
    order[n] = SLOTS
    return n


def clear(left_hi, left_lo, acc):
    acc[...] = jnp.zeros_like(acc)
    zeros = jnp.zeros((48, LANES), BF16)
    for u in range(2):
        left_hi[u, 0:48, LANES : 2 * LANES] = zeros
        left_lo[u, 0:48, LANES : 2 * LANES] = zeros


def scatter_half(tile_y, tile_ref, table, rows, codes, halves, face, order, left_hi, left_lo,
                 acc, turned):
    count = matching_slots(order, tile_ref, tile_y)

    def one(index, u):
        s = order[index]
        tile = tile_ref[0, jnp.minimum(s, SLOTS - 1)]
        tile_x = lax.shift_right_logical(tile, 6)
        tile_z = tile & 31

        def row(k):
            return table[k, pl.ds(s, 1), :] if k < MASS else rows[k - MASS, pl.ds(s, 1), :]

        dy = y_coords(tile_y) - row(POS_Y)
        wy = spline(dy)
        pos_x = row(POS_X)
        wxy = [wy * row(WX + x) for x in range(6)]

        def put(channel, column, values):
            for pair in range(3):
                hi, lo = split(jnp.concatenate(values[2 * pair : 2 * pair + 2], 0))
                at = channel * 48 + pair * 16
                left_hi[u, at : at + 16, column * LANES : (column + 1) * LANES] = hi
                left_lo[u, at : at + 16, column * LANES : (column + 1) * LANES] = lo

        m = row(MASS)
        put(0, 0, [w * m for w in wxy])
        for k in range(3):
            base = row(VEL + k) + row(AFF + 3 * k + 1) * dy
            ax = row(AFF + 3 * k)
            az = row(AFF + 3 * k + 2)
            put(1 + k, 0, [wxy[x] * (base + ax * (float(x) - pos_x)) for x in range(6)])
            put(1 + k, 1, [wxy[x] * az for x in range(6)])

        dz = iota((16, LANES), 0).astype(F32) - row(POS_Z)
        wz = spline(dz)
        mz = wz * dz
        parts = []
        for f in range(2):
            mask = row(FIELD0 + f)
            parts.append([split(wz * mask), split(mz * mask)])
        right_hi = jnp.concatenate(
            [jnp.concatenate([parts[f][0][0], parts[f][1][0]], 1) for f in range(2)], 0
        )
        right_lo = jnp.concatenate(
            [jnp.concatenate([parts[f][0][1], parts[f][1][1]], 1) for f in range(2)], 0
        )
        both = matmul_t(jnp.concatenate([right_hi, right_lo], 0), left_hi[u])
        rest = matmul_t(right_hi, left_lo[u])
        total = both[0:32] + both[32:64] + rest
        window = pl.ds(tile_z * 8 + 7, 16)
        for f in range(2):
            acc[tile_x, f, 0, window, :] += total[16 * f : 16 * f + 16, 0:LANES]
            acc[tile_x, f, 1, window, 0:64] += total[16 * f : 16 * f + 16, LANES:192]

    def step(pair, carry):
        one(pair * 2, 0)
        one(pair * 2 + 1, 1)
        return carry

    lax.fori_loop(0, lax.shift_right_logical(count + 1, 1), step, 0)

    for tx in range(2):
        for f in range(2):
            for h in range(2):
                z = slice(8 + LANES * h, 8 + LANES * (h + 1))
                turned[tx, f, 0:128, half(h)] = acc[tx, f, 0, z, :].T
                turned[tx, f, 128:192, half(h)] = acc[tx, f, 1, z, :].T[0:64]

    for f in range(2):
        for c in range(4):
            for x in range(SIDE):
                parts = [
                    turned[tx, f, (c * 6 + x - 4 * tx) * 8 : (c * 6 + x - 4 * tx) * 8 + 8, :]
                    for tx in range(2)
                    if 0 <= x - 4 * tx < 6
                ]
                total = sum(parts[1:], parts[0])
                channel = 4 * f + c
                halves[tile_y, channel, x, :, :] = total
                at = channel * 20 + x * 2
                face[at : at + 2, :] = total[0:2]
    for x in range(8):
        face[160 + x : 161 + x, :] = codes[x + 1, pl.ds(1 + tile_y * 7, 1), :]
    face[168:176, :] = jnp.zeros((8, DEPTH), F32)


def first_kernel(
    count_ref, tile_in, offset_in, mass_in, velocity_in, affine_in, deform_in, cell_in, body_in,
    code_in,
    halves, face, table, rows, codes, tile_ref,
    offset, mass, velocity, affine, deform, cell, body, code,
    order, left_hi, left_lo, acc, turned, sems,
):
    pairs = (
        (tile_in, tile_ref.at[0]), (deform_in, deform), (affine_in, affine),
        (offset_in, offset), (velocity_in, velocity), (mass_in, mass), (cell_in, cell),
        (body_in, body), (code_in, code),
    )
    copies = [
        pltpu.make_async_copy(src, dst, sems.at[i]) for i, (src, dst) in enumerate(pairs)
    ]
    for copy in copies:
        copy.start()
    clear(left_hi, left_lo, acc)
    codes[...] = jnp.zeros_like(codes)
    for out in (table, rows):
        for k in range(out.shape[0]):
            out[k, SLOTS:32, :] = jnp.zeros((32 - SLOTS, LANES), F32)
    for copy in copies:
        copy.wait()

    for x in range(8):
        codes[x + 1, 1:9, :] = code[x].astype(F32)
    live = (iota((SLOTS, LANES), 0) < count_ref[0, 0]).astype(F32)
    cell = cell[...]
    field_one = (body[...] & 1).astype(F32)
    pos_x = lax.shift_right_logical(cell, 5).astype(F32) + offset[0]
    own = slice(0, SLOTS)
    table[LIVE, own] = live
    table[POS_X, own] = pos_x
    table[POS_Y, own] = (lax.shift_right_logical(cell, 3) & 3).astype(F32) + offset[1]
    table[POS_Z, own] = (cell & 7).astype(F32) + offset[2]
    table[FIELD0, own] = 1.0 - field_one
    table[FIELD1, own] = field_one
    for x in range(6):
        table[WX + x, own] = spline(float(x) - pos_x)
    weighted = mass[...] * live
    rows[0, own] = weighted
    for k in range(3):
        rows[VEL - MASS + k, own] = weighted * velocity[k]
    stress = kirchhoff([deform[k] for k in range(9)])
    for k in range(9):
        rows[AFF - MASS + k, own] = weighted * (affine[k] - 4.0 * DT * stress[k])
    scatter_half(
        low_side("gy"), tile_ref, table, rows, codes, halves, face, order, left_hi, left_lo,
        acc, turned,
    )


def second_kernel(
    tile_ref, half_in, table, rows, codes, halves, face, order, left_hi, left_lo, acc, turned,
):
    clear(left_hi, left_lo, acc)
    scatter_half(
        1 - low_side("gy"), tile_ref, table, rows, codes, halves, face, order, left_hi, left_lo,
        acc, turned,
    )


def join(halves, channel, x):
    low, high = halves[0, channel, x], halves[1, channel, x]
    return low + jnp.where(iota((8, DEPTH), 0) >= 4, high, 0.0), high


def prepare_kernel(order, tile_ref, table, right):
    none = jnp.zeros((16, 2 * LANES), BF16)

    def one(s, carry):
        dz = iota((16, LANES), 0).astype(F32) - table[POS_Z, pl.ds(s, 1), :]
        wz = spline(dz)
        mz = wz * dz
        for f in range(2):
            mask = table[FIELD0 + f, pl.ds(s, 1), :]
            hi, lo = split(jnp.concatenate([wz * mask, mz * mask], 1))
            for k, rows in enumerate((hi, lo, hi, none)):
                right[s, 64 * f + 16 * k : 64 * f + 16 * k + 16, :] = rows
        return carry

    lax.fori_loop(0, SLOTS, one, 0, unroll=2)


def corner_kernel(order, halves, recv_a, recv_d, codes, face_a, face_d, edge, edge_codes):
    side_y = low_side("gy")
    side_x = low_side("gx")
    for plane in range(4):
        x = plane if plane < 2 else plane + 6
        for channel in range(8):
            edge[channel, plane, 0:8, :], edge[channel, plane, 8:16, :] = join(halves, channel, x)
    for recv, start in ((recv_a, (1 - side_y) * 8), (recv_d, side_y * 8)):
        start = pl.multiple_of(start, 8)
        for channel in range(8):
            for plane in range(4):
                x = plane if plane < 2 else plane + 6
                at = channel * 20 + x * 2
                edge[channel, plane, pl.ds(start, 2), :] += recv[at : at + 2, :]
    edge_codes[0] = codes[1]
    edge_codes[1] = codes[8]
    for recv, halo in ((recv_a, (1 - side_y) * 9), (recv_d, side_y * 9)):
        edge_codes[0, pl.ds(halo, 1), :] = recv[160:161, :]
        edge_codes[1, pl.ds(halo, 1), :] = recv[167:168, :]
    for face, high in ((face_a, 1 - side_x), (face_d, side_x)):
        first = high * 2
        for channel in range(8):
            for p in range(2):
                at = channel * 2 + p
                face[at * 8 : at * 8 + 8, :] = edge[channel, first + p, 0:8, :]
                face[128 + at * 2 : 130 + at * 2, :] = edge[channel, first + p, 8:10, :]
        face[160:170, :] = edge_codes[high, 0:10, :]
        face[170:176, :] = jnp.zeros((6, DEPTH), F32)


def node_speeds(sums, code, inside):
    m0, m1 = sums[0], sums[4]
    r0 = 1.0 / jnp.maximum(m0, FLOOR)
    r1 = 1.0 / jnp.maximum(m1, FLOOR)
    rc = 1.0 / jnp.maximum(m0 + m1, FLOOR)
    share = jnp.minimum(1.0, jnp.minimum(m0, m1) * (1.0 / FLOOR))
    shifted = code + jnp.where(code >= 13.0, 1.0, 0.0)
    third = jnp.where(shifted >= 9.0, 1.0, 0.0) + jnp.where(shifted >= 18.0, 1.0, 0.0)
    rest = shifted - 9.0 * third
    second = jnp.where(rest >= 3.0, 1.0, 0.0) + jnp.where(rest >= 6.0, 1.0, 0.0)
    direction = [third - 1.0, second - 1.0, rest - 3.0 * second - 1.0]
    square = (
        direction[0] * direction[0] + direction[1] * direction[1] + direction[2] * direction[2]
    )
    inverse = jnp.where(square > 2.5, 1.0 / 3.0, jnp.where(square > 1.5, 0.5, 1.0))
    u0 = [sums[1 + k] * r0 for k in range(3)]
    u1 = [sums[5 + k] * r1 for k in range(3)]
    uc = [(sums[1 + k] + sums[5 + k]) * rc for k in range(3)]
    approach0 = sum((u0[k] - uc[k]) * direction[k] for k in range(3))
    approach1 = sum((uc[k] - u1[k]) * direction[k] for k in range(3))
    scale = share * inverse
    push0 = scale * jnp.maximum(approach0, 0.0)
    push1 = scale * jnp.maximum(approach1, 0.0)
    gravity = [0.0, 0.0, DT * GRAVITY]
    v0 = [(u0[k] - push0 * direction[k] + gravity[k]) * inside for k in range(3)]
    v1 = [(u1[k] + push1 * direction[k] + gravity[k]) * inside for k in range(3)]
    return v0, v1


def store_nodes(x_first, sums_at, code_at, last, nodes):
    index_x = lax.axis_index("gx")
    index_y = lax.axis_index("gy")
    s8 = iota((8, LANES), 0)
    lane = iota((8, LANES), 1)
    inside_low = jnp.where((s8 == 0) & (index_y == 0), 0.0, 1.0)
    inside_high = jnp.where((s8 == 1) & (index_y == last[1]), 0.0, 1.0)
    local = lane & 63

    def tiles(v0, v1):
        def both(h, shift):
            return jnp.where(
                lane < 64, pltpu.roll(v0[h], shift, 1), pltpu.roll(v1[h], (shift + 64) % 128, 1)
            )

        return (
            jnp.where(local < 1, 0.0, both(0, 1)),
            both(0, 73),
            jnp.where(local < 17, both(0, 17), both(1, 17)),
            both(1, 89),
            jnp.where(local < 33, both(1, 33), 0.0),
        )

    for k in range(2):
        x = x_first + k
        edge = ((x == 0) & (index_x == 0)) | ((x == SIDE - 1) & (index_x == last[0]))
        inside_x = jnp.where(edge, 0.0, 1.0)
        found = []
        for r in range(2):
            inside = (inside_low if r == 0 else inside_high) * inside_x
            found.append(
                [
                    node_speeds([sums_at(c, k, r, h) for c in range(8)], code_at(k, r, h), inside)
                    for h in range(2)
                ]
            )
        at = pl.multiple_of(x * 8, 8)
        for c in range(3):
            low, high = (
                tiles(*([found[r][h][f][c] for h in range(2)] for f in range(2)))
                for r in range(2)
            )
            for j in range(5):
                nodes[0, j, c, pl.ds(at, 8), :] = low[j]
                nodes[1, j, c, pl.ds(at, 8), :] = jnp.where(s8 < 2, high[j], low[j])


def middle_kernel(last, order, halves, y_a, y_d, codes, nodes, work, own):
    side_y = low_side("gy")
    for x in range(2, 8):
        own[x - 2] = codes[x]
        for channel in range(8):
            low, high = join(halves, channel, x)
            work[channel, x - 2, 0:8, :] = low
            work[channel, x - 2, 8:16, :] = high
    for recv, high in ((y_a, 1 - side_y), (y_d, side_y)):
        start = pl.multiple_of(high * 8, 8)
        for x in range(2, 8):
            for channel in range(8):
                at = channel * 20 + x * 2
                work[channel, x - 2, pl.ds(start, 2), :] += recv[at : at + 2, :]
            own[x - 2, pl.ds(high * 9, 1), :] = recv[159 + x : 160 + x, :]

    def step(pair, carry):
        x = pair * 2

        def sums_at(c, k, r, h):
            return work[c, x - 2 + k, 8 * r : 8 * r + 8, half(h)]

        def code_at(k, r, h):
            return own[x - 2 + k, 8 * r : 8 * r + 8, half(h)]

        store_nodes(x, sums_at, code_at, last, nodes)
        return carry

    lax.fori_loop(1, 4, step, 0)


def gather_kernel(
    last, tile_ref, middle, edge, edge_codes, x_a, x_d, table, right, deform,
    velocity_out, affine_out, deform_out, stress_out, nodes,
    work, own, partial, new_velocity, new_affine, new_deform, new_stress, sems,
):
    side_x = low_side("gx")
    for recv, high in ((x_a, 1 - side_x), (x_d, side_x)):
        first = high * 2
        for channel in range(8):
            for p in range(2):
                at = channel * 2 + p
                plane = first + p
                work[channel, plane, 0:8, :] = (
                    edge[channel, plane, 0:8, :] + recv[at * 8 : at * 8 + 8, :]
                )
                work[channel, plane, 8:16, :] = edge[channel, plane, 8:16, :]
                work[channel, plane, 8:10, :] += recv[128 + at * 2 : 130 + at * 2, :]
        own[first + high, 0:10, :] = recv[160:170, :]
        own[first + 1 - high] = edge_codes[high]

    def edge_step(high, carry):
        def sums_at(c, k, r, h):
            return work[c, high * 2 + k, 8 * r : 8 * r + 8, half(h)]

        def code_at(k, r, h):
            return own[high * 2 + k, 8 * r : 8 * r + 8, half(h)]

        store_nodes(high * 8, sums_at, code_at, last, nodes)
        return carry

    lax.fori_loop(0, 2, edge_step, 0)

    def one(chunk, slot):
        s = chunk * CHUNK + slot
        tile = tile_ref[0, s]
        tile_x = lax.shift_right_logical(tile, 6)
        tile_y = lax.shift_right_logical(tile, 5) & 1
        tile_z = tile & 31
        j = lax.div(tile_z, 7)
        shift = (tile_z - 7 * j) * 8

        def row(k):
            return table[k, pl.ds(s, 1), :]

        first = pl.multiple_of(tile_x * 32, 32)
        lane = iota((48, LANES), 1) & 63
        left = []
        for c in range(3):
            value = nodes[tile_y, j, c, pl.ds(first, 48), :]
            window = pltpu.roll(value, lax.rem(128 - shift, 128), 1)
            window = jnp.where(lane < 16, window, pltpu.roll(value, lax.rem(144 - shift, 128), 1))
            window = jnp.where(lane < 32, window, pltpu.roll(value, 160 - shift - 128 * (shift <= 32).astype(jnp.int32), 1))
            high = window.astype(BF16).astype(F32)
            left.append(jnp.where(lane < 32, high, window - high).astype(BF16))
        summed = matmul(jnp.concatenate(left, 0), right[s])

        dy = y_coords(tile_y) - row(POS_Y)
        wy = spline(dy)
        pos_x = row(POS_X)
        wxy = [wy * row(WX + x) for x in range(6)]
        place = slice(slot * 8, slot * 8 + 8)
        for c in range(3):
            speed = along_x = along_z = None
            for x in range(5, -1, -1):
                at = (c * 6 + x) * 8
                part = wxy[x] * summed[at : at + 8, 0:LANES]
                moment = wxy[x] * summed[at : at + 8, LANES : 2 * LANES]
                speed = part if speed is None else speed + part
                along_z = moment if along_z is None else along_z + moment
                if x:
                    along_x = speed if along_x is None else along_x + speed
            partial[4 * c, place, :] = speed
            partial[4 * c + 1, place, :] = along_x - pos_x * speed
            partial[4 * c + 2, place, :] = speed * dy
            partial[4 * c + 3, place, :] = along_z

    def collect(k):
        total = partial[k, pl.ds(0, CHUNK, stride=8), :]
        for y in range(1, 8):
            total = total + partial[k, pl.ds(y, CHUNK, stride=8), :]
        return total

    ready = (new_velocity, new_affine, new_deform, new_stress)
    finals = (velocity_out, affine_out, deform_out, stress_out)

    def sends(chunk):
        own_slots = pl.ds(pl.multiple_of(chunk * CHUNK, CHUNK), CHUNK)
        return [
            pltpu.make_async_copy(src.at[:, own_slots], dst.at[:, own_slots], sems.at[chunk, i])
            for i, (src, dst) in enumerate(zip(ready, finals))
        ]

    def step(chunk, carry):
        for slot in range(CHUNK):
            one(chunk, slot)
        own_slots = pl.ds(pl.multiple_of(chunk * CHUNK, CHUNK), CHUNK)
        live = table[LIVE, own_slots, :]
        moved = []
        for c in range(3):
            new_velocity[c, own_slots, :] = collect(4 * c) * live
            for k in range(3):
                value = 4.0 * collect(4 * c + 1 + k) * live
                new_affine[3 * c + k, own_slots, :] = value
                moved.append(value)
        old = [deform[k, own_slots, :] for k in range(9)]
        fresh = []
        for i in range(3):
            for j in range(3):
                value = old[3 * i + j]
                for k in range(3):
                    value = value + DT * moved[3 * i + k] * old[3 * k + j]
                fresh.append(value * live)
        for k in range(9):
            new_deform[k, own_slots, :] = fresh[k]
        stress = kirchhoff(fresh)
        for k, entry in enumerate((0, 4, 8, 1, 2, 5)):
            new_stress[k, own_slots, :] = stress[entry] * live
        for send in sends(chunk):
            send.start()
        return carry

    lax.fori_loop(0, SLOTS // CHUNK, step, 0)
    for chunk in range(SLOTS // CHUNK):
        for send in sends(chunk):
            send.wait()


def vmem(shape, dtype=F32):
    return pltpu.VMEM(shape, dtype)


def cost(flops):
    return pl.CostEstimate(flops=flops, bytes_accessed=4000000, transcendentals=0)


def swap_pairs(block, axis, shift):
    size = lax.axis_size(axis)
    route = [(i, ((i + shift) ^ 1) - shift) for i in range(size)]
    return lax.ppermute(block, axis, [(i, k) for i, k in route if 0 <= k < size])


def per_device(
    offset, particle_mass, velocity, affine, deform,
    particle_cell, body_id, slot_tile_number, block_count, normal_code,
):
    params = pltpu.CompilerParams(vmem_limit_bytes=VMEM_LIMIT)
    smem = pl.BlockSpec(memory_space=pltpu.SMEM)
    hbm = pl.BlockSpec(memory_space=pltpu.HBM)
    whole = pl.BlockSpec(memory_space=pltpu.VMEM)
    face = jax.ShapeDtypeStruct((FACE_ROWS, DEPTH), F32)
    nodes = jax.ShapeDtypeStruct((2, 5, 3, 8 * SIDE, LANES), F32)
    right_shape = jax.ShapeDtypeStruct((SLOTS, LANES, 256), BF16)
    last = (lax.axis_size("gx") - 1, lax.axis_size("gy") - 1)
    inputs = (
        slot_tile_number, offset, particle_mass, velocity, affine, deform, particle_cell,
        body_id, normal_code,
    )

    halves_shape = jax.ShapeDtypeStruct((2, 8, SIDE, 8, DEPTH), F32)
    scatter_scratch = [
        pltpu.SMEM((32,), jnp.int32),
        vmem((2, 192, 256), BF16),
        vmem((2, 192, 256), BF16),
        vmem((2, 2, 2, 280, LANES)),
        vmem((2, 2, 192, DEPTH)),
    ]
    anywhere = pl.BlockSpec(memory_space=pl.ANY)

    halves, y_d, table, rows, codes, tile_numbers = pl.pallas_call(
        first_kernel,
        out_shape=(
            halves_shape,
            face,
            jax.ShapeDtypeStruct((GATHER_ROWS, 32, LANES), F32),
            jax.ShapeDtypeStruct((SCATTER_ROWS - GATHER_ROWS, 32, LANES), F32),
            jax.ShapeDtypeStruct((SIDE, 16, DEPTH), F32),
            jax.ShapeDtypeStruct((1, SLOTS), jnp.int32),
        ),
        in_specs=[smem] + [hbm] * 9,
        out_specs=(whole,) * 5 + (smem,),
        scratch_shapes=[vmem(x.shape, x.dtype) for x in inputs[1:]]
        + scatter_scratch
        + [pltpu.SemaphoreType.DMA((9,))],
        compiler_params=params,
        cost_estimate=cost(3000000),
        name="scatter_first",
    )(
        block_count,
        *(pltpu.with_memory_space_constraint(x, pltpu.HBM) for x in inputs),
    )
    got_y_d = swap_pairs(y_d, "gy", 1)
    halves, y_a = pl.pallas_call(
        second_kernel,
        out_shape=(halves_shape, face),
        in_specs=[smem] + [whole] * 4,
        out_specs=(whole,) * 2,
        scratch_shapes=scatter_scratch,
        input_output_aliases={1: 0},
        compiler_params=params,
        cost_estimate=cost(3000000),
        name="scatter_second",
    )(tile_numbers, halves, table, rows, codes)
    got_y_a = swap_pairs(y_a, "gy", 0)
    right = pl.pallas_call(
        prepare_kernel,
        out_shape=right_shape,
        in_specs=[anywhere, smem, whole],
        out_specs=whole,
        compiler_params=params,
        cost_estimate=cost(3000000),
        name="prepare",
    )(y_a, tile_numbers, table)
    x_a, x_d, edge, edge_codes = pl.pallas_call(
        corner_kernel,
        out_shape=(
            face,
            face,
            jax.ShapeDtypeStruct((8, 4, 16, DEPTH), F32),
            jax.ShapeDtypeStruct((2, 16, DEPTH), F32),
        ),
        in_specs=[pl.BlockSpec(memory_space=pl.ANY)] + [whole] * 4,
        out_specs=(whole,) * 4,
        compiler_params=params,
        name="corners",
    )(right, halves, got_y_a, got_y_d, codes)
    got_x_d = swap_pairs(x_d, "gx", 1)
    got_x_a = swap_pairs(x_a, "gx", 0)
    middle = pl.pallas_call(
        functools.partial(middle_kernel, last),
        out_shape=nodes,
        in_specs=[pl.BlockSpec(memory_space=pl.ANY)] + [whole] * 4,
        out_specs=whole,
        scratch_shapes=[vmem((8, 6, 16, DEPTH)), vmem((6, 16, DEPTH))],
        compiler_params=params,
        cost_estimate=cost(3000000),
        name="middle",
    )(edge_codes, halves, got_y_a, got_y_d, codes)

    slots, particles = particle_mass.shape
    out = pl.pallas_call(
        functools.partial(gather_kernel, last),
        out_shape=tuple(jax.ShapeDtypeStruct((k, slots, particles), F32) for k in (3, 9, 9, 6))
        + (nodes,),
        in_specs=[smem] + [whole] * 8,
        out_specs=(hbm,) * 4 + (whole,),
        scratch_shapes=[
            vmem((8, 4, 16, DEPTH)),
            vmem((4, 16, DEPTH)),
            vmem((12, 8 * CHUNK, LANES)),
        ]
        + [vmem((k, slots, particles)) for k in (3, 9, 9, 6)]
        + [pltpu.SemaphoreType.DMA((SLOTS // CHUNK, 4))],
        input_output_aliases={1: 4},
        compiler_params=params,
        name="gather",
    )(
        tile_numbers, middle, edge, edge_codes, got_x_a, got_x_d, table, right, deform,
    )
    return out[:4]


def solution(mesh):
    both = ("gx", "gy")
    field = P(None, both, None)
    flat = P(both, None)
    return jax.shard_map(
        per_device,
        mesh=mesh,
        in_specs=(
            field, flat, field, field, field, flat, flat, P(both), P("gx", "gy"),
            P("gx", "gy", None),
        ),
        out_specs=(field,) * 4,
        check_vma=False,
    )
```

```python
import functools

import jax
import jax.numpy as jnp
from jax import lax
from jax.experimental import pallas as pl
from jax.experimental.pallas import tpu as pltpu
from jax.sharding import PartitionSpec as P


DT = 0.1
MU = 2.0
LAM = 3.0
GRAVITY = -2.0
FLOOR = 0.25

F32 = jnp.float32
BF16 = jnp.bfloat16
VMEM_LIMIT = 24 * 1024 * 1024

SIDE = 10
DEPTH = 256
SLOTS = 24
LANES = 128
FACE_ROWS = 184
CHANNELS = 9
CHUNK = 8

POS_Y, POS_Z, FIELD0, FIELD1, POS_X, LIVE, WX = 0, 1, 2, 3, 4, 5, 6
GATHER_ROWS = WX + 6
MASS = GATHER_ROWS
VEL = MASS + 1
AFF = VEL + 3
SCATTER_ROWS = AFF + 9


def spline(distance):
    size = jnp.abs(distance)
    outer = jnp.maximum(1.5 - size, 0.0)
    inner = jnp.maximum(0.5 - size, 0.0)
    return 0.5 * outer * outer - 1.5 * inner * inner


def determinant(m):
    return (
        m[0] * (m[4] * m[8] - m[5] * m[7])
        - m[1] * (m[3] * m[8] - m[5] * m[6])
        + m[2] * (m[3] * m[7] - m[4] * m[6])
    )


def kirchhoff(m):
    ratio = determinant(m)
    pressure = 0.5 * LAM * (ratio * ratio - 1.0)
    entries = []
    for i in range(3):
        for j in range(3):
            e = m[3 * i] * m[3 * j] + m[3 * i + 1] * m[3 * j + 1] + m[3 * i + 2] * m[3 * j + 2]
            entries.append(MU * (e - 1.0) + pressure if i == j else MU * e)
    return entries


def split(x):
    high = x.astype(BF16)
    return high, (x - high.astype(F32)).astype(BF16)


def matmul_t(a, b):
    return lax.dot_general(a, b, (((1,), (1,)), ((), ())), preferred_element_type=F32)


def matmul(a, b):
    return lax.dot_general(a, b, (((1,), (0,)), ((), ())), preferred_element_type=F32)


def iota(shape, axis):
    return lax.broadcasted_iota(jnp.int32, shape, axis)


def y_coords(tile_y):
    s = iota((8, LANES), 0)
    wrapped = jnp.where(s < 4, s + 4, s - 4)
    return jnp.where(tile_y == 0, s, wrapped).astype(F32)


def low_side(axis):
    return lax.axis_index(axis) % 2


def half(h):
    return slice(h * LANES, (h + 1) * LANES)


def matching_slots(order, tile_ref, tile_x):
    def body(s, n):
        order[n] = s
        return n + (lax.shift_right_logical(tile_ref[0, s], 6) == tile_x).astype(jnp.int32)

    n = lax.fori_loop(0, SLOTS, body, 0)
    order[n] = SLOTS
    return n


def clear(left_hi, left_lo, acc):
    acc[...] = jnp.zeros_like(acc)
    zeros = jnp.zeros((48, LANES), BF16)
    for u in range(2):
        left_hi[u, 0:48, LANES : 2 * LANES] = zeros
        left_lo[u, 0:48, LANES : 2 * LANES] = zeros


def scatter_half(tile_x, tile_ref, table, rows, halves, face, order, left_hi, left_lo,
                 acc, turned):
    count = matching_slots(order, tile_ref, tile_x)

    def one(index, u):
        s = order[index]
        tile = tile_ref[0, jnp.minimum(s, SLOTS - 1)]
        tile_y = lax.shift_right_logical(tile, 5) & 1
        tile_z = tile & 31

        def row(k):
            return table[k, pl.ds(s, 1), :] if k < MASS else rows[k - MASS, pl.ds(s, 1), :]

        dy = y_coords(tile_y) - row(POS_Y)
        wy = spline(dy)
        pos_x = row(POS_X)
        wxy = [wy * row(WX + x) for x in range(6)]

        def put(channel, column, values):
            for pair in range(3):
                hi, lo = split(jnp.concatenate(values[2 * pair : 2 * pair + 2], 0))
                at = channel * 48 + pair * 16
                left_hi[u, at : at + 16, column * LANES : (column + 1) * LANES] = hi
                left_lo[u, at : at + 16, column * LANES : (column + 1) * LANES] = lo

        m = row(MASS)
        put(0, 0, [w * m for w in wxy])
        for k in range(3):
            base = row(VEL + k) + row(AFF + 3 * k + 1) * dy
            ax = row(AFF + 3 * k)
            az = row(AFF + 3 * k + 2)
            put(1 + k, 0, [wxy[x] * (base + ax * (float(x) - pos_x)) for x in range(6)])
            put(1 + k, 1, [wxy[x] * az for x in range(6)])

        dz = iota((16, LANES), 0).astype(F32) - row(POS_Z)
        wz = spline(dz)
        mz = wz * dz
        parts = []
        for f in range(2):
            mask = row(FIELD0 + f)
            parts.append([split(wz * mask), split(mz * mask)])
        right_hi = jnp.concatenate(
            [jnp.concatenate([parts[f][0][0], parts[f][1][0]], 1) for f in range(2)], 0
        )
        right_lo = jnp.concatenate(
            [jnp.concatenate([parts[f][0][1], parts[f][1][1]], 1) for f in range(2)], 0
        )
        both = matmul_t(jnp.concatenate([right_hi, right_lo], 0), left_hi[u])
        rest = matmul_t(right_hi, left_lo[u])
        total = both[0:32] + both[32:64] + rest
        window = pl.ds(tile_z * 8 + 7, 16)
        for f in range(2):
            acc[tile_y, f, 0, window, :] += total[16 * f : 16 * f + 16, 0:LANES]
            acc[tile_y, f, 1, window, 0:64] += total[16 * f : 16 * f + 16, LANES:192]

    def step(pair, carry):
        one(pair * 2, 0)
        one(pair * 2 + 1, 1)
        return carry

    lax.fori_loop(0, lax.shift_right_logical(count + 1, 1), step, 0)

    for ty in range(2):
        for f in range(2):
            for h in range(2):
                z = slice(8 + LANES * h, 8 + LANES * (h + 1))
                turned[ty, f, 0:128, half(h)] = acc[ty, f, 0, z, :].T
                turned[ty, f, 128:192, half(h)] = acc[ty, f, 1, z, :].T[0:64]

    upper = iota((8, DEPTH), 0) >= 4
    for f in range(2):
        for c in range(4):
            for x in range(6):
                at = (c * 6 + x) * 8
                high = turned[1, f, at : at + 8, :]
                halves[tile_x, 4 * f + c, x, 0:8, :] = turned[
                    0, f, at : at + 8, :
                ] + jnp.where(upper, high, 0.0)
                halves[tile_x, 4 * f + c, x, 8:16, :] = high
    for c in range(CHANNELS):
        for p in range(2):
            at = c * 2 + p
            face[at * 8 : at * 8 + 8, :] = halves[tile_x, c, 4 * tile_x + p, 0:8, :]
            face[144 + at * 2 : 146 + at * 2, :] = halves[tile_x, c, 4 * tile_x + p, 8:10, :]
    face[180:184, :] = jnp.zeros((4, DEPTH), F32)


def first_kernel(
    count_ref, tile_in, offset_in, mass_in, velocity_in, affine_in, deform_in, cell_in, body_in,
    code_in,
    halves, face, table, rows, tile_ref,
    offset, mass, velocity, affine, deform, cell, body, code,
    order, left_hi, left_lo, acc, turned, sems,
):
    pairs = (
        (tile_in, tile_ref.at[0]), (deform_in, deform), (affine_in, affine),
        (offset_in, offset), (velocity_in, velocity), (mass_in, mass), (cell_in, cell),
        (body_in, body), (code_in, code),
    )
    copies = [
        pltpu.make_async_copy(src, dst, sems.at[i]) for i, (src, dst) in enumerate(pairs)
    ]
    for copy in copies:
        copy.start()
    clear(left_hi, left_lo, acc)
    halves[:, 8] = jnp.zeros((2, 6, 16, DEPTH), F32)
    for out in (table, rows):
        for k in range(out.shape[0]):
            out[k, SLOTS:32, :] = jnp.zeros((32 - SLOTS, LANES), F32)
    for copy in copies:
        copy.wait()

    for x in range(1, 9):
        half_x = 0 if x < 6 else 1
        halves[half_x, 8, x - 4 * half_x, 1:9, :] = code[x - 1].astype(F32)
    live = (iota((SLOTS, LANES), 0) < count_ref[0, 0]).astype(F32)
    cell = cell[...]
    field_one = (body[...] & 1).astype(F32)
    pos_x = lax.shift_right_logical(cell, 5).astype(F32) + offset[0]
    own = slice(0, SLOTS)
    table[LIVE, own] = live
    table[POS_X, own] = pos_x
    table[POS_Y, own] = (lax.shift_right_logical(cell, 3) & 3).astype(F32) + offset[1]
    table[POS_Z, own] = (cell & 7).astype(F32) + offset[2]
    table[FIELD0, own] = 1.0 - field_one
    table[FIELD1, own] = field_one
    for x in range(6):
        table[WX + x, own] = spline(float(x) - pos_x)
    weighted = mass[...] * live
    rows[0, own] = weighted
    for k in range(3):
        rows[VEL - MASS + k, own] = weighted * velocity[k]
    stress = kirchhoff([deform[k] for k in range(9)])
    for k in range(9):
        rows[AFF - MASS + k, own] = weighted * (affine[k] - 4.0 * DT * stress[k])
    scatter_half(
        low_side("gx"), tile_ref, table, rows, halves, face, order, left_hi, left_lo, acc, turned,
    )


def second_kernel(
    tile_ref, half_in, table, rows, halves, face, order, left_hi, left_lo, acc, turned,
):
    clear(left_hi, left_lo, acc)
    scatter_half(
        1 - low_side("gx"), tile_ref, table, rows, halves, face, order, left_hi, left_lo,
        acc, turned,
    )


def prepare_kernel(order, tile_ref, table, right):
    none = jnp.zeros((16, 2 * LANES), BF16)

    def one(s, carry):
        dz = iota((16, LANES), 0).astype(F32) - table[POS_Z, pl.ds(s, 1), :]
        wz = spline(dz)
        mz = wz * dz
        for f in range(2):
            mask = table[FIELD0 + f, pl.ds(s, 1), :]
            hi, lo = split(jnp.concatenate([wz * mask, mz * mask], 1))
            for k, rows in enumerate((hi, lo, hi, none)):
                right[s, 64 * f + 16 * k : 64 * f + 16 * k + 16, :] = rows
        return carry

    lax.fori_loop(0, SLOTS, one, 0, unroll=2)


def plane(halves, edge, c, x, rows):
    if x < 2:
        return edge[c, x, rows, :]
    if x >= 8:
        return edge[c, x - 6, rows, :]
    if x < 4:
        return halves[0, c, x, rows, :]
    if x >= 6:
        return halves[1, c, x - 4, rows, :]
    return halves[0, c, x, rows, :] + halves[1, c, x - 4, rows, :]


def y_face_row(c, x):
    return c * 16 + x * 2 if x < 8 else 144 + c * 4 + (x - 8) * 2


def corner_kernel(order, halves, recv_a, recv_d, face_a, face_d, edge):
    side_y = low_side("gy")
    side_x = low_side("gx")
    for recv, high in ((recv_a, 1 - side_x), (recv_d, side_x)):
        for c in range(CHANNELS):
            for p in range(2):
                at = c * 2 + p
                own = (high, c, 4 * high + p)
                to = (c, 2 * high + p)
                edge[(*to, slice(0, 8))] = halves[(*own, slice(0, 8))] + recv[at * 8 : at * 8 + 8]
                edge[(*to, slice(8, 16))] = halves[(*own, slice(8, 16))]
                edge[(*to, slice(8, 10))] += recv[144 + at * 2 : 146 + at * 2]
    for face, high in ((face_a, 1 - side_y), (face_d, side_y)):
        rows = pl.ds(pl.multiple_of(high * 8, 8), 2)
        for c in range(CHANNELS):
            for x in range(SIDE):
                at = y_face_row(c, x)
                face[at : at + 2, :] = plane(halves, edge, c, x, rows)
        face[180:184, :] = jnp.zeros((4, DEPTH), F32)


def node_speeds(sums, code, inside):
    m0, m1 = sums[0], sums[4]
    r0 = 1.0 / jnp.maximum(m0, FLOOR)
    r1 = 1.0 / jnp.maximum(m1, FLOOR)
    rc = 1.0 / jnp.maximum(m0 + m1, FLOOR)
    share = jnp.minimum(1.0, jnp.minimum(m0, m1) * (1.0 / FLOOR))
    shifted = code + jnp.where(code >= 13.0, 1.0, 0.0)
    third = jnp.where(shifted >= 9.0, 1.0, 0.0) + jnp.where(shifted >= 18.0, 1.0, 0.0)
    rest = shifted - 9.0 * third
    second = jnp.where(rest >= 3.0, 1.0, 0.0) + jnp.where(rest >= 6.0, 1.0, 0.0)
    direction = [third - 1.0, second - 1.0, rest - 3.0 * second - 1.0]
    square = (
        direction[0] * direction[0] + direction[1] * direction[1] + direction[2] * direction[2]
    )
    inverse = jnp.where(square > 2.5, 1.0 / 3.0, jnp.where(square > 1.5, 0.5, 1.0))
    u0 = [sums[1 + k] * r0 for k in range(3)]
    u1 = [sums[5 + k] * r1 for k in range(3)]
    uc = [(sums[1 + k] + sums[5 + k]) * rc for k in range(3)]
    approach0 = sum((u0[k] - uc[k]) * direction[k] for k in range(3))
    approach1 = sum((uc[k] - u1[k]) * direction[k] for k in range(3))
    scale = share * inverse
    push0 = scale * jnp.maximum(approach0, 0.0)
    push1 = scale * jnp.maximum(approach1, 0.0)
    gravity = [0.0, 0.0, DT * GRAVITY]
    v0 = [(u0[k] - push0 * direction[k] + gravity[k]) * inside for k in range(3)]
    v1 = [(u1[k] + push1 * direction[k] + gravity[k]) * inside for k in range(3)]
    return v0, v1


def tiles(v0, v1):
    lane = iota(v0[0].shape, 1)
    local = lane & 63

    def both(h, shift):
        return jnp.where(
            lane < 64, pltpu.roll(v0[h], shift, 1), pltpu.roll(v1[h], (shift + 64) % 128, 1)
        )

    return (
        jnp.where(local < 1, 0.0, both(0, 1)),
        both(0, 73),
        jnp.where(local < 17, both(0, 17), both(1, 17)),
        both(1, 89),
        jnp.where(local < 33, both(1, 33), 0.0),
    )


def inside_x(x, last):
    index = lax.axis_index("gx")
    return jnp.where(((x == 0) & (index == 0)) | ((x == SIDE - 1) & (index == last[0])), 0.0, 1.0)


def middle_kernel(last, order, halves, edge, nodes, work):
    for c in range(CHANNELS):
        for x in range(SIDE):
            work[c, x] = plane(halves, edge, c, x, slice(0, 8))

    def step(x, carry):
        inside = inside_x(x, last)
        found = [
            node_speeds([work[c, x, :, half(h)] for c in range(8)], work[8, x, :, half(h)], inside)
            for h in range(2)
        ]
        at = pl.multiple_of(x * 8, 8)
        for c in range(3):
            ready = tiles(*([found[h][f][c] for h in range(2)] for f in range(2)))
            for j in range(5):
                for ty in range(2):
                    nodes[ty, j, c, pl.ds(at, 8), :] = ready[j]
        return carry

    lax.fori_loop(0, SIDE, step, 0, unroll=2)


def gather_kernel(
    last, tile_ref, middle, own_a, own_d, y_a, y_d, table, right, deform,
    velocity_out, affine_out, deform_out, stress_out, nodes,
    partial, new_velocity, new_affine, new_deform, new_stress, sems,
):
    side_y = low_side("gy")
    index_y = lax.axis_index("gy")
    for own, recv, high in ((own_a, y_a, 1 - side_y), (own_d, y_d, side_y)):
        edge_y = jnp.where(high == 0, (index_y == 0), (index_y == last[1]))
        for first, count in ((0, 8), (8, 2)):
            row = iota((2 * count, LANES), 0)
            inside = inside_x(lax.shift_right_logical(row, 1) + first, last)
            inside = jnp.where(((row & 1) == high) & edge_y, 0.0, inside)
            found = []
            for h in range(2):
                sums = []
                for c in range(CHANNELS):
                    at = y_face_row(c, first)
                    rows = slice(at, at + 2 * count)
                    sums.append(own[rows, half(h)] + recv[rows, half(h)])
                found.append(node_speeds(sums[:8], sums[8], inside))
            for c in range(3):
                ready = tiles(*([found[h][f][c] for h in range(2)] for f in range(2)))
                for j in range(5):
                    for x in range(count):
                        at = (first + x) * 8
                        nodes[high, j, c, at : at + 2, :] = ready[j][2 * x : 2 * x + 2]

    def one(chunk, slot):
        s = chunk * CHUNK + slot
        tile = tile_ref[0, s]
        tile_x = lax.shift_right_logical(tile, 6)
        tile_y = lax.shift_right_logical(tile, 5) & 1
        tile_z = tile & 31
        j = lax.div(tile_z, 7)
        shift = (tile_z - 7 * j) * 8

        def row(k):
            return table[k, pl.ds(s, 1), :]

        first = pl.multiple_of(tile_x * 32, 32)
        lane = iota((48, LANES), 1) & 63
        left = []
        for c in range(3):
            value = nodes[tile_y, j, c, pl.ds(first, 48), :]
            window = pltpu.roll(value, lax.rem(128 - shift, 128), 1)
            window = jnp.where(lane < 16, window, pltpu.roll(value, lax.rem(144 - shift, 128), 1))
            window = jnp.where(lane < 32, window, pltpu.roll(value, 160 - shift - 128 * (shift <= 32).astype(jnp.int32), 1))
            high = window.astype(BF16).astype(F32)
            left.append(jnp.where(lane < 32, high, window - high).astype(BF16))
        summed = matmul(jnp.concatenate(left, 0), right[s])

        dy = y_coords(tile_y) - row(POS_Y)
        wy = spline(dy)
        pos_x = row(POS_X)
        wxy = [wy * row(WX + x) for x in range(6)]
        place = slice(slot * 8, slot * 8 + 8)
        for c in range(3):
            speed = along_x = along_z = None
            for x in range(5, -1, -1):
                at = (c * 6 + x) * 8
                part = wxy[x] * summed[at : at + 8, 0:LANES]
                moment = wxy[x] * summed[at : at + 8, LANES : 2 * LANES]
                speed = part if speed is None else speed + part
                along_z = moment if along_z is None else along_z + moment
                if x:
                    along_x = speed if along_x is None else along_x + speed
            partial[4 * c, place, :] = speed
            partial[4 * c + 1, place, :] = along_x - pos_x * speed
            partial[4 * c + 2, place, :] = speed * dy
            partial[4 * c + 3, place, :] = along_z

    def collect(k):
        total = partial[k, pl.ds(0, CHUNK, stride=8), :]
        for y in range(1, 8):
            total = total + partial[k, pl.ds(y, CHUNK, stride=8), :]
        return total

    ready = (new_velocity, new_affine, new_deform, new_stress)
    finals = (velocity_out, affine_out, deform_out, stress_out)

    def sends(chunk):
        own_slots = pl.ds(pl.multiple_of(chunk * CHUNK, CHUNK), CHUNK)
        return [
            pltpu.make_async_copy(src.at[:, own_slots], dst.at[:, own_slots], sems.at[chunk, i])
            for i, (src, dst) in enumerate(zip(ready, finals))
        ]

    def step(chunk, carry):
        for slot in range(CHUNK):
            one(chunk, slot)
        own_slots = pl.ds(pl.multiple_of(chunk * CHUNK, CHUNK), CHUNK)
        live = table[LIVE, own_slots, :]
        moved = []
        for c in range(3):
            new_velocity[c, own_slots, :] = collect(4 * c) * live
            for k in range(3):
                value = 4.0 * collect(4 * c + 1 + k) * live
                new_affine[3 * c + k, own_slots, :] = value
                moved.append(value)
        old = [deform[k, own_slots, :] for k in range(9)]
        fresh = []
        for i in range(3):
            for j in range(3):
                value = old[3 * i + j]
                for k in range(3):
                    value = value + DT * moved[3 * i + k] * old[3 * k + j]
                fresh.append(value * live)
        for k in range(9):
            new_deform[k, own_slots, :] = fresh[k]
        stress = kirchhoff(fresh)
        for k, entry in enumerate((0, 4, 8, 1, 2, 5)):
            new_stress[k, own_slots, :] = stress[entry] * live
        for send in sends(chunk):
            send.start()
        return carry

    lax.fori_loop(0, SLOTS // CHUNK, step, 0)
    for chunk in range(SLOTS // CHUNK):
        for send in sends(chunk):
            send.wait()


def vmem(shape, dtype=F32):
    return pltpu.VMEM(shape, dtype)


def cost(flops):
    return pl.CostEstimate(flops=flops, bytes_accessed=4000000, transcendentals=0)


def swap_pairs(block, axis, shift):
    size = lax.axis_size(axis)
    route = [(i, ((i + shift) ^ 1) - shift) for i in range(size)]
    return lax.ppermute(block, axis, [(i, k) for i, k in route if 0 <= k < size])


def per_device(
    offset, particle_mass, velocity, affine, deform,
    particle_cell, body_id, slot_tile_number, block_count, normal_code,
):
    params = pltpu.CompilerParams(vmem_limit_bytes=VMEM_LIMIT)
    smem = pl.BlockSpec(memory_space=pltpu.SMEM)
    hbm = pl.BlockSpec(memory_space=pltpu.HBM)
    whole = pl.BlockSpec(memory_space=pltpu.VMEM)
    face = jax.ShapeDtypeStruct((FACE_ROWS, DEPTH), F32)
    nodes = jax.ShapeDtypeStruct((2, 5, 3, 8 * SIDE, LANES), F32)
    right_shape = jax.ShapeDtypeStruct((SLOTS, LANES, 256), BF16)
    last = (lax.axis_size("gx") - 1, lax.axis_size("gy") - 1)
    inputs = (
        slot_tile_number, offset, particle_mass, velocity, affine, deform, particle_cell,
        body_id, normal_code,
    )

    halves_shape = jax.ShapeDtypeStruct((2, CHANNELS, 6, 16, DEPTH), F32)
    scatter_scratch = [
        pltpu.SMEM((32,), jnp.int32),
        vmem((2, 192, 256), BF16),
        vmem((2, 192, 256), BF16),
        vmem((2, 2, 2, 280, LANES)),
        vmem((2, 2, 192, DEPTH)),
    ]
    anywhere = pl.BlockSpec(memory_space=pl.ANY)

    halves, x_d, table, rows, tile_numbers = pl.pallas_call(
        first_kernel,
        out_shape=(
            halves_shape,
            face,
            jax.ShapeDtypeStruct((GATHER_ROWS, 32, LANES), F32),
            jax.ShapeDtypeStruct((SCATTER_ROWS - GATHER_ROWS, 32, LANES), F32),
            jax.ShapeDtypeStruct((1, SLOTS), jnp.int32),
        ),
        in_specs=[smem] + [hbm] * 9,
        out_specs=(whole,) * 4 + (smem,),
        scratch_shapes=[vmem(x.shape, x.dtype) for x in inputs[1:]]
        + scatter_scratch
        + [pltpu.SemaphoreType.DMA((9,))],
        compiler_params=params,
        cost_estimate=cost(3000000),
        name="scatter_first",
    )(
        block_count,
        *(pltpu.with_memory_space_constraint(x, pltpu.HBM) for x in inputs),
    )
    got_x_d = swap_pairs(x_d, "gx", 1)
    halves, x_a = pl.pallas_call(
        second_kernel,
        out_shape=(halves_shape, face),
        in_specs=[smem] + [whole] * 3,
        out_specs=(whole,) * 2,
        scratch_shapes=scatter_scratch,
        input_output_aliases={1: 0},
        compiler_params=params,
        cost_estimate=cost(3000000),
        name="scatter_second",
    )(tile_numbers, halves, table, rows)
    got_x_a = swap_pairs(x_a, "gx", 0)
    right = pl.pallas_call(
        prepare_kernel,
        out_shape=right_shape,
        in_specs=[anywhere, smem, whole],
        out_specs=whole,
        compiler_params=params,
        cost_estimate=cost(3000000),
        name="prepare",
    )(x_a, tile_numbers, table)
    y_a, y_d, edge = pl.pallas_call(
        corner_kernel,
        out_shape=(face, face, jax.ShapeDtypeStruct((CHANNELS, 4, 16, DEPTH), F32)),
        in_specs=[anywhere] + [whole] * 3,
        out_specs=(whole,) * 3,
        compiler_params=params,
        name="corners",
    )(right, halves, got_x_a, got_x_d)
    got_y_d = swap_pairs(y_d, "gy", 1)
    got_y_a = swap_pairs(y_a, "gy", 0)
    middle = pl.pallas_call(
        functools.partial(middle_kernel, last),
        out_shape=nodes,
        in_specs=[anywhere] + [whole] * 2,
        out_specs=whole,
        scratch_shapes=[vmem((CHANNELS, SIDE, 8, DEPTH))],
        compiler_params=params,
        cost_estimate=cost(3000000),
        name="middle",
    )(y_a, halves, edge)

    slots, particles = particle_mass.shape
    out = pl.pallas_call(
        functools.partial(gather_kernel, last),
        out_shape=tuple(jax.ShapeDtypeStruct((k, slots, particles), F32) for k in (3, 9, 9, 6))
        + (nodes,),
        in_specs=[smem] + [whole] * 8,
        out_specs=(hbm,) * 4 + (whole,),
        scratch_shapes=[vmem((12, 8 * CHUNK, LANES))]
        + [vmem((k, slots, particles)) for k in (3, 9, 9, 6)]
        + [pltpu.SemaphoreType.DMA((SLOTS // CHUNK, 4))],
        input_output_aliases={1: 4},
        compiler_params=params,
        name="gather",
    )(
        tile_numbers, middle, y_a, y_d, got_y_a, got_y_d, table, right, deform,
    )
    return out[:4]


def solution(mesh):
    both = ("gx", "gy")
    field = P(None, both, None)
    flat = P(both, None)
    return jax.shard_map(
        per_device,
        mesh=mesh,
        in_specs=(
            field, flat, field, field, field, flat, flat, P(both), P("gx", "gy"),
            P("gx", "gy", None),
        ),
        out_specs=(field,) * 4,
        check_vma=False,
    )
```

```python
import functools

import jax
import jax.numpy as jnp
from jax import lax
from jax.experimental import pallas as pl
from jax.experimental.pallas import tpu as pltpu
from jax.sharding import PartitionSpec as P


DT = 0.1
MU = 2.0
LAM = 3.0
GRAVITY = -2.0
FLOOR = 0.25

F32 = jnp.float32
BF16 = jnp.bfloat16
VMEM_LIMIT = 24 * 1024 * 1024

SIDE = 10
DEPTH = 256
SLOTS = 24
LANES = 128
FACE_ROWS = 184
CHANNELS = 9
CHUNK = 8
UNROLL = 4

POS_Y, POS_Z, FIELD0, FIELD1, POS_X, LIVE, WX = 0, 1, 2, 3, 4, 5, 6
GATHER_ROWS = WX + 6
MASS = GATHER_ROWS
VEL = MASS + 1
AFF = VEL + 3
SCATTER_ROWS = AFF + 9


def spline(distance):
    size = jnp.abs(distance)
    outer = jnp.maximum(1.5 - size, 0.0)
    inner = jnp.maximum(0.5 - size, 0.0)
    return 0.5 * outer * outer - 1.5 * inner * inner


def determinant(m):
    return (
        m[0] * (m[4] * m[8] - m[5] * m[7])
        - m[1] * (m[3] * m[8] - m[5] * m[6])
        + m[2] * (m[3] * m[7] - m[4] * m[6])
    )


def kirchhoff(m):
    ratio = determinant(m)
    pressure = 0.5 * LAM * (ratio * ratio - 1.0)
    entries = []
    for i in range(3):
        for j in range(3):
            e = m[3 * i] * m[3 * j] + m[3 * i + 1] * m[3 * j + 1] + m[3 * i + 2] * m[3 * j + 2]
            entries.append(MU * (e - 1.0) + pressure if i == j else MU * e)
    return entries


def split(x):
    high = x.astype(BF16)
    return high, (x - high.astype(F32)).astype(BF16)


def matmul_t(a, b):
    return lax.dot_general(a, b, (((1,), (1,)), ((), ())), preferred_element_type=F32)


def matmul(a, b):
    return lax.dot_general(a, b, (((1,), (0,)), ((), ())), preferred_element_type=F32)


def iota(shape, axis):
    return lax.broadcasted_iota(jnp.int32, shape, axis)


def y_coords(tile_y):
    s = iota((8, LANES), 0)
    wrapped = jnp.where(s < 4, s + 4, s - 4)
    return jnp.where(tile_y == 0, s, wrapped).astype(F32)


def low_side(axis):
    return lax.axis_index(axis) % 2


def half(h):
    return slice(h * LANES, (h + 1) * LANES)


def matching_slots(order, tile_ref, tile_x):
    def body(s, n):
        order[n] = s
        return n + (lax.shift_right_logical(tile_ref[0, s], 6) == tile_x).astype(jnp.int32)

    n = lax.fori_loop(0, SLOTS, body, 0)
    for k in range(UNROLL - 1):
        order[n + k] = SLOTS
    return n


def clear(left_hi, left_lo, acc):
    acc[...] = jnp.zeros_like(acc)
    zeros = jnp.zeros((48, LANES), BF16)
    for u in range(UNROLL):
        left_hi[u, 0:48, LANES : 2 * LANES] = zeros
        left_lo[u, 0:48, LANES : 2 * LANES] = zeros


def scatter_half(tile_x, tile_ref, table, rows, halves, face, order, left_hi, left_lo,
                 acc, turned):
    count = matching_slots(order, tile_ref, tile_x)

    def one(index, u):
        s = order[index]
        tile = tile_ref[0, jnp.minimum(s, SLOTS - 1)]
        tile_y = lax.shift_right_logical(tile, 5) & 1
        tile_z = tile & 31

        def row(k):
            return table[k, pl.ds(s, 1), :] if k < MASS else rows[k - MASS, pl.ds(s, 1), :]

        dy = y_coords(tile_y) - row(POS_Y)
        wy = spline(dy)
        pos_x = row(POS_X)
        wxy = [wy * row(WX + x) for x in range(6)]

        def put(channel, column, values):
            for pair in range(3):
                hi, lo = split(jnp.concatenate(values[2 * pair : 2 * pair + 2], 0))
                at = channel * 48 + pair * 16
                left_hi[u, at : at + 16, column * LANES : (column + 1) * LANES] = hi
                left_lo[u, at : at + 16, column * LANES : (column + 1) * LANES] = lo

        m = row(MASS)
        put(0, 0, [w * m for w in wxy])
        for k in range(3):
            base = row(VEL + k) + row(AFF + 3 * k + 1) * dy
            ax = row(AFF + 3 * k)
            az = row(AFF + 3 * k + 2)
            put(1 + k, 0, [wxy[x] * (base + ax * (float(x) - pos_x)) for x in range(6)])
            put(1 + k, 1, [wxy[x] * az for x in range(6)])

        dz = iota((16, LANES), 0).astype(F32) - row(POS_Z)
        wz = spline(dz)
        mz = wz * dz
        parts = []
        for f in range(2):
            mask = row(FIELD0 + f)
            parts.append([split(wz * mask), split(mz * mask)])
        right_hi = jnp.concatenate(
            [jnp.concatenate([parts[f][0][0], parts[f][1][0]], 1) for f in range(2)], 0
        )
        right_lo = jnp.concatenate(
            [jnp.concatenate([parts[f][0][1], parts[f][1][1]], 1) for f in range(2)], 0
        )
        both = matmul_t(jnp.concatenate([right_hi, right_lo], 0), left_hi[u])
        rest = matmul_t(right_hi, left_lo[u])
        total = both[0:32] + both[32:64] + rest
        window = pl.ds(tile_z * 8 + 7, 16)
        for f in range(2):
            acc[tile_y, f, 0, window, :] += total[16 * f : 16 * f + 16, 0:LANES]
            acc[tile_y, f, 1, window, 0:64] += total[16 * f : 16 * f + 16, LANES:192]

    def step(group, carry):
        for u in range(UNROLL):
            one(group * UNROLL + u, u)
        return carry

    lax.fori_loop(0, lax.div(count + UNROLL - 1, UNROLL), step, 0)

    for ty in range(2):
        for f in range(2):
            for h in range(2):
                z = slice(8 + LANES * h, 8 + LANES * (h + 1))
                turned[ty, f, 0:128, half(h)] = acc[ty, f, 0, z, :].T
                turned[ty, f, 128:192, half(h)] = acc[ty, f, 1, z, :].T[0:64]

    upper = iota((8, DEPTH), 0) >= 4
    for f in range(2):
        for c in range(4):
            for x in range(6):
                at = (c * 6 + x) * 8
                high = turned[1, f, at : at + 8, :]
                halves[tile_x, 4 * f + c, x, 0:8, :] = turned[
                    0, f, at : at + 8, :
                ] + jnp.where(upper, high, 0.0)
                halves[tile_x, 4 * f + c, x, 8:16, :] = high
    for c in range(CHANNELS):
        for p in range(2):
            at = c * 2 + p
            face[at * 8 : at * 8 + 8, :] = halves[tile_x, c, 4 * tile_x + p, 0:8, :]
            face[144 + at * 2 : 146 + at * 2, :] = halves[tile_x, c, 4 * tile_x + p, 8:10, :]
    face[180:184, :] = jnp.zeros((4, DEPTH), F32)


def first_kernel(
    count_ref, tile_in, offset_in, mass_in, velocity_in, affine_in, deform_in, cell_in, body_in,
    code_in,
    halves, face, table, rows, tile_ref,
    offset, mass, velocity, affine, deform, cell, body, code,
    order, left_hi, left_lo, acc, turned, sems,
):
    pairs = (
        (tile_in, tile_ref.at[0]), (deform_in, deform), (affine_in, affine),
        (offset_in, offset), (velocity_in, velocity), (mass_in, mass), (cell_in, cell),
        (body_in, body), (code_in, code),
    )
    copies = [
        pltpu.make_async_copy(src, dst, sems.at[i]) for i, (src, dst) in enumerate(pairs)
    ]
    for copy in copies:
        copy.start()
    clear(left_hi, left_lo, acc)
    halves[:, 8] = jnp.zeros((2, 6, 16, DEPTH), F32)
    for out in (table, rows):
        for k in range(out.shape[0]):
            out[k, SLOTS:32, :] = jnp.zeros((32 - SLOTS, LANES), F32)
    for copy in copies:
        copy.wait()

    for x in range(1, 9):
        half_x = 0 if x < 6 else 1
        halves[half_x, 8, x - 4 * half_x, 1:9, :] = code[x - 1].astype(F32)
    live = (iota((SLOTS, LANES), 0) < count_ref[0, 0]).astype(F32)
    cell = cell[...]
    field_one = (body[...] & 1).astype(F32)
    pos_x = lax.shift_right_logical(cell, 5).astype(F32) + offset[0]
    own = slice(0, SLOTS)
    table[LIVE, own] = live
    table[POS_X, own] = pos_x
    table[POS_Y, own] = (lax.shift_right_logical(cell, 3) & 3).astype(F32) + offset[1]
    table[POS_Z, own] = (cell & 7).astype(F32) + offset[2]
    table[FIELD0, own] = 1.0 - field_one
    table[FIELD1, own] = field_one
    for x in range(6):
        table[WX + x, own] = spline(float(x) - pos_x)
    weighted = mass[...] * live
    rows[0, own] = weighted
    for k in range(3):
        rows[VEL - MASS + k, own] = weighted * velocity[k]
    stress = kirchhoff([deform[k] for k in range(9)])
    for k in range(9):
        rows[AFF - MASS + k, own] = weighted * (affine[k] - 4.0 * DT * stress[k])
    scatter_half(
        low_side("gx"), tile_ref, table, rows, halves, face, order, left_hi, left_lo, acc, turned,
    )


def second_kernel(
    tile_ref, half_in, table, rows, halves, face, order, left_hi, left_lo, acc, turned,
):
    clear(left_hi, left_lo, acc)
    scatter_half(
        1 - low_side("gx"), tile_ref, table, rows, halves, face, order, left_hi, left_lo,
        acc, turned,
    )


def prepare_kernel(order, tile_ref, table, right):
    none = jnp.zeros((16, 2 * LANES), BF16)

    def one(s, carry):
        dz = iota((16, LANES), 0).astype(F32) - table[POS_Z, pl.ds(s, 1), :]
        wz = spline(dz)
        mz = wz * dz
        for f in range(2):
            mask = table[FIELD0 + f, pl.ds(s, 1), :]
            hi, lo = split(jnp.concatenate([wz * mask, mz * mask], 1))
            for k, rows in enumerate((hi, lo, hi, none)):
                right[s, 64 * f + 16 * k : 64 * f + 16 * k + 16, :] = rows
        return carry

    lax.fori_loop(0, SLOTS, one, 0, unroll=2)


def plane(halves, edge, c, x, rows):
    if x < 2:
        return edge[c, x, rows, :]
    if x >= 8:
        return edge[c, x - 6, rows, :]
    if x < 4:
        return halves[0, c, x, rows, :]
    if x >= 6:
        return halves[1, c, x - 4, rows, :]
    return halves[0, c, x, rows, :] + halves[1, c, x - 4, rows, :]


def y_face_row(c, x):
    return c * 16 + x * 2 if x < 8 else 144 + c * 4 + (x - 8) * 2


def corner_kernel(order, halves, recv_a, recv_d, face_a, face_d, edge):
    side_y = low_side("gy")
    side_x = low_side("gx")
    for recv, high in ((recv_a, 1 - side_x), (recv_d, side_x)):
        for c in range(CHANNELS):
            for p in range(2):
                at = c * 2 + p
                own = (high, c, 4 * high + p)
                to = (c, 2 * high + p)
                edge[(*to, slice(0, 8))] = halves[(*own, slice(0, 8))] + recv[at * 8 : at * 8 + 8]
                edge[(*to, slice(8, 16))] = halves[(*own, slice(8, 16))]
                edge[(*to, slice(8, 10))] += recv[144 + at * 2 : 146 + at * 2]
    for face, high in ((face_a, 1 - side_y), (face_d, side_y)):
        rows = pl.ds(pl.multiple_of(high * 8, 8), 2)
        for c in range(CHANNELS):
            for x in range(SIDE):
                at = y_face_row(c, x)
                face[at : at + 2, :] = plane(halves, edge, c, x, rows)
        face[180:184, :] = jnp.zeros((4, DEPTH), F32)


def node_speeds(sums, code, inside):
    m0, m1 = sums[0], sums[4]
    r0 = 1.0 / jnp.maximum(m0, FLOOR)
    r1 = 1.0 / jnp.maximum(m1, FLOOR)
    rc = 1.0 / jnp.maximum(m0 + m1, FLOOR)
    share = jnp.minimum(1.0, jnp.minimum(m0, m1) * (1.0 / FLOOR))
    shifted = code + jnp.where(code >= 13.0, 1.0, 0.0)
    third = jnp.where(shifted >= 9.0, 1.0, 0.0) + jnp.where(shifted >= 18.0, 1.0, 0.0)
    rest = shifted - 9.0 * third
    second = jnp.where(rest >= 3.0, 1.0, 0.0) + jnp.where(rest >= 6.0, 1.0, 0.0)
    direction = [third - 1.0, second - 1.0, rest - 3.0 * second - 1.0]
    square = (
        direction[0] * direction[0] + direction[1] * direction[1] + direction[2] * direction[2]
    )
    inverse = jnp.where(square > 2.5, 1.0 / 3.0, jnp.where(square > 1.5, 0.5, 1.0))
    u0 = [sums[1 + k] * r0 for k in range(3)]
    u1 = [sums[5 + k] * r1 for k in range(3)]
    uc = [(sums[1 + k] + sums[5 + k]) * rc for k in range(3)]
    approach0 = sum((u0[k] - uc[k]) * direction[k] for k in range(3))
    approach1 = sum((uc[k] - u1[k]) * direction[k] for k in range(3))
    scale = share * inverse
    push0 = scale * jnp.maximum(approach0, 0.0)
    push1 = scale * jnp.maximum(approach1, 0.0)
    gravity = [0.0, 0.0, DT * GRAVITY]
    v0 = [(u0[k] - push0 * direction[k] + gravity[k]) * inside for k in range(3)]
    v1 = [(u1[k] + push1 * direction[k] + gravity[k]) * inside for k in range(3)]
    return v0, v1


def tiles(v0, v1):
    lane = iota(v0[0].shape, 1)
    local = lane & 63

    def both(h, shift):
        return jnp.where(
            lane < 64, pltpu.roll(v0[h], shift, 1), pltpu.roll(v1[h], (shift + 64) % 128, 1)
        )

    return (
        jnp.where(local < 1, 0.0, both(0, 1)),
        both(0, 73),
        jnp.where(local < 17, both(0, 17), both(1, 17)),
        both(1, 89),
        jnp.where(local < 33, both(1, 33), 0.0),
    )


def inside_x(x, last):
    index = lax.axis_index("gx")
    return jnp.where(((x == 0) & (index == 0)) | ((x == SIDE - 1) & (index == last[0])), 0.0, 1.0)


def tile_of(tile_ref, s):
    tile = tile_ref[0, s]
    tile_z = tile & 31
    j = lax.div(tile_z, 7)
    return (
        lax.shift_right_logical(tile, 6),
        lax.shift_right_logical(tile, 5) & 1,
        j,
        (tile_z - 7 * j) * 8,
    )


def z_window(value, shift):
    lane = iota(value.shape, 1) & 63
    window = pltpu.roll(value, lax.rem(128 - shift, 128), 1)
    window = jnp.where(lane < 16, window, pltpu.roll(value, lax.rem(144 - shift, 128), 1))
    window = jnp.where(lane < 32, window, pltpu.roll(value, lax.rem(160 - shift, 128), 1))
    high = window.astype(BF16).astype(F32)
    return jnp.where(lane < 32, high, window - high).astype(BF16)


def collect(partial, k):
    total = partial[k, pl.ds(0, CHUNK, stride=8), :]
    for y in range(1, 8):
        total = total + partial[k, pl.ds(y, CHUNK, stride=8), :]
    return total


def chunk_of(chunk):
    return pl.ds(pl.multiple_of(chunk * CHUNK, CHUNK), CHUNK)


def middle_kernel(
    last, order, tile_ref, halves, edge, table, right, gathered, work, nodes, partial,
):
    for c in range(CHANNELS):
        for x in range(SIDE):
            work[c, x] = plane(halves, edge, c, x, slice(0, 8))
    inner = iota((8, LANES), 0) >= 2

    def node_step(x, carry):
        inside = inside_x(x, last)
        found = [
            node_speeds([work[c, x, :, half(h)] for c in range(8)], work[8, x, :, half(h)], inside)
            for h in range(2)
        ]
        at = pl.multiple_of(x * 8, 8)
        for c in range(3):
            ready = tiles(*([found[h][f][c] for h in range(2)] for f in range(2)))
            for j in range(5):
                nodes[j, c, pl.ds(at, 8), :] = jnp.where(inner, ready[j], 0.0)
        return carry

    lax.fori_loop(0, SIDE, node_step, 0, unroll=2)

    def one(chunk, slot):
        s = chunk * CHUNK + slot
        tile_x, tile_y, j, shift = tile_of(tile_ref, s)

        def row(k):
            return table[k, pl.ds(s, 1), :]

        first = pl.multiple_of(tile_x * 32, 32)
        left = [z_window(nodes[j, c, pl.ds(first, 48), :], shift) for c in range(3)]
        summed = matmul(jnp.concatenate(left, 0), right[s])
        dy = y_coords(tile_y) - row(POS_Y)
        wy = spline(dy)
        pos_x = row(POS_X)
        wxy = [wy * row(WX + x) for x in range(6)]
        place = slice(slot * 8, slot * 8 + 8)
        for c in range(3):
            speed = along_x = along_z = None
            for x in range(5, -1, -1):
                at = (c * 6 + x) * 8
                part = wxy[x] * summed[at : at + 8, 0:LANES]
                moment = wxy[x] * summed[at : at + 8, LANES : 2 * LANES]
                speed = part if speed is None else speed + part
                along_z = moment if along_z is None else along_z + moment
                if x:
                    along_x = speed if along_x is None else along_x + speed
            partial[4 * c, place, :] = speed
            partial[4 * c + 1, place, :] = along_x - pos_x * speed
            partial[4 * c + 2, place, :] = speed * dy
            partial[4 * c + 3, place, :] = along_z

    def step(chunk, carry):
        for slot in range(CHUNK):
            one(chunk, slot)
        for k in range(12):
            gathered[k, chunk_of(chunk), :] = collect(partial, k)
        return carry

    lax.fori_loop(0, SLOTS // CHUNK, step, 0)


def gather_kernel(
    last, tile_ref, gathered, own_a, own_d, y_a, y_d, table, right, deform,
    velocity_out, affine_out, deform_out, stress_out,
    nodes, partial, new_velocity, new_affine, new_deform, new_stress, sems,
):
    side_y = low_side("gy")
    index_y = lax.axis_index("gy")
    for own, recv, high in ((own_a, y_a, 1 - side_y), (own_d, y_d, side_y)):
        edge_y = jnp.where(high == 0, (index_y == 0), (index_y == last[1]))
        for first, count in ((0, 8), (8, 2)):
            row = iota((2 * count, LANES), 0)
            inside = inside_x(lax.shift_right_logical(row, 1) + first, last)
            inside = jnp.where(((row & 1) == high) & edge_y, 0.0, inside)
            found = []
            for h in range(2):
                sums = []
                for c in range(CHANNELS):
                    at = y_face_row(c, first)
                    rows = slice(at, at + 2 * count)
                    sums.append(own[rows, half(h)] + recv[rows, half(h)])
                found.append(node_speeds(sums[:8], sums[8], inside))
            for c in range(3):
                ready = tiles(*([found[h][f][c] for h in range(2)] for f in range(2)))
                for j in range(5):
                    nodes[high, j, c, 2 * first : 2 * (first + count), :] = ready[j]
        for c in range(3):
            for j in range(5):
                nodes[high, j, c, 2 * SIDE : 24, :] = jnp.zeros((24 - 2 * SIDE, LANES), F32)

    def one(chunk, slot):
        s = chunk * CHUNK + slot
        tile_x, tile_y, j, shift = tile_of(tile_ref, s)

        def row(k):
            return table[k, pl.ds(s, 1), :]

        first = pl.multiple_of(tile_x * 8, 8)
        left = [nodes[tile_y, j, c, pl.ds(first, 16), :] for c in range(3)]
        summed = matmul(z_window(jnp.concatenate(left, 0), shift), right[s])
        sublane = iota((8, LANES), 0)
        dy = ((sublane & 1) + 4 * tile_y).astype(F32) - row(POS_Y)
        wy = spline(dy)
        speed, along_x, along_z = [None] * 3, [None] * 3, [None] * 3
        for q in range(2):
            dx = (lax.shift_right_logical(sublane, 1) + 4 * q).astype(F32) - row(POS_X)
            weight = wy * spline(dx)
            for c in range(3):
                at = c * 16 + q * 8
                part = weight * summed[at : at + 8, 0:LANES]
                moment = weight * summed[at : at + 8, LANES : 2 * LANES]
                speed[c] = part if q == 0 else speed[c] + part
                along_x[c] = part * dx if q == 0 else along_x[c] + part * dx
                along_z[c] = moment if q == 0 else along_z[c] + moment
        place = slice(slot * 8, slot * 8 + 8)
        for c in range(3):
            partial[4 * c, place, :] = speed[c]
            partial[4 * c + 1, place, :] = along_x[c]
            partial[4 * c + 2, place, :] = speed[c] * dy
            partial[4 * c + 3, place, :] = along_z[c]

    ready = (new_velocity, new_affine, new_deform, new_stress)
    finals = (velocity_out, affine_out, deform_out, stress_out)

    def sends(chunk):
        slots = chunk_of(chunk)
        return [
            pltpu.make_async_copy(src.at[:, slots], dst.at[:, slots], sems.at[chunk, i])
            for i, (src, dst) in enumerate(zip(ready, finals))
        ]

    def step(chunk, carry):
        for slot in range(CHUNK):
            one(chunk, slot)
        slots = chunk_of(chunk)
        live = table[LIVE, slots, :]
        total = [(gathered[k, slots, :] + collect(partial, k)) * live for k in range(12)]
        moved = []
        for c in range(3):
            new_velocity[c, slots, :] = total[4 * c]
            for k in range(3):
                value = 4.0 * total[4 * c + 1 + k]
                new_affine[3 * c + k, slots, :] = value
                moved.append(value)
        old = [deform[k, slots, :] for k in range(9)]
        fresh = []
        for i in range(3):
            for j in range(3):
                value = old[3 * i + j]
                for k in range(3):
                    value = value + DT * moved[3 * i + k] * old[3 * k + j]
                fresh.append(value * live)
        for k in range(9):
            new_deform[k, slots, :] = fresh[k]
        stress = kirchhoff(fresh)
        for k, entry in enumerate((0, 4, 8, 1, 2, 5)):
            new_stress[k, slots, :] = stress[entry] * live
        for send in sends(chunk):
            send.start()
        return carry

    lax.fori_loop(0, SLOTS // CHUNK, step, 0)
    for chunk in range(SLOTS // CHUNK):
        for send in sends(chunk):
            send.wait()


def vmem(shape, dtype=F32):
    return pltpu.VMEM(shape, dtype)


def cost(flops):
    return pl.CostEstimate(flops=flops, bytes_accessed=4000000, transcendentals=0)


def swap_pairs(block, axis, shift):
    size = lax.axis_size(axis)
    route = [(i, ((i + shift) ^ 1) - shift) for i in range(size)]
    return lax.ppermute(block, axis, [(i, k) for i, k in route if 0 <= k < size])


def per_device(
    offset, particle_mass, velocity, affine, deform,
    particle_cell, body_id, slot_tile_number, block_count, normal_code,
):
    params = pltpu.CompilerParams(vmem_limit_bytes=VMEM_LIMIT)
    smem = pl.BlockSpec(memory_space=pltpu.SMEM)
    hbm = pl.BlockSpec(memory_space=pltpu.HBM)
    whole = pl.BlockSpec(memory_space=pltpu.VMEM)
    face = jax.ShapeDtypeStruct((FACE_ROWS, DEPTH), F32)
    right_shape = jax.ShapeDtypeStruct((SLOTS, LANES, 256), BF16)
    last = (lax.axis_size("gx") - 1, lax.axis_size("gy") - 1)
    inputs = (
        slot_tile_number, offset, particle_mass, velocity, affine, deform, particle_cell,
        body_id, normal_code,
    )

    halves_shape = jax.ShapeDtypeStruct((2, CHANNELS, 6, 16, DEPTH), F32)
    scatter_scratch = [
        pltpu.SMEM((32,), jnp.int32),
        vmem((UNROLL, 192, 256), BF16),
        vmem((UNROLL, 192, 256), BF16),
        vmem((2, 2, 2, 280, LANES)),
        vmem((2, 2, 192, DEPTH)),
    ]
    anywhere = pl.BlockSpec(memory_space=pl.ANY)

    halves, x_d, table, rows, tile_numbers = pl.pallas_call(
        first_kernel,
        out_shape=(
            halves_shape,
            face,
            jax.ShapeDtypeStruct((GATHER_ROWS, 32, LANES), F32),
            jax.ShapeDtypeStruct((SCATTER_ROWS - GATHER_ROWS, 32, LANES), F32),
            jax.ShapeDtypeStruct((1, SLOTS), jnp.int32),
        ),
        in_specs=[smem] + [hbm] * 9,
        out_specs=(whole,) * 4 + (smem,),
        scratch_shapes=[vmem(x.shape, x.dtype) for x in inputs[1:]]
        + scatter_scratch
        + [pltpu.SemaphoreType.DMA((9,))],
        compiler_params=params,
        cost_estimate=cost(3000000),
        name="scatter_first",
    )(
        block_count,
        *(pltpu.with_memory_space_constraint(x, pltpu.HBM) for x in inputs),
    )
    got_x_d = swap_pairs(x_d, "gx", 1)
    halves, x_a = pl.pallas_call(
        second_kernel,
        out_shape=(halves_shape, face),
        in_specs=[smem] + [whole] * 3,
        out_specs=(whole,) * 2,
        scratch_shapes=scatter_scratch,
        input_output_aliases={1: 0},
        compiler_params=params,
        cost_estimate=cost(3000000),
        name="scatter_second",
    )(tile_numbers, halves, table, rows)
    got_x_a = swap_pairs(x_a, "gx", 0)
    right = pl.pallas_call(
        prepare_kernel,
        out_shape=right_shape,
        in_specs=[anywhere, smem, whole],
        out_specs=whole,
        compiler_params=params,
        cost_estimate=cost(3000000),
        name="prepare",
    )(x_a, tile_numbers, table)
    y_a, y_d, edge = pl.pallas_call(
        corner_kernel,
        out_shape=(face, face, jax.ShapeDtypeStruct((CHANNELS, 4, 16, DEPTH), F32)),
        in_specs=[anywhere] + [whole] * 3,
        out_specs=(whole,) * 3,
        compiler_params=params,
        name="corners",
    )(right, halves, got_x_a, got_x_d)
    got_y_d = swap_pairs(y_d, "gy", 1)
    got_y_a = swap_pairs(y_a, "gy", 0)
    slots, particles = particle_mass.shape
    gathered = pl.pallas_call(
        functools.partial(middle_kernel, last),
        out_shape=jax.ShapeDtypeStruct((12, slots, particles), F32),
        in_specs=[anywhere, smem] + [whole] * 4,
        out_specs=whole,
        scratch_shapes=[
            vmem((CHANNELS, SIDE, 8, DEPTH)),
            vmem((5, 3, 8 * SIDE, LANES)),
            vmem((12, 8 * CHUNK, LANES)),
        ],
        compiler_params=params,
        cost_estimate=cost(3000000),
        name="middle",
    )(y_a, tile_numbers, halves, edge, table, right)
    return pl.pallas_call(
        functools.partial(gather_kernel, last),
        out_shape=tuple(jax.ShapeDtypeStruct((k, slots, particles), F32) for k in (3, 9, 9, 6)),
        in_specs=[smem] + [whole] * 8,
        out_specs=(hbm,) * 4,
        scratch_shapes=[vmem((2, 5, 3, 24, LANES)), vmem((12, 8 * CHUNK, LANES))]
        + [vmem((k, slots, particles)) for k in (3, 9, 9, 6)]
        + [pltpu.SemaphoreType.DMA((SLOTS // CHUNK, 4))],
        compiler_params=params,
        name="gather",
    )(tile_numbers, gathered, y_a, y_d, got_y_a, got_y_d, table, right, deform)


def solution(mesh):
    both = ("gx", "gy")
    field = P(None, both, None)
    flat = P(both, None)
    return jax.shard_map(
        per_device,
        mesh=mesh,
        in_specs=(
            field, flat, field, field, field, flat, flat, P(both), P("gx", "gy"),
            P("gx", "gy", None),
        ),
        out_specs=(field,) * 4,
        check_vma=False,
    )
```

```python
import functools

import jax
import jax.numpy as jnp
from jax import lax
from jax.experimental import pallas as pl
from jax.experimental.pallas import tpu as pltpu
from jax.sharding import PartitionSpec as P


DT = 0.1
MU = 2.0
LAM = 3.0
GRAVITY = -2.0
FLOOR = 0.25

F32 = jnp.float32
BF16 = jnp.bfloat16
VMEM_LIMIT = 24 * 1024 * 1024

SIDE = 10
DEPTH = 256
SLOTS = 24
LANES = 128
X_FACE_ROWS = 184
Y_FACE_ROWS = 176
CHANNELS = 9
CHUNK = 8
UNROLL = 4

POS_Y, POS_Z, FIELD0, FIELD1, POS_X, LIVE, WX = 0, 1, 2, 3, 4, 5, 6
GATHER_ROWS = WX + 6
MASS = GATHER_ROWS
VEL = MASS + 1
AFF = VEL + 3
SCATTER_ROWS = AFF + 9


def spline(distance):
    size = jnp.abs(distance)
    outer = jnp.maximum(1.5 - size, 0.0)
    inner = jnp.maximum(0.5 - size, 0.0)
    return 0.5 * outer * outer - 1.5 * inner * inner


def determinant(m):
    return (
        m[0] * (m[4] * m[8] - m[5] * m[7])
        - m[1] * (m[3] * m[8] - m[5] * m[6])
        + m[2] * (m[3] * m[7] - m[4] * m[6])
    )


def kirchhoff(m):
    ratio = determinant(m)
    pressure = 0.5 * LAM * (ratio * ratio - 1.0)
    entries = []
    for i in range(3):
        for j in range(3):
            e = m[3 * i] * m[3 * j] + m[3 * i + 1] * m[3 * j + 1] + m[3 * i + 2] * m[3 * j + 2]
            entries.append(MU * (e - 1.0) + pressure if i == j else MU * e)
    return entries


def split(x):
    high = x.astype(BF16)
    return high, (x - high.astype(F32)).astype(BF16)


def matmul_t(a, b):
    return lax.dot_general(a, b, (((1,), (1,)), ((), ())), preferred_element_type=F32)


def matmul(a, b):
    return lax.dot_general(a, b, (((1,), (0,)), ((), ())), preferred_element_type=F32)


def iota(shape, axis):
    return lax.broadcasted_iota(jnp.int32, shape, axis)


def y_coords(tile_y):
    s = iota((8, LANES), 0)
    wrapped = jnp.where(s < 4, s + 4, s - 4)
    return jnp.where(tile_y == 0, s, wrapped).astype(F32)


def low_side(axis):
    return lax.axis_index(axis) % 2


def half(h):
    return slice(h * LANES, (h + 1) * LANES)


def matching_slots(order, tile_ref, tile_x):
    n = jnp.int32(0)
    for s in range(SLOTS):
        order[n] = s
        n = n + (lax.shift_right_logical(tile_ref[0, s], 6) == tile_x).astype(jnp.int32)
    for k in range(UNROLL - 1):
        order[n + k] = SLOTS
    return n


def clear(left_hi, left_lo, acc):
    acc[...] = jnp.zeros_like(acc)
    zeros = jnp.zeros((48, LANES), BF16)
    for u in range(UNROLL):
        left_hi[u, 0:48, LANES : 2 * LANES] = zeros
        left_lo[u, 0:48, LANES : 2 * LANES] = zeros


def scatter_half(tile_x, tile_ref, table, rows, halves, face, order, left_hi, left_lo,
                 acc, turned):
    count = matching_slots(order, tile_ref, tile_x)

    def one(index, u):
        s = order[index]
        tile = tile_ref[0, jnp.minimum(s, SLOTS - 1)]
        tile_y = lax.shift_right_logical(tile, 5) & 1
        tile_z = tile & 31

        def row(k):
            return table[k, pl.ds(s, 1), :] if k < MASS else rows[k - MASS, pl.ds(s, 1), :]

        dy = y_coords(tile_y) - row(POS_Y)
        wy = spline(dy)
        pos_x = row(POS_X)
        wxy = [wy * row(WX + x) for x in range(6)]

        def put(channel, column, values):
            for pair in range(3):
                hi, lo = split(jnp.concatenate(values[2 * pair : 2 * pair + 2], 0))
                at = channel * 48 + pair * 16
                left_hi[u, at : at + 16, column * LANES : (column + 1) * LANES] = hi
                left_lo[u, at : at + 16, column * LANES : (column + 1) * LANES] = lo

        m = row(MASS)
        put(0, 0, [w * m for w in wxy])
        for k in range(3):
            base = row(VEL + k) + row(AFF + 3 * k + 1) * dy
            ax = row(AFF + 3 * k)
            az = row(AFF + 3 * k + 2)
            put(1 + k, 0, [wxy[x] * (base + ax * (float(x) - pos_x)) for x in range(6)])
            put(1 + k, 1, [wxy[x] * az for x in range(6)])

        dz = iota((16, LANES), 0).astype(F32) - row(POS_Z)
        wz = spline(dz)
        mz = wz * dz
        parts = []
        for f in range(2):
            mask = row(FIELD0 + f)
            parts.append([split(wz * mask), split(mz * mask)])
        right_hi = jnp.concatenate(
            [jnp.concatenate([parts[f][0][0], parts[f][1][0]], 1) for f in range(2)], 0
        )
        right_lo = jnp.concatenate(
            [jnp.concatenate([parts[f][0][1], parts[f][1][1]], 1) for f in range(2)], 0
        )
        both = matmul_t(jnp.concatenate([right_hi, right_lo], 0), left_hi[u])
        rest = matmul_t(right_hi, left_lo[u])
        total = both[0:32] + both[32:64] + rest
        window = pl.ds(tile_z * 8 + 7, 16)
        for f in range(2):
            acc[tile_y, f, 0, window, :] += total[16 * f : 16 * f + 16, 0:LANES]
            acc[tile_y, f, 1, window, 0:64] += total[16 * f : 16 * f + 16, LANES:192]

    def step(group, carry):
        for u in range(UNROLL):
            one(group * UNROLL + u, u)
        return carry

    lax.fori_loop(0, lax.div(count + UNROLL - 1, UNROLL), step, 0)

    for ty in range(2):
        for f in range(2):
            for h in range(2):
                z = slice(8 + LANES * h, 8 + LANES * (h + 1))
                turned[ty, f, 0:128, half(h)] = acc[ty, f, 0, z, :].T
                turned[ty, f, 128:192, half(h)] = acc[ty, f, 1, z, :].T[0:64]

    upper = iota((8, DEPTH), 0) >= 4
    for f in range(2):
        for c in range(4):
            for x in range(6):
                at = (c * 6 + x) * 8
                high = turned[1, f, at : at + 8, :]
                halves[tile_x, 4 * f + c, x, 0:8, :] = turned[
                    0, f, at : at + 8, :
                ] + jnp.where(upper, high, 0.0)
                halves[tile_x, 4 * f + c, x, 8:16, :] = high
    for c in range(CHANNELS):
        for p in range(2):
            at = c * 2 + p
            face[at * 8 : at * 8 + 8, :] = halves[tile_x, c, 4 * tile_x + p, 0:8, :]
            face[144 + at * 2 : 146 + at * 2, :] = halves[tile_x, c, 4 * tile_x + p, 8:10, :]
    face[180:184, :] = jnp.zeros((4, DEPTH), F32)


def first_kernel(
    count_ref, tile_in, offset_in, mass_in, velocity_in, affine_in, deform_in, cell_in, body_in,
    code_in,
    halves, face, table, rows, tile_ref,
    offset, mass, velocity, affine, deform, cell, body, code,
    order, left_hi, left_lo, acc, turned, sems,
):
    pairs = (
        (tile_in, tile_ref.at[0]), (deform_in, deform), (affine_in, affine),
        (offset_in, offset), (velocity_in, velocity), (mass_in, mass), (cell_in, cell),
        (body_in, body), (code_in, code),
    )
    copies = [
        pltpu.make_async_copy(src, dst, sems.at[i]) for i, (src, dst) in enumerate(pairs)
    ]
    for copy in copies:
        copy.start()
    clear(left_hi, left_lo, acc)
    halves[:, 8] = jnp.zeros((2, 6, 16, DEPTH), F32)
    for out in (table, rows):
        for k in range(out.shape[0]):
            out[k, SLOTS:32, :] = jnp.zeros((32 - SLOTS, LANES), F32)
    for copy in copies:
        copy.wait()

    for x in range(1, 9):
        half_x = 0 if x < 6 else 1
        halves[half_x, 8, x - 4 * half_x, 1:9, :] = code[x - 1].astype(F32)
    live = (iota((SLOTS, LANES), 0) < count_ref[0, 0]).astype(F32)
    cell = cell[...]
    field_one = (body[...] & 1).astype(F32)
    pos_x = lax.shift_right_logical(cell, 5).astype(F32) + offset[0]
    own = slice(0, SLOTS)
    table[LIVE, own] = live
    table[POS_X, own] = pos_x
    table[POS_Y, own] = (lax.shift_right_logical(cell, 3) & 3).astype(F32) + offset[1]
    table[POS_Z, own] = (cell & 7).astype(F32) + offset[2]
    table[FIELD0, own] = 1.0 - field_one
    table[FIELD1, own] = field_one
    for x in range(6):
        table[WX + x, own] = spline(float(x) - pos_x)
    weighted = mass[...] * live
    rows[0, own] = weighted
    for k in range(3):
        rows[VEL - MASS + k, own] = weighted * velocity[k]
    stress = kirchhoff([deform[k] for k in range(9)])
    for k in range(9):
        rows[AFF - MASS + k, own] = weighted * (affine[k] - 4.0 * DT * stress[k])
    scatter_half(
        low_side("gx"), tile_ref, table, rows, halves, face, order, left_hi, left_lo, acc, turned,
    )


def second_kernel(
    tile_ref, half_in, table, rows, halves, face, order, left_hi, left_lo, acc, turned,
):
    clear(left_hi, left_lo, acc)
    scatter_half(
        1 - low_side("gx"), tile_ref, table, rows, halves, face, order, left_hi, left_lo,
        acc, turned,
    )


def prepare_kernel(order, tile_ref, table, right):
    none = jnp.zeros((16, 2 * LANES), BF16)

    def one(s, carry):
        dz = iota((16, LANES), 0).astype(F32) - table[POS_Z, pl.ds(s, 1), :]
        wz = spline(dz)
        mz = wz * dz
        for f in range(2):
            mask = table[FIELD0 + f, pl.ds(s, 1), :]
            hi, lo = split(jnp.concatenate([wz * mask, mz * mask], 1))
            for k, rows in enumerate((hi, lo, hi, none)):
                right[s, 64 * f + 16 * k : 64 * f + 16 * k + 16, :] = rows
        return carry

    lax.fori_loop(0, SLOTS, one, 0, unroll=2)


def plane(halves, edge, c, x, rows):
    if x < 2:
        return edge[c, x, rows, :]
    if x >= 8:
        return edge[c, x - 6, rows, :]
    if x < 4:
        return halves[0, c, x, rows, :]
    if x >= 6:
        return halves[1, c, x - 4, rows, :]
    return halves[0, c, x, rows, :] + halves[1, c, x - 4, rows, :]


def y_face_row(c, x):
    return c * 16 + x * 2 if x < 8 else 128 + c * 4 + (x - 8) * 2


def corner_kernel(order, halves, recv_a, recv_d, face_a, face_d, edge):
    side_y = low_side("gy")
    side_x = low_side("gx")
    for recv, high in ((recv_a, 1 - side_x), (recv_d, side_x)):
        for c in range(CHANNELS):
            for p in range(2):
                at = c * 2 + p
                own = (high, c, 4 * high + p)
                to = (c, 2 * high + p)
                edge[(*to, slice(0, 8))] = halves[(*own, slice(0, 8))] + recv[at * 8 : at * 8 + 8]
                edge[(*to, slice(8, 16))] = halves[(*own, slice(8, 16))]
                edge[(*to, slice(8, 10))] += recv[144 + at * 2 : 146 + at * 2]
    for face, high in ((face_a, 1 - side_y), (face_d, side_y)):
        rows = pl.ds(pl.multiple_of(high * 8, 8), 2)
        for c in range(8):
            for x in range(SIDE):
                at = y_face_row(c, x)
                face[at : at + 2, :] = plane(halves, edge, c, x, rows)
        own_row = pl.ds(1 + 7 * high, 1)
        for x in range(SIDE):
            face[160 + x : 161 + x, :] = plane(halves, edge, 8, x, own_row)
        face[170:176, :] = jnp.zeros((6, DEPTH), F32)


def node_speeds(sums, code, inside):
    m0, m1 = sums[0], sums[4]
    r0 = 1.0 / jnp.maximum(m0, FLOOR)
    r1 = 1.0 / jnp.maximum(m1, FLOOR)
    rc = 1.0 / jnp.maximum(m0 + m1, FLOOR)
    share = jnp.minimum(1.0, jnp.minimum(m0, m1) * (1.0 / FLOOR))
    shifted = code + jnp.where(code >= 13.0, 1.0, 0.0)
    third = jnp.where(shifted >= 9.0, 1.0, 0.0) + jnp.where(shifted >= 18.0, 1.0, 0.0)
    rest = shifted - 9.0 * third
    second = jnp.where(rest >= 3.0, 1.0, 0.0) + jnp.where(rest >= 6.0, 1.0, 0.0)
    direction = [third - 1.0, second - 1.0, rest - 3.0 * second - 1.0]
    square = (
        direction[0] * direction[0] + direction[1] * direction[1] + direction[2] * direction[2]
    )
    inverse = jnp.where(square > 2.5, 1.0 / 3.0, jnp.where(square > 1.5, 0.5, 1.0))
    u0 = [sums[1 + k] * r0 for k in range(3)]
    u1 = [sums[5 + k] * r1 for k in range(3)]
    uc = [(sums[1 + k] + sums[5 + k]) * rc for k in range(3)]
    approach0 = sum((u0[k] - uc[k]) * direction[k] for k in range(3))
    approach1 = sum((uc[k] - u1[k]) * direction[k] for k in range(3))
    scale = share * inverse
    push0 = scale * jnp.maximum(approach0, 0.0)
    push1 = scale * jnp.maximum(approach1, 0.0)
    gravity = [0.0, 0.0, DT * GRAVITY]
    v0 = [(u0[k] - push0 * direction[k] + gravity[k]) * inside for k in range(3)]
    v1 = [(u1[k] + push1 * direction[k] + gravity[k]) * inside for k in range(3)]
    return v0, v1


def tiles(v0, v1):
    lane = iota(v0[0].shape, 1)
    local = lane & 63

    def both(h, shift):
        return jnp.where(
            lane < 64, pltpu.roll(v0[h], shift, 1), pltpu.roll(v1[h], (shift + 64) % 128, 1)
        )

    return (
        jnp.where(local < 1, 0.0, both(0, 1)),
        both(0, 73),
        jnp.where(local < 17, both(0, 17), both(1, 17)),
        both(1, 89),
        jnp.where(local < 33, both(1, 33), 0.0),
    )


def inside_x(x, last):
    index = lax.axis_index("gx")
    return jnp.where(((x == 0) & (index == 0)) | ((x == SIDE - 1) & (index == last[0])), 0.0, 1.0)


def tile_of(tile_ref, s):
    tile = tile_ref[0, s]
    tile_z = tile & 31
    j = lax.div(tile_z, 7)
    return (
        lax.shift_right_logical(tile, 6),
        lax.shift_right_logical(tile, 5) & 1,
        j,
        (tile_z - 7 * j) * 8,
    )


def z_window(value, shift):
    lane = iota(value.shape, 1) & 63
    window = pltpu.roll(value, lax.rem(128 - shift, 128), 1)
    window = jnp.where(lane < 16, window, pltpu.roll(value, lax.rem(144 - shift, 128), 1))
    window = jnp.where(lane < 32, window, pltpu.roll(value, lax.rem(160 - shift, 128), 1))
    high = window.astype(BF16).astype(F32)
    return jnp.where(lane < 32, high, window - high).astype(BF16)


def collect(partial, k):
    total = partial[k, pl.ds(0, CHUNK, stride=8), :]
    for y in range(1, 8):
        total = total + partial[k, pl.ds(y, CHUNK, stride=8), :]
    return total


def chunk_of(chunk):
    if isinstance(chunk, int):
        return slice(chunk * CHUNK, (chunk + 1) * CHUNK)
    return pl.ds(pl.multiple_of(chunk * CHUNK, CHUNK), CHUNK)


def middle_kernel(
    last, order, tile_ref, halves, edge, table, right, gathered, work, nodes, partial,
):
    for c in range(CHANNELS):
        for x in range(SIDE):
            work[c, x] = plane(halves, edge, c, x, slice(0, 8))
    inner = iota((8, LANES), 0) >= 2

    def node_step(x, carry):
        inside = inside_x(x, last)
        found = [
            node_speeds([work[c, x, :, half(h)] for c in range(8)], work[8, x, :, half(h)], inside)
            for h in range(2)
        ]
        at = pl.multiple_of(x * 8, 8)
        for c in range(3):
            ready = tiles(*([found[h][f][c] for h in range(2)] for f in range(2)))
            for j in range(5):
                nodes[j, c, pl.ds(at, 8), :] = jnp.where(inner, ready[j], 0.0)
        return carry

    lax.fori_loop(0, SIDE, node_step, 0, unroll=2)

    def one(chunk, slot):
        s = chunk * CHUNK + slot
        tile_x, tile_y, j, shift = tile_of(tile_ref, s)

        def row(k):
            return table[k, pl.ds(s, 1), :]

        first = pl.multiple_of(tile_x * 32, 32)
        left = [z_window(nodes[j, c, pl.ds(first, 48), :], shift) for c in range(3)]
        summed = matmul(jnp.concatenate(left, 0), right[s])
        dy = y_coords(tile_y) - row(POS_Y)
        wy = spline(dy)
        pos_x = row(POS_X)
        wxy = [wy * row(WX + x) for x in range(6)]
        place = slice(slot * 8, slot * 8 + 8)
        for c in range(3):
            speed = along_x = along_z = None
            for x in range(5, -1, -1):
                at = (c * 6 + x) * 8
                part = wxy[x] * summed[at : at + 8, 0:LANES]
                moment = wxy[x] * summed[at : at + 8, LANES : 2 * LANES]
                speed = part if speed is None else speed + part
                along_z = moment if along_z is None else along_z + moment
                if x:
                    along_x = speed if along_x is None else along_x + speed
            partial[4 * c, place, :] = speed
            partial[4 * c + 1, place, :] = along_x - pos_x * speed
            partial[4 * c + 2, place, :] = speed * dy
            partial[4 * c + 3, place, :] = along_z

    def step(chunk, carry):
        for slot in range(CHUNK):
            one(chunk, slot)
        for k in range(12):
            gathered[k, chunk_of(chunk), :] = collect(partial, k)
        return carry

    lax.fori_loop(0, SLOTS // CHUNK, step, 0)


def gather_kernel(
    last, tile_ref, gathered, own_a, own_d, y_a, y_d, table, right, deform,
    velocity_out, affine_out, deform_out, stress_out,
    nodes, codes, partial, new_velocity, new_affine, new_deform, new_stress, sems,
):
    side_y = low_side("gy")
    index_y = lax.axis_index("gy")
    for own, recv, high in ((own_a, y_a, 1 - side_y), (own_d, y_d, side_y)):
        edge_y = jnp.where(high == 0, (index_y == 0), (index_y == last[1]))
        for x in range(SIDE):
            codes[pl.ds(2 * x + 1 - high, 1), :] = own[160 + x : 161 + x, :]
            codes[pl.ds(2 * x + high, 1), :] = recv[160 + x : 161 + x, :]
        for first, count in ((0, 8), (8, 2)):
            row = iota((2 * count, LANES), 0)
            inside = inside_x(lax.shift_right_logical(row, 1) + first, last)
            inside = jnp.where(((row & 1) == high) & edge_y, 0.0, inside)
            found = []
            for h in range(2):
                sums = []
                for c in range(8):
                    at = y_face_row(c, first)
                    rows = slice(at, at + 2 * count)
                    sums.append(own[rows, half(h)] + recv[rows, half(h)])
                code = codes[2 * first : 2 * (first + count), half(h)]
                found.append(node_speeds(sums, code, inside))
            for c in range(3):
                ready = tiles(*([found[h][f][c] for h in range(2)] for f in range(2)))
                for j in range(5):
                    nodes[high, j, c, 2 * first : 2 * (first + count), :] = ready[j]
        for c in range(3):
            for j in range(5):
                nodes[high, j, c, 2 * SIDE : 24, :] = jnp.zeros((24 - 2 * SIDE, LANES), F32)

    def one(chunk, slot):
        s = chunk * CHUNK + slot
        tile_x, tile_y, j, shift = tile_of(tile_ref, s)

        def row(k):
            return table[k, pl.ds(s, 1), :]

        first = pl.multiple_of(tile_x * 8, 8)
        left = [nodes[tile_y, j, c, pl.ds(first, 16), :] for c in range(3)]
        summed = matmul(z_window(jnp.concatenate(left, 0), shift), right[s])
        sublane = iota((8, LANES), 0)
        dy = ((sublane & 1) + 4 * tile_y).astype(F32) - row(POS_Y)
        wy = spline(dy)
        speed, along_x, along_z = [None] * 3, [None] * 3, [None] * 3
        for q in range(2):
            dx = (lax.shift_right_logical(sublane, 1) + 4 * q).astype(F32) - row(POS_X)
            weight = wy * spline(dx)
            for c in range(3):
                at = c * 16 + q * 8
                part = weight * summed[at : at + 8, 0:LANES]
                moment = weight * summed[at : at + 8, LANES : 2 * LANES]
                speed[c] = part if q == 0 else speed[c] + part
                along_x[c] = part * dx if q == 0 else along_x[c] + part * dx
                along_z[c] = moment if q == 0 else along_z[c] + moment
        place = slice(slot * 8, slot * 8 + 8)
        for c in range(3):
            partial[chunk, 4 * c, place, :] = speed[c]
            partial[chunk, 4 * c + 1, place, :] = along_x[c]
            partial[chunk, 4 * c + 2, place, :] = speed[c] * dy
            partial[chunk, 4 * c + 3, place, :] = along_z[c]

    ready = (new_velocity, new_affine, new_deform, new_stress)
    finals = (velocity_out, affine_out, deform_out, stress_out)

    def sends(chunk):
        slots = chunk_of(chunk)
        return [
            pltpu.make_async_copy(src.at[:, slots], dst.at[:, slots], sems.at[chunk, i])
            for i, (src, dst) in enumerate(zip(ready, finals))
        ]

    def step(chunk):
        for slot in range(CHUNK):
            one(chunk, slot)
        slots = chunk_of(chunk)
        live = table[LIVE, slots, :]
        total = [(gathered[k, slots, :] + collect(partial.at[chunk], k)) * live for k in range(12)]
        moved = []
        for c in range(3):
            new_velocity[c, slots, :] = total[4 * c]
            for k in range(3):
                value = 4.0 * total[4 * c + 1 + k]
                new_affine[3 * c + k, slots, :] = value
                moved.append(value)
        old = [deform[k, slots, :] for k in range(9)]
        fresh = []
        for i in range(3):
            for j in range(3):
                value = old[3 * i + j]
                for k in range(3):
                    value = value + DT * moved[3 * i + k] * old[3 * k + j]
                fresh.append(value * live)
        for k in range(9):
            new_deform[k, slots, :] = fresh[k]
        stress = kirchhoff(fresh)
        for k, entry in enumerate((0, 4, 8, 1, 2, 5)):
            new_stress[k, slots, :] = stress[entry] * live
        for send in sends(chunk):
            send.start()

    for chunk in range(SLOTS // CHUNK):
        step(chunk)
    for chunk in range(SLOTS // CHUNK):
        for send in sends(chunk):
            send.wait()


def vmem(shape, dtype=F32):
    return pltpu.VMEM(shape, dtype)


def cost(flops):
    return pl.CostEstimate(flops=flops, bytes_accessed=4000000, transcendentals=0)


def swap_pairs(block, axis, shift):
    size = lax.axis_size(axis)
    route = [(i, ((i + shift) ^ 1) - shift) for i in range(size)]
    return lax.ppermute(block, axis, [(i, k) for i, k in route if 0 <= k < size])


def per_device(
    offset, particle_mass, velocity, affine, deform,
    particle_cell, body_id, slot_tile_number, block_count, normal_code,
):
    params = pltpu.CompilerParams(vmem_limit_bytes=VMEM_LIMIT)
    smem = pl.BlockSpec(memory_space=pltpu.SMEM)
    hbm = pl.BlockSpec(memory_space=pltpu.HBM)
    whole = pl.BlockSpec(memory_space=pltpu.VMEM)
    x_face = jax.ShapeDtypeStruct((X_FACE_ROWS, DEPTH), F32)
    y_face = jax.ShapeDtypeStruct((Y_FACE_ROWS, DEPTH), F32)
    right_shape = jax.ShapeDtypeStruct((SLOTS, LANES, 256), BF16)
    last = (lax.axis_size("gx") - 1, lax.axis_size("gy") - 1)
    inputs = (
        slot_tile_number, offset, particle_mass, velocity, affine, deform, particle_cell,
        body_id, normal_code,
    )

    halves_shape = jax.ShapeDtypeStruct((2, CHANNELS, 6, 16, DEPTH), F32)
    scatter_scratch = [
        pltpu.SMEM((32,), jnp.int32),
        vmem((UNROLL, 192, 256), BF16),
        vmem((UNROLL, 192, 256), BF16),
        vmem((2, 2, 2, 280, LANES)),
        vmem((2, 2, 192, DEPTH)),
    ]
    anywhere = pl.BlockSpec(memory_space=pl.ANY)

    halves, x_d, table, rows, tile_numbers = pl.pallas_call(
        first_kernel,
        out_shape=(
            halves_shape,
            x_face,
            jax.ShapeDtypeStruct((GATHER_ROWS, 32, LANES), F32),
            jax.ShapeDtypeStruct((SCATTER_ROWS - GATHER_ROWS, 32, LANES), F32),
            jax.ShapeDtypeStruct((1, SLOTS), jnp.int32),
        ),
        in_specs=[smem] + [hbm] * 9,
        out_specs=(whole,) * 4 + (smem,),
        scratch_shapes=[vmem(x.shape, x.dtype) for x in inputs[1:]]
        + scatter_scratch
        + [pltpu.SemaphoreType.DMA((9,))],
        compiler_params=params,
        cost_estimate=cost(3000000),
        name="scatter_first",
    )(
        block_count,
        *(pltpu.with_memory_space_constraint(x, pltpu.HBM) for x in inputs),
    )
    got_x_d = swap_pairs(x_d, "gx", 1)
    halves, x_a = pl.pallas_call(
        second_kernel,
        out_shape=(halves_shape, x_face),
        in_specs=[smem] + [whole] * 3,
        out_specs=(whole,) * 2,
        scratch_shapes=scatter_scratch,
        input_output_aliases={1: 0},
        compiler_params=params,
        cost_estimate=cost(3000000),
        name="scatter_second",
    )(tile_numbers, halves, table, rows)
    got_x_a = swap_pairs(x_a, "gx", 0)
    right = pl.pallas_call(
        prepare_kernel,
        out_shape=right_shape,
        in_specs=[anywhere, smem, whole],
        out_specs=whole,
        compiler_params=params,
        cost_estimate=cost(3000000),
        name="prepare",
    )(x_a, tile_numbers, table)
    y_a, y_d, edge = pl.pallas_call(
        corner_kernel,
        out_shape=(y_face, y_face, jax.ShapeDtypeStruct((CHANNELS, 4, 16, DEPTH), F32)),
        in_specs=[anywhere] + [whole] * 3,
        out_specs=(whole,) * 3,
        compiler_params=params,
        name="corners",
    )(right, halves, got_x_a, got_x_d)
    got_y_d = swap_pairs(y_d, "gy", 1)
    got_y_a = swap_pairs(y_a, "gy", 0)
    slots, particles = particle_mass.shape
    gathered = pl.pallas_call(
        functools.partial(middle_kernel, last),
        out_shape=jax.ShapeDtypeStruct((12, slots, particles), F32),
        in_specs=[anywhere, smem] + [whole] * 4,
        out_specs=whole,
        scratch_shapes=[
            vmem((CHANNELS, SIDE, 8, DEPTH)),
            vmem((5, 3, 8 * SIDE, LANES)),
            vmem((12, 8 * CHUNK, LANES)),
        ],
        compiler_params=params,
        cost_estimate=cost(3000000),
        name="middle",
    )(y_a, tile_numbers, halves, edge, table, right)
    return pl.pallas_call(
        functools.partial(gather_kernel, last),
        out_shape=tuple(jax.ShapeDtypeStruct((k, slots, particles), F32) for k in (3, 9, 9, 6)),
        in_specs=[smem] + [whole] * 8,
        out_specs=(hbm,) * 4,
        scratch_shapes=[vmem((2, 5, 3, 24, LANES)), vmem((24, DEPTH)), vmem((SLOTS // CHUNK, 12, 8 * CHUNK, LANES))]
        + [vmem((k, slots, particles)) for k in (3, 9, 9, 6)]
        + [pltpu.SemaphoreType.DMA((SLOTS // CHUNK, 4))],
        compiler_params=params,
        name="gather",
    )(tile_numbers, gathered, y_a, y_d, got_y_a, got_y_d, table, right, deform)


def solution(mesh):
    both = ("gx", "gy")
    field = P(None, both, None)
    flat = P(both, None)
    return jax.shard_map(
        per_device,
        mesh=mesh,
        in_specs=(
            field, flat, field, field, field, flat, flat, P(both), P("gx", "gy"),
            P("gx", "gy", None),
        ),
        out_specs=(field,) * 4,
        check_vma=False,
    )
```

```python
import functools

import jax
import jax.numpy as jnp
from jax import lax
from jax.experimental import pallas as pl
from jax.experimental.pallas import tpu as pltpu
from jax.sharding import PartitionSpec as P


DT = 0.1
MU = 2.0
LAM = 3.0
GRAVITY = -2.0
FLOOR = 0.25

F32 = jnp.float32
BF16 = jnp.bfloat16
VMEM_LIMIT = 24 * 1024 * 1024

SIDE = 10
DEPTH = 256
SLOTS = 24
LANES = 128
X_FACE_ROWS = 184
Y_FACE_ROWS = 176
CHANNELS = 9
CHUNK = 8
UNROLL = 4

POS_Y, POS_Z, FIELD0, FIELD1, POS_X, LIVE, WX = 0, 1, 2, 3, 4, 5, 6
GATHER_ROWS = WX + 6
MASS = GATHER_ROWS
VEL = MASS + 1
AFF = VEL + 3
SCATTER_ROWS = AFF + 9


def spline(distance):
    size = jnp.abs(distance)
    outer = jnp.maximum(1.5 - size, 0.0)
    inner = jnp.maximum(0.5 - size, 0.0)
    return 0.5 * outer * outer - 1.5 * inner * inner


def determinant(m):
    return (
        m[0] * (m[4] * m[8] - m[5] * m[7])
        - m[1] * (m[3] * m[8] - m[5] * m[6])
        + m[2] * (m[3] * m[7] - m[4] * m[6])
    )


def kirchhoff(m):
    ratio = determinant(m)
    pressure = 0.5 * LAM * (ratio * ratio - 1.0)
    entries = []
    for i in range(3):
        for j in range(3):
            e = m[3 * i] * m[3 * j] + m[3 * i + 1] * m[3 * j + 1] + m[3 * i + 2] * m[3 * j + 2]
            entries.append(MU * (e - 1.0) + pressure if i == j else MU * e)
    return entries


def split(x):
    high = x.astype(BF16)
    return high, (x - high.astype(F32)).astype(BF16)


def matmul_t(a, b):
    return lax.dot_general(a, b, (((1,), (1,)), ((), ())), preferred_element_type=F32)


def matmul(a, b):
    return lax.dot_general(a, b, (((1,), (0,)), ((), ())), preferred_element_type=F32)


def iota(shape, axis):
    return lax.broadcasted_iota(jnp.int32, shape, axis)


def y_coords(tile_y):
    s = iota((8, LANES), 0)
    wrapped = jnp.where(s < 4, s + 4, s - 4)
    return jnp.where(tile_y == 0, s, wrapped).astype(F32)


def low_side(axis):
    return lax.axis_index(axis) % 2


def half(h):
    return slice(h * LANES, (h + 1) * LANES)


def matching_slots(order, tile_ref, tile_x):
    n = jnp.int32(0)
    for s in range(SLOTS):
        order[n] = s
        n = n + (lax.shift_right_logical(tile_ref[0, s], 6) == tile_x).astype(jnp.int32)
    for k in range(UNROLL - 1):
        order[n + k] = SLOTS
    return n


def clear(left_hi, left_lo, acc):
    acc[...] = jnp.zeros_like(acc)
    zeros = jnp.zeros((48, LANES), BF16)
    for u in range(UNROLL):
        left_hi[u, 0:48, LANES : 2 * LANES] = zeros
        left_lo[u, 0:48, LANES : 2 * LANES] = zeros


def scatter_half(tile_x, tile_ref, table, rows, halves, face, order, left_hi, left_lo,
                 acc, turned):
    count = matching_slots(order, tile_ref, tile_x)

    def one(index, u):
        s = order[index]
        tile = tile_ref[0, jnp.minimum(s, SLOTS - 1)]
        tile_y = lax.shift_right_logical(tile, 5) & 1
        tile_z = tile & 31

        def row(k):
            return table[k, pl.ds(s, 1), :] if k < MASS else rows[k - MASS, pl.ds(s, 1), :]

        dy = y_coords(tile_y) - row(POS_Y)
        wy = spline(dy)
        pos_x = row(POS_X)
        wxy = [wy * row(WX + x) for x in range(6)]

        def put(channel, column, values):
            for pair in range(3):
                hi, lo = split(jnp.concatenate(values[2 * pair : 2 * pair + 2], 0))
                at = channel * 48 + pair * 16
                left_hi[u, at : at + 16, column * LANES : (column + 1) * LANES] = hi
                left_lo[u, at : at + 16, column * LANES : (column + 1) * LANES] = lo

        m = row(MASS)
        put(0, 0, [w * m for w in wxy])
        for k in range(3):
            base = row(VEL + k) + row(AFF + 3 * k + 1) * dy
            ax = row(AFF + 3 * k)
            az = row(AFF + 3 * k + 2)
            put(1 + k, 0, [wxy[x] * (base + ax * (float(x) - pos_x)) for x in range(6)])
            put(1 + k, 1, [wxy[x] * az for x in range(6)])

        dz = iota((16, LANES), 0).astype(F32) - row(POS_Z)
        wz = spline(dz)
        mz = wz * dz
        parts = []
        for f in range(2):
            mask = row(FIELD0 + f)
            parts.append([split(wz * mask), split(mz * mask)])
        right_hi = jnp.concatenate(
            [jnp.concatenate([parts[f][0][0], parts[f][1][0]], 1) for f in range(2)], 0
        )
        right_lo = jnp.concatenate(
            [jnp.concatenate([parts[f][0][1], parts[f][1][1]], 1) for f in range(2)], 0
        )
        both = matmul_t(jnp.concatenate([right_hi, right_lo], 0), left_hi[u])
        rest = matmul_t(right_hi, left_lo[u])
        total = both[0:32] + both[32:64] + rest
        window = pl.ds(tile_z * 8 + 7, 16)
        for f in range(2):
            acc[tile_y, f, 0, window, :] += total[16 * f : 16 * f + 16, 0:LANES]
            acc[tile_y, f, 1, window, 0:64] += total[16 * f : 16 * f + 16, LANES:192]

    def step(group, carry):
        for u in range(UNROLL):
            one(group * UNROLL + u, u)
        return carry

    lax.fori_loop(0, lax.div(count + UNROLL - 1, UNROLL), step, 0)

    for ty in range(2):
        for f in range(2):
            for h in range(2):
                z = slice(8 + LANES * h, 8 + LANES * (h + 1))
                turned[ty, f, 0:128, half(h)] = acc[ty, f, 0, z, :].T
                turned[ty, f, 128:192, half(h)] = acc[ty, f, 1, z, :].T[0:64]

    upper = iota((8, DEPTH), 0) >= 4
    for f in range(2):
        for c in range(4):
            for x in range(6):
                at = (c * 6 + x) * 8
                high = turned[1, f, at : at + 8, :]
                halves[tile_x, 4 * f + c, x, 0:8, :] = turned[
                    0, f, at : at + 8, :
                ] + jnp.where(upper, high, 0.0)
                halves[tile_x, 4 * f + c, x, 8:16, :] = high
    for c in range(CHANNELS):
        for p in range(2):
            at = c * 2 + p
            face[at * 8 : at * 8 + 8, :] = halves[tile_x, c, 4 * tile_x + p, 0:8, :]
            face[144 + at * 2 : 146 + at * 2, :] = halves[tile_x, c, 4 * tile_x + p, 8:10, :]
    face[180:184, :] = jnp.zeros((4, DEPTH), F32)


def first_kernel(
    count_ref, tile_in, offset_in, mass_in, velocity_in, affine_in, deform_in, cell_in, body_in,
    code_in,
    halves, face, table, rows, tile_ref,
    offset, mass, velocity, affine, deform, cell, body, code,
    order, left_hi, left_lo, acc, turned, sems,
):
    pairs = (
        (tile_in, tile_ref.at[0]), (deform_in, deform), (affine_in, affine),
        (offset_in, offset), (velocity_in, velocity), (mass_in, mass), (cell_in, cell),
        (body_in, body), (code_in, code),
    )
    copies = [
        pltpu.make_async_copy(src, dst, sems.at[i]) for i, (src, dst) in enumerate(pairs)
    ]
    for copy in copies:
        copy.start()
    clear(left_hi, left_lo, acc)
    halves[:, 8] = jnp.zeros((2, 6, 16, DEPTH), F32)
    for out in (table, rows):
        for k in range(out.shape[0]):
            out[k, SLOTS:32, :] = jnp.zeros((32 - SLOTS, LANES), F32)
    for copy in copies:
        copy.wait()

    for x in range(1, 9):
        half_x = 0 if x < 6 else 1
        halves[half_x, 8, x - 4 * half_x, 1:9, :] = code[x - 1].astype(F32)
    live = (iota((SLOTS, LANES), 0) < count_ref[0, 0]).astype(F32)
    cell = cell[...]
    field_one = (body[...] & 1).astype(F32)
    pos_x = lax.shift_right_logical(cell, 5).astype(F32) + offset[0]
    own = slice(0, SLOTS)
    table[LIVE, own] = live
    table[POS_X, own] = pos_x
    table[POS_Y, own] = (lax.shift_right_logical(cell, 3) & 3).astype(F32) + offset[1]
    table[POS_Z, own] = (cell & 7).astype(F32) + offset[2]
    table[FIELD0, own] = 1.0 - field_one
    table[FIELD1, own] = field_one
    for x in range(6):
        table[WX + x, own] = spline(float(x) - pos_x)
    weighted = mass[...] * live
    rows[0, own] = weighted
    for k in range(3):
        rows[VEL - MASS + k, own] = weighted * velocity[k]
    stress = kirchhoff([deform[k] for k in range(9)])
    for k in range(9):
        rows[AFF - MASS + k, own] = weighted * (affine[k] - 4.0 * DT * stress[k])
    scatter_half(
        low_side("gx"), tile_ref, table, rows, halves, face, order, left_hi, left_lo, acc, turned,
    )


def second_kernel(
    tile_ref, half_in, table, rows, halves, face, order, left_hi, left_lo, acc, turned,
):
    clear(left_hi, left_lo, acc)
    scatter_half(
        1 - low_side("gx"), tile_ref, table, rows, halves, face, order, left_hi, left_lo,
        acc, turned,
    )


def prepare_kernel(order, tile_ref, table, right, edge_weights):
    none = jnp.zeros((16, 2 * LANES), BF16)

    def one(s, carry):
        dz = iota((16, LANES), 0).astype(F32) - table[POS_Z, pl.ds(s, 1), :]
        wz = spline(dz)
        mz = wz * dz
        for f in range(2):
            mask = table[FIELD0 + f, pl.ds(s, 1), :]
            hi, lo = split(jnp.concatenate([wz * mask, mz * mask], 1))
            for k, rows in enumerate((hi, lo, hi, none)):
                right[s, 64 * f + 16 * k : 64 * f + 16 * k + 16, :] = rows
        sublane = iota((8, LANES), 0)
        tile_y = lax.shift_right_logical(tile_ref[0, s], 5) & 1
        wy = spline(((sublane & 1) + 4 * tile_y).astype(F32) - table[POS_Y, pl.ds(s, 1), :])
        for q in range(2):
            dx = (lax.shift_right_logical(sublane, 1) + 4 * q).astype(F32)
            edge_weights[s, q] = wy * spline(dx - table[POS_X, pl.ds(s, 1), :])
        return carry

    lax.fori_loop(0, SLOTS, one, 0, unroll=2)


def plane(halves, edge, c, x, rows):
    if x < 2:
        return edge[c, x, rows, :]
    if x >= 8:
        return edge[c, x - 6, rows, :]
    if x < 4:
        return halves[0, c, x, rows, :]
    if x >= 6:
        return halves[1, c, x - 4, rows, :]
    return halves[0, c, x, rows, :] + halves[1, c, x - 4, rows, :]


def y_face_row(c, x):
    return c * 16 + x * 2 if x < 8 else 128 + c * 4 + (x - 8) * 2


def corner_kernel(order, halves, recv_a, recv_d, face_a, face_d, edge):
    side_y = low_side("gy")
    side_x = low_side("gx")
    for recv, high in ((recv_a, 1 - side_x), (recv_d, side_x)):
        for c in range(CHANNELS):
            for p in range(2):
                at = c * 2 + p
                own = (high, c, 4 * high + p)
                to = (c, 2 * high + p)
                edge[(*to, slice(0, 2))] = halves[(*own, slice(0, 2))] + recv[at * 8 : at * 8 + 2]
                edge[(*to, slice(8, 10))] = (
                    halves[(*own, slice(8, 10))] + recv[144 + at * 2 : 146 + at * 2]
                )
    for face, high in ((face_a, 1 - side_y), (face_d, side_y)):
        rows = pl.ds(pl.multiple_of(high * 8, 8), 2)
        for c in range(8):
            for x in range(SIDE):
                at = y_face_row(c, x)
                face[at : at + 2, :] = plane(halves, edge, c, x, rows)
        own_row = pl.ds(1 + 7 * high, 1)
        for x in range(SIDE):
            face[160 + x : 161 + x, :] = plane(halves, edge, 8, x, own_row)
        face[170:176, :] = jnp.zeros((6, DEPTH), F32)


def node_speeds(sums, code, inside):
    m0, m1 = sums[0], sums[4]
    r0 = 1.0 / jnp.maximum(m0, FLOOR)
    r1 = 1.0 / jnp.maximum(m1, FLOOR)
    rc = 1.0 / jnp.maximum(m0 + m1, FLOOR)
    share = jnp.minimum(1.0, jnp.minimum(m0, m1) * (1.0 / FLOOR))
    shifted = code + jnp.where(code >= 13.0, 1.0, 0.0)
    third = jnp.where(shifted >= 9.0, 1.0, 0.0) + jnp.where(shifted >= 18.0, 1.0, 0.0)
    rest = shifted - 9.0 * third
    second = jnp.where(rest >= 3.0, 1.0, 0.0) + jnp.where(rest >= 6.0, 1.0, 0.0)
    direction = [third - 1.0, second - 1.0, rest - 3.0 * second - 1.0]
    square = (
        direction[0] * direction[0] + direction[1] * direction[1] + direction[2] * direction[2]
    )
    inverse = jnp.where(square > 2.5, 1.0 / 3.0, jnp.where(square > 1.5, 0.5, 1.0))
    u0 = [sums[1 + k] * r0 for k in range(3)]
    u1 = [sums[5 + k] * r1 for k in range(3)]
    uc = [(sums[1 + k] + sums[5 + k]) * rc for k in range(3)]
    approach0 = sum((u0[k] - uc[k]) * direction[k] for k in range(3))
    approach1 = sum((uc[k] - u1[k]) * direction[k] for k in range(3))
    scale = share * inverse
    push0 = scale * jnp.maximum(approach0, 0.0)
    push1 = scale * jnp.maximum(approach1, 0.0)
    gravity = [0.0, 0.0, DT * GRAVITY]
    v0 = [(u0[k] - push0 * direction[k] + gravity[k]) * inside for k in range(3)]
    v1 = [(u1[k] + push1 * direction[k] + gravity[k]) * inside for k in range(3)]
    return v0, v1


def tiles(v0, v1):
    lane = iota(v0[0].shape, 1)
    local = lane & 63

    def both(h, shift):
        return jnp.where(
            lane < 64, pltpu.roll(v0[h], shift, 1), pltpu.roll(v1[h], (shift + 64) % 128, 1)
        )

    return (
        jnp.where(local < 1, 0.0, both(0, 1)),
        both(0, 73),
        jnp.where(local < 17, both(0, 17), both(1, 17)),
        both(1, 89),
        jnp.where(local < 33, both(1, 33), 0.0),
    )


def inside_x(x, last):
    index = lax.axis_index("gx")
    return jnp.where(((x == 0) & (index == 0)) | ((x == SIDE - 1) & (index == last[0])), 0.0, 1.0)


def tile_of(tile_ref, s):
    tile = tile_ref[0, s]
    tile_z = tile & 31
    j = lax.div(tile_z, 7)
    return (
        lax.shift_right_logical(tile, 6),
        lax.shift_right_logical(tile, 5) & 1,
        j,
        (tile_z - 7 * j) * 8,
    )


def z_window(value, shift):
    lane = iota(value.shape, 1) & 63
    window = pltpu.roll(value, lax.rem(128 - shift, 128), 1)
    window = jnp.where(lane < 16, window, pltpu.roll(value, lax.rem(144 - shift, 128), 1))
    window = jnp.where(lane < 32, window, pltpu.roll(value, lax.rem(160 - shift, 128), 1))
    high = window.astype(BF16).astype(F32)
    return jnp.where(lane < 32, high, window - high).astype(BF16)


def collect(partial, k):
    total = partial[k, pl.ds(0, CHUNK, stride=8), :]
    for y in range(1, 8):
        total = total + partial[k, pl.ds(y, CHUNK, stride=8), :]
    return total


def chunk_of(chunk):
    if isinstance(chunk, int):
        return slice(chunk * CHUNK, (chunk + 1) * CHUNK)
    return pl.ds(pl.multiple_of(chunk * CHUNK, CHUNK), CHUNK)


def middle_kernel(
    last, order, tile_ref, halves, x_a, x_d, table, right, gathered, work, nodes, partial,
):
    side_x = low_side("gx")
    for c in range(CHANNELS):
        for x in range(2, SIDE - 2):
            work[c, x] = plane(halves, None, c, x, slice(0, 8))
        for recv, high in ((x_a, 1 - side_x), (x_d, side_x)):
            for p in range(2):
                at = (c * 2 + p) * 8
                work[c, 8 * high + p] = halves[high, c, 4 * high + p, 0:8, :] + recv[at : at + 8]
    inner = iota((8, LANES), 0) >= 2

    def node_step(x, carry):
        inside = inside_x(x, last)
        found = [
            node_speeds([work[c, x, :, half(h)] for c in range(8)], work[8, x, :, half(h)], inside)
            for h in range(2)
        ]
        at = pl.multiple_of(x * 8, 8)
        for c in range(3):
            ready = tiles(*([found[h][f][c] for h in range(2)] for f in range(2)))
            for j in range(5):
                nodes[j, c, pl.ds(at, 8), :] = jnp.where(inner, ready[j], 0.0)
        return carry

    lax.fori_loop(0, SIDE, node_step, 0, unroll=2)

    def one(chunk, slot):
        s = chunk * CHUNK + slot
        tile_x, tile_y, j, shift = tile_of(tile_ref, s)

        def row(k):
            return table[k, pl.ds(s, 1), :]

        first = pl.multiple_of(tile_x * 32, 32)
        left = [z_window(nodes[j, c, pl.ds(first, 48), :], shift) for c in range(3)]
        summed = matmul(jnp.concatenate(left, 0), right[s])
        dy = y_coords(tile_y) - row(POS_Y)
        wy = spline(dy)
        pos_x = row(POS_X)
        wxy = [wy * row(WX + x) for x in range(6)]
        place = slice(slot * 8, slot * 8 + 8)
        for c in range(3):
            speed = along_x = along_z = None
            for x in range(5, -1, -1):
                at = (c * 6 + x) * 8
                part = wxy[x] * summed[at : at + 8, 0:LANES]
                moment = wxy[x] * summed[at : at + 8, LANES : 2 * LANES]
                speed = part if speed is None else speed + part
                along_z = moment if along_z is None else along_z + moment
                if x:
                    along_x = speed if along_x is None else along_x + speed
            partial[4 * c, place, :] = speed
            partial[4 * c + 1, place, :] = along_x - pos_x * speed
            partial[4 * c + 2, place, :] = speed * dy
            partial[4 * c + 3, place, :] = along_z

    def step(chunk, carry):
        for slot in range(CHUNK):
            one(chunk, slot)
        for k in range(12):
            gathered[k, chunk_of(chunk), :] = collect(partial, k)
        return carry

    lax.fori_loop(0, SLOTS // CHUNK, step, 0)


def gather_kernel(
    last, tile_ref, gathered, own_a, own_d, y_a, y_d, table, right, edge_weights, deform,
    velocity_out, affine_out, deform_out, stress_out,
    nodes, codes, partial, new_velocity, new_affine, new_deform, new_stress, sems,
):
    side_y = low_side("gy")
    index_y = lax.axis_index("gy")
    for own, recv, high in ((own_a, y_a, 1 - side_y), (own_d, y_d, side_y)):
        edge_y = jnp.where(high == 0, (index_y == 0), (index_y == last[1]))
        for x in range(SIDE):
            codes[pl.ds(2 * x + 1 - high, 1), :] = own[160 + x : 161 + x, :]
            codes[pl.ds(2 * x + high, 1), :] = recv[160 + x : 161 + x, :]
        for first, count in ((0, 8), (8, 2)):
            row = iota((2 * count, LANES), 0)
            inside = inside_x(lax.shift_right_logical(row, 1) + first, last)
            inside = jnp.where(((row & 1) == high) & edge_y, 0.0, inside)
            found = []
            for h in range(2):
                sums = []
                for c in range(8):
                    at = y_face_row(c, first)
                    rows = slice(at, at + 2 * count)
                    sums.append(own[rows, half(h)] + recv[rows, half(h)])
                code = codes[2 * first : 2 * (first + count), half(h)]
                found.append(node_speeds(sums, code, inside))
            for c in range(3):
                ready = tiles(*([found[h][f][c] for h in range(2)] for f in range(2)))
                for j in range(5):
                    nodes[high, j, c, 2 * first : 2 * (first + count), :] = ready[j]
        for c in range(3):
            for j in range(5):
                nodes[high, j, c, 2 * SIDE : 24, :] = jnp.zeros((24 - 2 * SIDE, LANES), F32)

    def one(chunk, slot):
        s = chunk * CHUNK + slot
        tile_x, tile_y, j, shift = tile_of(tile_ref, s)

        def row(k):
            return table[k, pl.ds(s, 1), :]

        first = pl.multiple_of(tile_x * 8, 8)
        left = [nodes[tile_y, j, c, pl.ds(first, 16), :] for c in range(3)]
        summed = matmul(z_window(jnp.concatenate(left, 0), shift), right[s])
        sublane = iota((8, LANES), 0)
        dy = ((sublane & 1) + 4 * tile_y).astype(F32) - row(POS_Y)
        speed, along_x, along_z = [None] * 3, [None] * 3, [None] * 3
        for q in range(2):
            dx = (lax.shift_right_logical(sublane, 1) + 4 * q).astype(F32) - row(POS_X)
            weight = edge_weights[s, q]
            for c in range(3):
                at = c * 16 + q * 8
                part = weight * summed[at : at + 8, 0:LANES]
                moment = weight * summed[at : at + 8, LANES : 2 * LANES]
                speed[c] = part if q == 0 else speed[c] + part
                along_x[c] = part * dx if q == 0 else along_x[c] + part * dx
                along_z[c] = moment if q == 0 else along_z[c] + moment
        place = slice(slot * 8, slot * 8 + 8)
        for c in range(3):
            partial[chunk, 4 * c, place, :] = speed[c]
            partial[chunk, 4 * c + 1, place, :] = along_x[c]
            partial[chunk, 4 * c + 2, place, :] = speed[c] * dy
            partial[chunk, 4 * c + 3, place, :] = along_z[c]

    ready = (new_velocity, new_affine, new_deform, new_stress)
    finals = (velocity_out, affine_out, deform_out, stress_out)

    def sends(chunk):
        slots = chunk_of(chunk)
        return [
            pltpu.make_async_copy(src.at[:, slots], dst.at[:, slots], sems.at[chunk, i])
            for i, (src, dst) in enumerate(zip(ready, finals))
        ]

    def step(chunk):
        for slot in range(CHUNK):
            one(chunk, slot)
        slots = chunk_of(chunk)
        live = table[LIVE, slots, :]
        total = [(gathered[k, slots, :] + collect(partial.at[chunk], k)) * live for k in range(12)]
        moved = []
        for c in range(3):
            new_velocity[c, slots, :] = total[4 * c]
            for k in range(3):
                value = 4.0 * total[4 * c + 1 + k]
                new_affine[3 * c + k, slots, :] = value
                moved.append(value)
        old = [deform[k, slots, :] for k in range(9)]
        fresh = []
        for i in range(3):
            for j in range(3):
                value = old[3 * i + j]
                for k in range(3):
                    value = value + DT * moved[3 * i + k] * old[3 * k + j]
                fresh.append(value * live)
        for k in range(9):
            new_deform[k, slots, :] = fresh[k]
        stress = kirchhoff(fresh)
        for k, entry in enumerate((0, 4, 8, 1, 2, 5)):
            new_stress[k, slots, :] = stress[entry] * live
        for send in sends(chunk):
            send.start()

    for chunk in range(SLOTS // CHUNK):
        step(chunk)
    for chunk in range(SLOTS // CHUNK):
        for send in sends(chunk):
            send.wait()


def vmem(shape, dtype=F32):
    return pltpu.VMEM(shape, dtype)


def cost(flops):
    return pl.CostEstimate(flops=flops, bytes_accessed=4000000, transcendentals=0)


def swap_pairs(block, axis, shift):
    size = lax.axis_size(axis)
    route = [(i, ((i + shift) ^ 1) - shift) for i in range(size)]
    return lax.ppermute(block, axis, [(i, k) for i, k in route if 0 <= k < size])


def per_device(
    offset, particle_mass, velocity, affine, deform,
    particle_cell, body_id, slot_tile_number, block_count, normal_code,
):
    params = pltpu.CompilerParams(vmem_limit_bytes=VMEM_LIMIT)
    smem = pl.BlockSpec(memory_space=pltpu.SMEM)
    hbm = pl.BlockSpec(memory_space=pltpu.HBM)
    whole = pl.BlockSpec(memory_space=pltpu.VMEM)
    x_face = jax.ShapeDtypeStruct((X_FACE_ROWS, DEPTH), F32)
    y_face = jax.ShapeDtypeStruct((Y_FACE_ROWS, DEPTH), F32)
    right_shape = jax.ShapeDtypeStruct((SLOTS, LANES, 256), BF16)
    last = (lax.axis_size("gx") - 1, lax.axis_size("gy") - 1)
    inputs = (
        slot_tile_number, offset, particle_mass, velocity, affine, deform, particle_cell,
        body_id, normal_code,
    )

    halves_shape = jax.ShapeDtypeStruct((2, CHANNELS, 6, 16, DEPTH), F32)
    scatter_scratch = [
        pltpu.SMEM((32,), jnp.int32),
        vmem((UNROLL, 192, 256), BF16),
        vmem((UNROLL, 192, 256), BF16),
        vmem((2, 2, 2, 280, LANES)),
        vmem((2, 2, 192, DEPTH)),
    ]
    anywhere = pl.BlockSpec(memory_space=pl.ANY)

    halves, x_d, table, rows, tile_numbers = pl.pallas_call(
        first_kernel,
        out_shape=(
            halves_shape,
            x_face,
            jax.ShapeDtypeStruct((GATHER_ROWS, 32, LANES), F32),
            jax.ShapeDtypeStruct((SCATTER_ROWS - GATHER_ROWS, 32, LANES), F32),
            jax.ShapeDtypeStruct((1, SLOTS), jnp.int32),
        ),
        in_specs=[smem] + [hbm] * 9,
        out_specs=(whole,) * 4 + (smem,),
        scratch_shapes=[vmem(x.shape, x.dtype) for x in inputs[1:]]
        + scatter_scratch
        + [pltpu.SemaphoreType.DMA((9,))],
        compiler_params=params,
        cost_estimate=cost(3000000),
        name="scatter_first",
    )(
        block_count,
        *(pltpu.with_memory_space_constraint(x, pltpu.HBM) for x in inputs),
    )
    got_x_d = swap_pairs(x_d, "gx", 1)
    halves, x_a = pl.pallas_call(
        second_kernel,
        out_shape=(halves_shape, x_face),
        in_specs=[smem] + [whole] * 3,
        out_specs=(whole,) * 2,
        scratch_shapes=scatter_scratch,
        input_output_aliases={1: 0},
        compiler_params=params,
        cost_estimate=cost(3000000),
        name="scatter_second",
    )(tile_numbers, halves, table, rows)
    got_x_a = swap_pairs(x_a, "gx", 0)
    right, edge_weights = pl.pallas_call(
        prepare_kernel,
        out_shape=(right_shape, jax.ShapeDtypeStruct((SLOTS, 2, 8, LANES), F32)),
        in_specs=[anywhere, smem, whole],
        out_specs=(whole,) * 2,
        compiler_params=params,
        cost_estimate=cost(3000000),
        name="prepare",
    )(x_a, tile_numbers, table)
    y_a, y_d = pl.pallas_call(
        corner_kernel,
        out_shape=(y_face, y_face),
        in_specs=[anywhere] + [whole] * 3,
        out_specs=(whole,) * 2,
        scratch_shapes=[vmem((CHANNELS, 4, 16, DEPTH))],
        compiler_params=params,
        name="corners",
    )(right, halves, got_x_a, got_x_d)
    got_y_d = swap_pairs(y_d, "gy", 1)
    got_y_a = swap_pairs(y_a, "gy", 0)
    slots, particles = particle_mass.shape
    gathered = pl.pallas_call(
        functools.partial(middle_kernel, last),
        out_shape=jax.ShapeDtypeStruct((12, slots, particles), F32),
        in_specs=[anywhere, smem] + [whole] * 5,
        out_specs=whole,
        scratch_shapes=[
            vmem((CHANNELS, SIDE, 8, DEPTH)),
            vmem((5, 3, 8 * SIDE, LANES)),
            vmem((12, 8 * CHUNK, LANES)),
        ],
        compiler_params=params,
        cost_estimate=cost(3000000),
        name="middle",
    )(y_a, tile_numbers, halves, got_x_a, got_x_d, table, right)
    return pl.pallas_call(
        functools.partial(gather_kernel, last),
        out_shape=tuple(jax.ShapeDtypeStruct((k, slots, particles), F32) for k in (3, 9, 9, 6)),
        in_specs=[smem] + [whole] * 9,
        out_specs=(hbm,) * 4,
        scratch_shapes=[vmem((2, 5, 3, 24, LANES)), vmem((24, DEPTH)), vmem((SLOTS // CHUNK, 12, 8 * CHUNK, LANES))]
        + [vmem((k, slots, particles)) for k in (3, 9, 9, 6)]
        + [pltpu.SemaphoreType.DMA((SLOTS // CHUNK, 4))],
        compiler_params=params,
        name="gather",
    )(
        tile_numbers, gathered, y_a, y_d, got_y_a, got_y_d, table, right, edge_weights, deform
    )


def solution(mesh):
    both = ("gx", "gy")
    field = P(None, both, None)
    flat = P(both, None)
    return jax.shard_map(
        per_device,
        mesh=mesh,
        in_specs=(
            field, flat, field, field, field, flat, flat, P(both), P("gx", "gy"),
            P("gx", "gy", None),
        ),
        out_specs=(field,) * 4,
        check_vma=False,
    )
```

```python
import functools

import jax
import jax.numpy as jnp
from jax import lax
from jax.experimental import pallas as pl
from jax.experimental.pallas import tpu as pltpu
from jax.sharding import PartitionSpec as P


DT = 0.1
MU = 2.0
LAM = 3.0
GRAVITY = -2.0
FLOOR = 0.25

F32 = jnp.float32
BF16 = jnp.bfloat16
VMEM_LIMIT = 24 * 1024 * 1024

SIDE = 10
DEPTH = 256
SLOTS = 24
LANES = 128
X_FACE_ROWS = 184
Y_FACE_ROWS = 176
CHANNELS = 9
CHUNK = 8
UNROLL = 4

POS_Y, POS_Z, FIELD0, FIELD1, POS_X, LIVE, WX = 0, 1, 2, 3, 4, 5, 6
GATHER_ROWS = WX + 6
MASS = GATHER_ROWS
VEL = MASS + 1
AFF = VEL + 3
SCATTER_ROWS = AFF + 9


def spline(distance):
    size = jnp.abs(distance)
    outer = jnp.maximum(1.5 - size, 0.0)
    inner = jnp.maximum(0.5 - size, 0.0)
    return 0.5 * outer * outer - 1.5 * inner * inner


def determinant(m):
    return (
        m[0] * (m[4] * m[8] - m[5] * m[7])
        - m[1] * (m[3] * m[8] - m[5] * m[6])
        + m[2] * (m[3] * m[7] - m[4] * m[6])
    )


def kirchhoff(m):
    ratio = determinant(m)
    pressure = 0.5 * LAM * (ratio * ratio - 1.0)
    entries = []
    for i in range(3):
        for j in range(3):
            e = m[3 * i] * m[3 * j] + m[3 * i + 1] * m[3 * j + 1] + m[3 * i + 2] * m[3 * j + 2]
            entries.append(MU * (e - 1.0) + pressure if i == j else MU * e)
    return entries


def split(x):
    high = x.astype(BF16)
    return high, (x - high.astype(F32)).astype(BF16)


def matmul_t(a, b):
    return lax.dot_general(a, b, (((1,), (1,)), ((), ())), preferred_element_type=F32)


def matmul(a, b):
    return lax.dot_general(a, b, (((1,), (0,)), ((), ())), preferred_element_type=F32)


def iota(shape, axis):
    return lax.broadcasted_iota(jnp.int32, shape, axis)


def y_coords(tile_y):
    s = iota((8, LANES), 0)
    wrapped = jnp.where(s < 4, s + 4, s - 4)
    return jnp.where(tile_y == 0, s, wrapped).astype(F32)


def low_side(axis):
    return lax.axis_index(axis) % 2


def half(h):
    return slice(h * LANES, (h + 1) * LANES)


def matching_slots(order, tile_ref, tile_x):
    n = jnp.int32(0)
    for s in range(SLOTS):
        order[n] = s
        n = n + (lax.shift_right_logical(tile_ref[0, s], 6) == tile_x).astype(jnp.int32)
    for k in range(UNROLL - 1):
        order[n + k] = SLOTS
    return n


def clear(left_hi, left_lo, acc):
    acc[...] = jnp.zeros_like(acc)
    zeros = jnp.zeros((48, LANES), BF16)
    for u in range(UNROLL):
        left_hi[u, 0:48, LANES : 2 * LANES] = zeros
        left_lo[u, 0:48, LANES : 2 * LANES] = zeros


def scatter_half(tile_x, tile_ref, table, rows, halves, face, order, left_hi, left_lo,
                 acc, turned):
    count = matching_slots(order, tile_ref, tile_x)

    def one(index, u):
        s = order[index]
        tile = tile_ref[0, jnp.minimum(s, SLOTS - 1)]
        tile_y = lax.shift_right_logical(tile, 5) & 1
        tile_z = tile & 31

        def row(k):
            return table[k, pl.ds(s, 1), :] if k < MASS else rows[k - MASS, pl.ds(s, 1), :]

        dy = y_coords(tile_y) - row(POS_Y)
        wy = spline(dy)
        pos_x = row(POS_X)
        wxy = [wy * row(WX + x) for x in range(6)]

        def put(channel, column, values):
            for pair in range(3):
                hi, lo = split(jnp.concatenate(values[2 * pair : 2 * pair + 2], 0))
                at = channel * 48 + pair * 16
                left_hi[u, at : at + 16, column * LANES : (column + 1) * LANES] = hi
                left_lo[u, at : at + 16, column * LANES : (column + 1) * LANES] = lo

        m = row(MASS)
        put(0, 0, [w * m for w in wxy])
        for k in range(3):
            base = row(VEL + k) + row(AFF + 3 * k + 1) * dy
            ax = row(AFF + 3 * k)
            az = row(AFF + 3 * k + 2)
            put(1 + k, 0, [wxy[x] * (base + ax * (float(x) - pos_x)) for x in range(6)])
            put(1 + k, 1, [wxy[x] * az for x in range(6)])

        dz = iota((16, LANES), 0).astype(F32) - row(POS_Z)
        wz = spline(dz)
        mz = wz * dz
        parts = []
        for f in range(2):
            mask = row(FIELD0 + f)
            parts.append([split(wz * mask), split(mz * mask)])
        right_hi = jnp.concatenate(
            [jnp.concatenate([parts[f][0][0], parts[f][1][0]], 1) for f in range(2)], 0
        )
        right_lo = jnp.concatenate(
            [jnp.concatenate([parts[f][0][1], parts[f][1][1]], 1) for f in range(2)], 0
        )
        both = matmul_t(jnp.concatenate([right_hi, right_lo], 0), left_hi[u])
        rest = matmul_t(right_hi, left_lo[u])
        total = both[0:32] + both[32:64] + rest
        window = pl.ds(tile_z * 8 + 7, 16)
        for f in range(2):
            acc[tile_y, f, 0, window, :] += total[16 * f : 16 * f + 16, 0:LANES]
            acc[tile_y, f, 1, window, 0:64] += total[16 * f : 16 * f + 16, LANES:192]

    def step(group, carry):
        for u in range(UNROLL):
            one(group * UNROLL + u, u)
        return carry

    groups = lax.shift_right_logical(count + 1, 2)
    lax.fori_loop(0, groups, step, 0)

    def pair(k, carry):
        for u in range(2):
            one(groups * UNROLL + u, u)
        return carry

    lax.fori_loop(0, lax.shift_right_logical(count - groups * UNROLL + 1, 1), pair, 0)

    for ty in range(2):
        for f in range(2):
            for h in range(2):
                z = slice(8 + LANES * h, 8 + LANES * (h + 1))
                turned[ty, f, 0:128, half(h)] = acc[ty, f, 0, z, :].T
                turned[ty, f, 128:192, half(h)] = acc[ty, f, 1, z, :].T[0:64]

    upper = iota((8, DEPTH), 0) >= 4
    for f in range(2):
        for c in range(4):
            for x in range(6):
                at = (c * 6 + x) * 8
                high = turned[1, f, at : at + 8, :]
                halves[tile_x, 4 * f + c, x, 0:8, :] = turned[
                    0, f, at : at + 8, :
                ] + jnp.where(upper, high, 0.0)
                halves[tile_x, 4 * f + c, x, 8:16, :] = high
    for c in range(CHANNELS):
        for p in range(2):
            at = c * 2 + p
            face[at * 8 : at * 8 + 8, :] = halves[tile_x, c, 4 * tile_x + p, 0:8, :]
            face[144 + at * 2 : 146 + at * 2, :] = halves[tile_x, c, 4 * tile_x + p, 8:10, :]
    face[180:184, :] = jnp.zeros((4, DEPTH), F32)


def first_kernel(
    count_ref, tile_in, offset_in, mass_in, velocity_in, affine_in, deform_in, cell_in, body_in,
    code_in,
    halves, face, table, rows, tile_ref,
    offset, mass, velocity, affine, deform, cell, body, code,
    order, left_hi, left_lo, acc, turned, sems,
):
    pairs = (
        (tile_in, tile_ref.at[0]), (deform_in, deform), (affine_in, affine),
        (offset_in, offset), (velocity_in, velocity), (mass_in, mass), (cell_in, cell),
        (body_in, body), (code_in, code),
    )
    copies = [
        pltpu.make_async_copy(src, dst, sems.at[i]) for i, (src, dst) in enumerate(pairs)
    ]
    for copy in copies:
        copy.start()
    clear(left_hi, left_lo, acc)
    halves[:, 8] = jnp.zeros((2, 6, 16, DEPTH), F32)
    for out in (table, rows):
        for k in range(out.shape[0]):
            out[k, SLOTS:32, :] = jnp.zeros((32 - SLOTS, LANES), F32)
    for copy in copies:
        copy.wait()

    for x in range(1, 9):
        half_x = 0 if x < 6 else 1
        halves[half_x, 8, x - 4 * half_x, 1:9, :] = code[x - 1].astype(F32)
    live = (iota((SLOTS, LANES), 0) < count_ref[0, 0]).astype(F32)
    cell = cell[...]
    field_one = (body[...] & 1).astype(F32)
    pos_x = lax.shift_right_logical(cell, 5).astype(F32) + offset[0]
    own = slice(0, SLOTS)
    table[LIVE, own] = live
    table[POS_X, own] = pos_x
    table[POS_Y, own] = (lax.shift_right_logical(cell, 3) & 3).astype(F32) + offset[1]
    table[POS_Z, own] = (cell & 7).astype(F32) + offset[2]
    table[FIELD0, own] = 1.0 - field_one
    table[FIELD1, own] = field_one
    for x in range(6):
        table[WX + x, own] = spline(float(x) - pos_x)
    weighted = mass[...] * live
    rows[0, own] = weighted
    for k in range(3):
        rows[VEL - MASS + k, own] = weighted * velocity[k]
    stress = kirchhoff([deform[k] for k in range(9)])
    for k in range(9):
        rows[AFF - MASS + k, own] = weighted * (affine[k] - 4.0 * DT * stress[k])
    scatter_half(
        low_side("gx"), tile_ref, table, rows, halves, face, order, left_hi, left_lo, acc, turned,
    )


def second_kernel(
    tile_ref, half_in, table, rows, halves, face, order, left_hi, left_lo, acc, turned,
):
    clear(left_hi, left_lo, acc)
    scatter_half(
        1 - low_side("gx"), tile_ref, table, rows, halves, face, order, left_hi, left_lo,
        acc, turned,
    )


def prepare_kernel(order, tile_ref, table, right, edge_weights):
    none = jnp.zeros((16, 2 * LANES), BF16)

    def one(s, carry):
        dz = iota((16, LANES), 0).astype(F32) - table[POS_Z, pl.ds(s, 1), :]
        wz = spline(dz)
        mz = wz * dz
        for f in range(2):
            mask = table[FIELD0 + f, pl.ds(s, 1), :]
            hi, lo = split(jnp.concatenate([wz * mask, mz * mask], 1))
            for k, rows in enumerate((hi, lo, hi, none)):
                right[s, 64 * f + 16 * k : 64 * f + 16 * k + 16, :] = rows
        sublane = iota((8, LANES), 0)
        tile_y = lax.shift_right_logical(tile_ref[0, s], 5) & 1
        wy = spline(((sublane & 1) + 4 * tile_y).astype(F32) - table[POS_Y, pl.ds(s, 1), :])
        for q in range(2):
            dx = (lax.shift_right_logical(sublane, 1) + 4 * q).astype(F32)
            edge_weights[s, q] = wy * spline(dx - table[POS_X, pl.ds(s, 1), :])
        return carry

    lax.fori_loop(0, SLOTS, one, 0, unroll=2)


def plane(halves, edge, c, x, rows):
    if x < 2:
        return edge[c, x, rows, :]
    if x >= 8:
        return edge[c, x - 6, rows, :]
    if x < 4:
        return halves[0, c, x, rows, :]
    if x >= 6:
        return halves[1, c, x - 4, rows, :]
    return halves[0, c, x, rows, :] + halves[1, c, x - 4, rows, :]


def y_face_row(c, x):
    return c * 16 + x * 2 if x < 8 else 128 + c * 4 + (x - 8) * 2


def corner_kernel(order, halves, recv_a, recv_d, face_a, face_d, edge):
    side_y = low_side("gy")
    side_x = low_side("gx")
    for recv, high in ((recv_a, 1 - side_x), (recv_d, side_x)):
        for c in range(CHANNELS):
            for p in range(2):
                at = c * 2 + p
                own = (high, c, 4 * high + p)
                to = (c, 2 * high + p)
                edge[(*to, slice(0, 2))] = halves[(*own, slice(0, 2))] + recv[at * 8 : at * 8 + 2]
                edge[(*to, slice(8, 10))] = (
                    halves[(*own, slice(8, 10))] + recv[144 + at * 2 : 146 + at * 2]
                )
    for face, high in ((face_a, 1 - side_y), (face_d, side_y)):
        rows = pl.ds(pl.multiple_of(high * 8, 8), 2)
        for c in range(8):
            for x in range(SIDE):
                at = y_face_row(c, x)
                face[at : at + 2, :] = plane(halves, edge, c, x, rows)
        own_row = pl.ds(1 + 7 * high, 1)
        for x in range(SIDE):
            face[160 + x : 161 + x, :] = plane(halves, edge, 8, x, own_row)
        face[170:176, :] = jnp.zeros((6, DEPTH), F32)


def node_speeds(sums, code, inside):
    m0, m1 = sums[0], sums[4]
    r0 = 1.0 / jnp.maximum(m0, FLOOR)
    r1 = 1.0 / jnp.maximum(m1, FLOOR)
    rc = 1.0 / jnp.maximum(m0 + m1, FLOOR)
    share = jnp.minimum(1.0, jnp.minimum(m0, m1) * (1.0 / FLOOR))
    shifted = code + jnp.where(code >= 13.0, 1.0, 0.0)
    third = jnp.where(shifted >= 9.0, 1.0, 0.0) + jnp.where(shifted >= 18.0, 1.0, 0.0)
    rest = shifted - 9.0 * third
    second = jnp.where(rest >= 3.0, 1.0, 0.0) + jnp.where(rest >= 6.0, 1.0, 0.0)
    direction = [third - 1.0, second - 1.0, rest - 3.0 * second - 1.0]
    square = (
        direction[0] * direction[0] + direction[1] * direction[1] + direction[2] * direction[2]
    )
    inverse = jnp.where(square > 2.5, 1.0 / 3.0, jnp.where(square > 1.5, 0.5, 1.0))
    u0 = [sums[1 + k] * r0 for k in range(3)]
    u1 = [sums[5 + k] * r1 for k in range(3)]
    uc = [(sums[1 + k] + sums[5 + k]) * rc for k in range(3)]
    approach0 = sum((u0[k] - uc[k]) * direction[k] for k in range(3))
    approach1 = sum((uc[k] - u1[k]) * direction[k] for k in range(3))
    scale = share * inverse
    push0 = scale * jnp.maximum(approach0, 0.0)
    push1 = scale * jnp.maximum(approach1, 0.0)
    gravity = [0.0, 0.0, DT * GRAVITY]
    v0 = [(u0[k] - push0 * direction[k] + gravity[k]) * inside for k in range(3)]
    v1 = [(u1[k] + push1 * direction[k] + gravity[k]) * inside for k in range(3)]
    return v0, v1


def tiles(v0, v1):
    lane = iota(v0[0].shape, 1)
    local = lane & 63

    def both(h, shift):
        return jnp.where(
            lane < 64, pltpu.roll(v0[h], shift, 1), pltpu.roll(v1[h], (shift + 64) % 128, 1)
        )

    return (
        jnp.where(local < 1, 0.0, both(0, 1)),
        both(0, 73),
        jnp.where(local < 17, both(0, 17), both(1, 17)),
        both(1, 89),
        jnp.where(local < 33, both(1, 33), 0.0),
    )


def inside_x(x, last):
    index = lax.axis_index("gx")
    return jnp.where(((x == 0) & (index == 0)) | ((x == SIDE - 1) & (index == last[0])), 0.0, 1.0)


def tile_of(tile_ref, s):
    tile = tile_ref[0, s]
    tile_z = tile & 31
    j = lax.div(tile_z, 7)
    return (
        lax.shift_right_logical(tile, 6),
        lax.shift_right_logical(tile, 5) & 1,
        j,
        (tile_z - 7 * j) * 8,
    )


def z_window(value, shift):
    lane = iota(value.shape, 1) & 63
    window = pltpu.roll(value, lax.rem(128 - shift, 128), 1)
    window = jnp.where(lane < 16, window, pltpu.roll(value, lax.rem(144 - shift, 128), 1))
    window = jnp.where(lane < 32, window, pltpu.roll(value, lax.rem(160 - shift, 128), 1))
    high = window.astype(BF16).astype(F32)
    return jnp.where(lane < 32, high, window - high).astype(BF16)


def collect(partial, k):
    total = partial[k, pl.ds(0, CHUNK, stride=8), :]
    for y in range(1, 8):
        total = total + partial[k, pl.ds(y, CHUNK, stride=8), :]
    return total


def chunk_of(chunk):
    if isinstance(chunk, int):
        return slice(chunk * CHUNK, (chunk + 1) * CHUNK)
    return pl.ds(pl.multiple_of(chunk * CHUNK, CHUNK), CHUNK)


def middle_kernel(
    last, order, tile_ref, halves, x_a, x_d, table, right, gathered, work, nodes, partial,
):
    side_x = low_side("gx")
    for c in range(CHANNELS):
        for x in range(2, SIDE - 2):
            work[c, x] = plane(halves, None, c, x, slice(0, 8))
        for recv, high in ((x_a, 1 - side_x), (x_d, side_x)):
            for p in range(2):
                at = (c * 2 + p) * 8
                work[c, 8 * high + p] = halves[high, c, 4 * high + p, 0:8, :] + recv[at : at + 8]
    inner = iota((8, LANES), 0) >= 2

    def node_step(x, carry):
        inside = inside_x(x, last)
        found = [
            node_speeds([work[c, x, :, half(h)] for c in range(8)], work[8, x, :, half(h)], inside)
            for h in range(2)
        ]
        at = pl.multiple_of(x * 8, 8)
        for c in range(3):
            ready = tiles(*([found[h][f][c] for h in range(2)] for f in range(2)))
            for j in range(5):
                nodes[j, c, pl.ds(at, 8), :] = jnp.where(inner, ready[j], 0.0)
        return carry

    lax.fori_loop(0, SIDE, node_step, 0, unroll=2)

    def one(chunk, slot):
        s = chunk * CHUNK + slot
        tile_x, tile_y, j, shift = tile_of(tile_ref, s)

        def row(k):
            return table[k, pl.ds(s, 1), :]

        first = pl.multiple_of(tile_x * 32, 32)
        left = [z_window(nodes[j, c, pl.ds(first, 48), :], shift) for c in range(3)]
        summed = matmul(jnp.concatenate(left, 0), right[s])
        dy = y_coords(tile_y) - row(POS_Y)
        wy = spline(dy)
        pos_x = row(POS_X)
        wxy = [wy * row(WX + x) for x in range(6)]
        place = slice(slot * 8, slot * 8 + 8)
        for c in range(3):
            speed = along_x = along_z = None
            for x in range(5, -1, -1):
                at = (c * 6 + x) * 8
                part = wxy[x] * summed[at : at + 8, 0:LANES]
                moment = wxy[x] * summed[at : at + 8, LANES : 2 * LANES]
                speed = part if speed is None else speed + part
                along_z = moment if along_z is None else along_z + moment
                if x:
                    along_x = speed if along_x is None else along_x + speed
            partial[4 * c, place, :] = speed
            partial[4 * c + 1, place, :] = along_x - pos_x * speed
            partial[4 * c + 2, place, :] = speed * dy
            partial[4 * c + 3, place, :] = along_z

    def step(chunk, carry):
        for slot in range(CHUNK):
            one(chunk, slot)
        for k in range(12):
            gathered[k, chunk_of(chunk), :] = collect(partial, k)
        return carry

    lax.fori_loop(0, SLOTS // CHUNK, step, 0)


def gather_kernel(
    last, tile_ref, gathered, own_a, own_d, y_a, y_d, table, right, edge_weights, deform,
    velocity_out, affine_out, deform_out, stress_out,
    nodes, codes, partial, new_velocity, new_affine, new_deform, new_stress, sems,
):
    side_y = low_side("gy")
    index_y = lax.axis_index("gy")
    for own, recv, high in ((own_a, y_a, 1 - side_y), (own_d, y_d, side_y)):
        edge_y = jnp.where(high == 0, (index_y == 0), (index_y == last[1]))
        for x in range(SIDE):
            codes[pl.ds(2 * x + 1 - high, 1), :] = own[160 + x : 161 + x, :]
            codes[pl.ds(2 * x + high, 1), :] = recv[160 + x : 161 + x, :]
        for first, count in ((0, 8), (8, 2)):
            row = iota((2 * count, LANES), 0)
            inside = inside_x(lax.shift_right_logical(row, 1) + first, last)
            inside = jnp.where(((row & 1) == high) & edge_y, 0.0, inside)
            found = []
            for h in range(2):
                sums = []
                for c in range(8):
                    at = y_face_row(c, first)
                    rows = slice(at, at + 2 * count)
                    sums.append(own[rows, half(h)] + recv[rows, half(h)])
                code = codes[2 * first : 2 * (first + count), half(h)]
                found.append(node_speeds(sums, code, inside))
            for c in range(3):
                ready = tiles(*([found[h][f][c] for h in range(2)] for f in range(2)))
                for j in range(5):
                    nodes[high, j, c, 2 * first : 2 * (first + count), :] = ready[j]
        for c in range(3):
            for j in range(5):
                nodes[high, j, c, 2 * SIDE : 24, :] = jnp.zeros((24 - 2 * SIDE, LANES), F32)

    def one(chunk, slot):
        s = chunk * CHUNK + slot
        tile_x, tile_y, j, shift = tile_of(tile_ref, s)

        def row(k):
            return table[k, pl.ds(s, 1), :]

        first = pl.multiple_of(tile_x * 8, 8)
        left = [nodes[tile_y, j, c, pl.ds(first, 16), :] for c in range(3)]
        summed = matmul(z_window(jnp.concatenate(left, 0), shift), right[s])
        sublane = iota((8, LANES), 0)
        dy = ((sublane & 1) + 4 * tile_y).astype(F32) - row(POS_Y)
        speed, along_x, along_z = [None] * 3, [None] * 3, [None] * 3
        for q in range(2):
            dx = (lax.shift_right_logical(sublane, 1) + 4 * q).astype(F32) - row(POS_X)
            weight = edge_weights[s, q]
            for c in range(3):
                at = c * 16 + q * 8
                part = weight * summed[at : at + 8, 0:LANES]
                moment = weight * summed[at : at + 8, LANES : 2 * LANES]
                speed[c] = part if q == 0 else speed[c] + part
                along_x[c] = part * dx if q == 0 else along_x[c] + part * dx
                along_z[c] = moment if q == 0 else along_z[c] + moment
        place = slice(slot * 8, slot * 8 + 8)
        for c in range(3):
            partial[chunk, 4 * c, place, :] = speed[c]
            partial[chunk, 4 * c + 1, place, :] = along_x[c]
            partial[chunk, 4 * c + 2, place, :] = speed[c] * dy
            partial[chunk, 4 * c + 3, place, :] = along_z[c]

    ready = (new_velocity, new_affine, new_deform, new_stress)
    finals = (velocity_out, affine_out, deform_out, stress_out)

    def sends(chunk):
        slots = chunk_of(chunk)
        return [
            pltpu.make_async_copy(src.at[:, slots], dst.at[:, slots], sems.at[chunk, i])
            for i, (src, dst) in enumerate(zip(ready, finals))
        ]

    def step(chunk):
        for slot in range(CHUNK):
            one(chunk, slot)
        slots = chunk_of(chunk)
        live = table[LIVE, slots, :]
        total = [(gathered[k, slots, :] + collect(partial.at[chunk], k)) * live for k in range(12)]
        moved = []
        for c in range(3):
            new_velocity[c, slots, :] = total[4 * c]
            for k in range(3):
                value = 4.0 * total[4 * c + 1 + k]
                new_affine[3 * c + k, slots, :] = value
                moved.append(value)
        old = [deform[k, slots, :] for k in range(9)]
        fresh = []
        for i in range(3):
            for j in range(3):
                value = old[3 * i + j]
                for k in range(3):
                    value = value + DT * moved[3 * i + k] * old[3 * k + j]
                fresh.append(value * live)
        for k in range(9):
            new_deform[k, slots, :] = fresh[k]
        stress = kirchhoff(fresh)
        for k, entry in enumerate((0, 4, 8, 1, 2, 5)):
            new_stress[k, slots, :] = stress[entry] * live
        for send in sends(chunk):
            send.start()

    for chunk in range(SLOTS // CHUNK):
        step(chunk)
    for chunk in range(SLOTS // CHUNK):
        for send in sends(chunk):
            send.wait()


def vmem(shape, dtype=F32):
    return pltpu.VMEM(shape, dtype)


def cost(flops):
    return pl.CostEstimate(flops=flops, bytes_accessed=4000000, transcendentals=0)


def swap_pairs(block, axis, shift):
    size = lax.axis_size(axis)
    route = [(i, ((i + shift) ^ 1) - shift) for i in range(size)]
    return lax.ppermute(block, axis, [(i, k) for i, k in route if 0 <= k < size])


def per_device(
    offset, particle_mass, velocity, affine, deform,
    particle_cell, body_id, slot_tile_number, block_count, normal_code,
):
    params = pltpu.CompilerParams(vmem_limit_bytes=VMEM_LIMIT)
    smem = pl.BlockSpec(memory_space=pltpu.SMEM)
    hbm = pl.BlockSpec(memory_space=pltpu.HBM)
    whole = pl.BlockSpec(memory_space=pltpu.VMEM)
    x_face = jax.ShapeDtypeStruct((X_FACE_ROWS, DEPTH), F32)
    y_face = jax.ShapeDtypeStruct((Y_FACE_ROWS, DEPTH), F32)
    right_shape = jax.ShapeDtypeStruct((SLOTS, LANES, 256), BF16)
    last = (lax.axis_size("gx") - 1, lax.axis_size("gy") - 1)
    inputs = (
        slot_tile_number, offset, particle_mass, velocity, affine, deform, particle_cell,
        body_id, normal_code,
    )

    halves_shape = jax.ShapeDtypeStruct((2, CHANNELS, 6, 16, DEPTH), F32)
    scatter_scratch = [
        pltpu.SMEM((32,), jnp.int32),
        vmem((UNROLL, 192, 256), BF16),
        vmem((UNROLL, 192, 256), BF16),
        vmem((2, 2, 2, 280, LANES)),
        vmem((2, 2, 192, DEPTH)),
    ]
    anywhere = pl.BlockSpec(memory_space=pl.ANY)

    halves, x_d, table, rows, tile_numbers = pl.pallas_call(
        first_kernel,
        out_shape=(
            halves_shape,
            x_face,
            jax.ShapeDtypeStruct((GATHER_ROWS, 32, LANES), F32),
            jax.ShapeDtypeStruct((SCATTER_ROWS - GATHER_ROWS, 32, LANES), F32),
            jax.ShapeDtypeStruct((1, SLOTS), jnp.int32),
        ),
        in_specs=[smem] + [hbm] * 9,
        out_specs=(whole,) * 4 + (smem,),
        scratch_shapes=[vmem(x.shape, x.dtype) for x in inputs[1:]]
        + scatter_scratch
        + [pltpu.SemaphoreType.DMA((9,))],
        compiler_params=params,
        cost_estimate=cost(3000000),
        name="scatter_first",
    )(
        block_count,
        *(pltpu.with_memory_space_constraint(x, pltpu.HBM) for x in inputs),
    )
    got_x_d = swap_pairs(x_d, "gx", 1)
    halves, x_a = pl.pallas_call(
        second_kernel,
        out_shape=(halves_shape, x_face),
        in_specs=[smem] + [whole] * 3,
        out_specs=(whole,) * 2,
        scratch_shapes=scatter_scratch,
        input_output_aliases={1: 0},
        compiler_params=params,
        cost_estimate=cost(3000000),
        name="scatter_second",
    )(tile_numbers, halves, table, rows)
    got_x_a = swap_pairs(x_a, "gx", 0)
    right, edge_weights = pl.pallas_call(
        prepare_kernel,
        out_shape=(right_shape, jax.ShapeDtypeStruct((SLOTS, 2, 8, LANES), F32)),
        in_specs=[anywhere, smem, whole],
        out_specs=(whole,) * 2,
        compiler_params=params,
        cost_estimate=cost(3000000),
        name="prepare",
    )(x_a, tile_numbers, table)
    y_a, y_d = pl.pallas_call(
        corner_kernel,
        out_shape=(y_face, y_face),
        in_specs=[anywhere] + [whole] * 3,
        out_specs=(whole,) * 2,
        scratch_shapes=[vmem((CHANNELS, 4, 16, DEPTH))],
        compiler_params=params,
        name="corners",
    )(right, halves, got_x_a, got_x_d)
    got_y_d = swap_pairs(y_d, "gy", 1)
    got_y_a = swap_pairs(y_a, "gy", 0)
    slots, particles = particle_mass.shape
    gathered = pl.pallas_call(
        functools.partial(middle_kernel, last),
        out_shape=jax.ShapeDtypeStruct((12, slots, particles), F32),
        in_specs=[anywhere, smem] + [whole] * 5,
        out_specs=whole,
        scratch_shapes=[
            vmem((CHANNELS, SIDE, 8, DEPTH)),
            vmem((5, 3, 8 * SIDE, LANES)),
            vmem((12, 8 * CHUNK, LANES)),
        ],
        compiler_params=params,
        cost_estimate=cost(3000000),
        name="middle",
    )(y_a, tile_numbers, halves, got_x_a, got_x_d, table, right)
    return pl.pallas_call(
        functools.partial(gather_kernel, last),
        out_shape=tuple(jax.ShapeDtypeStruct((k, slots, particles), F32) for k in (3, 9, 9, 6)),
        in_specs=[smem] + [whole] * 9,
        out_specs=(hbm,) * 4,
        scratch_shapes=[vmem((2, 5, 3, 24, LANES)), vmem((24, DEPTH)), vmem((SLOTS // CHUNK, 12, 8 * CHUNK, LANES))]
        + [vmem((k, slots, particles)) for k in (3, 9, 9, 6)]
        + [pltpu.SemaphoreType.DMA((SLOTS // CHUNK, 4))],
        compiler_params=params,
        name="gather",
    )(
        tile_numbers, gathered, y_a, y_d, got_y_a, got_y_d, table, right, edge_weights, deform
    )


def solution(mesh):
    both = ("gx", "gy")
    field = P(None, both, None)
    flat = P(both, None)
    return jax.shard_map(
        per_device,
        mesh=mesh,
        in_specs=(
            field, flat, field, field, field, flat, flat, P(both), P("gx", "gy"),
            P("gx", "gy", None),
        ),
        out_specs=(field,) * 4,
        check_vma=False,
    )
```
